32 devices in a mesh: dp: 8 (over y, x, core), fsdp: 4 (over z).
Axes of the slice: x: 2, y: 2, z: 4, core: 2. Of those that a mesh axis runs over, the one named last changes fastest.
Arguments:
- cells_in: bfloat16 [32, 1024, 768], P(('dp', 'fsdp')), may hold values from -6 to 6
- out_grad: bfloat16 [32, 1024, 768], P(('dp', 'fsdp')), may hold values from -6 to 6
- cell_length: int32 [32], replicated, may hold values from 300 to 1024, as said below
- cell_place: int32 [32], replicated, may hold values from 0 to 31, each once
- gene_ids: int32 [32, 1024], P(('dp', 'fsdp')), may hold values from 0 to 35999
- attn_norm_gain: bfloat16 [768], P('fsdp'), may hold values from 0.5 to 1.5
- attn_norm_bias: bfloat16 [768], P('fsdp'), may hold values from -3 to 3
- query_weight: bfloat16 [768, 768], P('fsdp'), may hold values from -0.21875 to 0.21875
- query_bias: bfloat16 [768], P('fsdp'), may hold values from -3 to 3
- key_weight: bfloat16 [768, 768], P('fsdp'), may hold values from -0.21875 to 0.21875
- value_weight: bfloat16 [768, 768], P('fsdp'), may hold values from -0.21875 to 0.21875
- value_bias: bfloat16 [768], P('fsdp'), may hold values from -3 to 3
- out_weight: bfloat16 [768, 768], P('fsdp'), may hold values from -1.75 to 1.75
- out_bias: bfloat16 [768], P('fsdp'), may hold values from -3 to 3
- ffn_norm_gain: bfloat16 [768], P('fsdp'), may hold values from 0.5 to 1.5
- ffn_norm_bias: bfloat16 [768], P('fsdp'), may hold values from -3 to 3
- up_weight: bfloat16 [768, 3072], P('fsdp'), may hold values from -0.21875 to 0.21875
- up_bias: bfloat16 [3072], P('fsdp'), may hold values from -3 to 3
- down_weight: bfloat16 [3072, 768], P('fsdp'), may hold values from -0.109375 to 0.109375
- down_bias: bfloat16 [768], P('fsdp'), may hold values from -3 to 3
Outputs:
- block_out: bfloat16 [32, 1024, 768], P(('dp', 'fsdp'))
- input_grad: bfloat16 [32, 1024, 768], P(('dp', 'fsdp'))
- grad_attn_norm_gain: float32 [768], P('fsdp')
- grad_attn_norm_bias: float32 [768], P('fsdp')
- grad_query_weight: float32 [768, 768], P('fsdp')
- grad_query_bias: float32 [768], P('fsdp')
- grad_key_weight: float32 [768, 768], P('fsdp')
- grad_value_weight: float32 [768, 768], P('fsdp')
- grad_value_bias: float32 [768], P('fsdp')
- grad_out_weight: float32 [768, 768], P('fsdp')
- grad_out_bias: float32 [768], P('fsdp')
- grad_ffn_norm_gain: float32 [768], P('fsdp')
- grad_ffn_norm_bias: float32 [768], P('fsdp')
- grad_up_weight: float32 [768, 3072], P('fsdp')
- grad_up_bias: float32 [3072], P('fsdp')
- grad_down_weight: float32 [3072, 768], P('fsdp')
- grad_down_bias: float32 [768], P('fsdp')
- gene_counts: int32 [36000], replicated
The draws below stay inside these ranges and needn't reach their ends.
Inputs may be any that keep to these rules, and one draw needn't show every extreme that they name: `cell_length`: every cell has 300 to 1024 live genes; in every draw one cell has exactly 1024 and another exactly 300. `cell_place`: each cell number appears once.
All inputs are finite; a program needn't handle non-finite values.
Results may differ from the reference program's by a relative error of at most 0.017.
Values may be sent and summed in bfloat16 or wider, within the bound.
No kernel may reach another device: no remote copies, remote signals or barrier semaphores. Data moves between devices by JAX's collectives and lax.ppermute only.
A program may use at most 320 MiB of HBM per device.

```python
import math
import jax
import jax.numpy as jnp
import numpy as np
from jax import lax

D = 768
FF = 3072
HEADS = 12
HEAD_DIM = 64
VOCAB = 36000
SEQ = 1024
MIN_LEN = 300
CELLS = 32


def draw_cell_length(key, part):
    key = jax.random.fold_in(key, 7)
    key_rand, key_long, key_short = jax.random.split(key, 3)
    drawn = jax.random.randint(key_rand, (CELLS,), MIN_LEN, SEQ + 1)
    longest = jax.random.randint(key_long, (), 0, CELLS)
    offset = jax.random.randint(key_short, (), 1, CELLS)
    shortest = (longest + offset) % CELLS
    places = jnp.arange(CELLS)
    drawn = jnp.where(places == longest, SEQ, drawn)
    drawn = jnp.where(places == shortest, MIN_LEN, drawn)
    return drawn.astype(jnp.int32)


def plant(values, own_key, least, largest):
    place = [jax.random.randint(jax.random.fold_in(own_key, axis), (), 0, length) for axis, length in enumerate(values.shape)]
    main_axis = values.shape.index(max(values.shape))
    neighbour = place[:main_axis] + [(place[main_axis] + 1) % values.shape[main_axis]] + place[main_axis + 1:]
    return values.at[tuple(place)].set(least).at[tuple(neighbour)].set(largest)


def steps_of(rng, dims, pieces, low, largest):
    level = 1.0
    for position, parts in pieces:
        draws = jax.random.uniform(jax.random.fold_in(jax.random.fold_in(rng, 6), position), (parts,), jnp.float32, low / len(pieces), largest / len(pieces))
        level = level * jnp.repeat(jnp.exp(draws), dims[position] // parts).reshape((-1,) + (1,) * (len(dims) - 1 - position))
    return level


def rank_table(count, skew):
    portions = [(1 << 20) // math.isqrt(grade ** skew) + 1 for grade in range(1, count + 1)]
    deviation = 1 + sum(portions) // (1 << 30)
    return np.cumsum(np.array([max(1, weight // deviation) for weight in portions]))


def skewed_ids(key, dims, amount, lean):
    grid = rank_table(amount, lean)
    pick = jax.random.randint(jax.random.fold_in(key, 1), dims, 0, int(grid[amount - 1]))
    rank = jnp.searchsorted(jnp.asarray(grid, jnp.int32), pick, side="right")
    return jax.random.permutation(jax.random.fold_in(key, 2), amount)[rank].astype(jnp.int32)


def gaussian(stream_key, dims, width, reach, shards=(), held_as=jnp.bfloat16):
    values = jax.random.normal(stream_key, dims, jnp.float32) * width
    if len(shards) > 0:
        values = steps_of(stream_key, dims, shards, -0.22, 0.18) * values
    return jnp.clip(values, min=-reach, max=reach).astype(held_as)


def setup_inputs(seed: int = 0) -> dict:
    seeds = jax.random.split(jax.random.key(seed), 21)
    return {
        "cells_in": gaussian(seeds[0], (CELLS, SEQ, D), 1.0, 6.0, ((0, 32),)),
        "out_grad": gaussian(seeds[1], (CELLS, SEQ, D), 1.0, 6.0, ((0, 32),)),
        "cell_length": draw_cell_length(jax.random.fold_in(seeds[20], 71), 0),
        "cell_place": jax.random.permutation(seeds[3], CELLS).astype(jnp.int32),
        "gene_ids": plant(skewed_ids(seeds[4], (CELLS, SEQ), VOCAB, 2), jax.random.fold_in(seeds[4], 3), 0, VOCAB - 1).astype(jnp.int32),
        "attn_norm_gain": jnp.clip(1.0 + 0.1 * jax.random.normal(seeds[5], (D,), jnp.float32), 0.5, 1.5).astype(jnp.bfloat16),
        "attn_norm_bias": gaussian(seeds[6], (D,), 0.5, 3.0, ((0, 4),)),
        "query_weight": gaussian(seeds[7], (D, D), D ** -0.5, 0.21875, ((0, 4),)),
        "query_bias": gaussian(seeds[8], (D,), 0.5, 3.0, ((0, 4),)),
        "key_weight": gaussian(seeds[9], (D, D), D ** -0.5, 0.21875, ((0, 4),)),
        "value_weight": gaussian(seeds[10], (D, D), D ** -0.5, 0.21875, ((0, 4),)),
        "value_bias": gaussian(seeds[11], (D,), 0.5, 3.0, ((0, 4),)),
        "out_weight": gaussian(seeds[12], (D, D), (D // 64) ** -0.5, 1.75, ((0, 4),)),
        "out_bias": gaussian(seeds[13], (D,), 0.5, 3.0, ((0, 4),)),
        "ffn_norm_gain": jnp.clip(1.0 + 0.1 * jax.random.normal(seeds[14], (D,), jnp.float32), 0.5, 1.5).astype(jnp.bfloat16),
        "ffn_norm_bias": gaussian(seeds[15], (D,), 0.5, 3.0, ((0, 4),)),
        "up_weight": gaussian(seeds[16], (D, FF), D ** -0.5, 0.21875, ((0, 4),)),
        "up_bias": gaussian(seeds[17], (FF,), 0.5, 3.0, ((0, 4),)),
        "down_weight": gaussian(seeds[18], (FF, D), FF ** -0.5, 0.109375, ((0, 4),)),
        "down_bias": gaussian(seeds[19], (D,), 0.5, 3.0, ((0, 4),)),
    }


EPSILON = 1e-05
NEGATIVE = -1e+30

@jax.custom_vjp
def low(v):
    return lax.optimization_barrier(v.astype(jnp.bfloat16)).astype(jnp.float32)

@jax.custom_vjp
def low_back(v):
    return v

def low_keep(v):
    return (low(v), None)

def low_pass(kept, grad):
    return (grad,)

def back_keep(v):
    return (v, None)

def back_low(kept, grad):
    return (low(grad),)
low.defvjp(low_keep, low_pass)
low_back.defvjp(back_keep, back_low)

def product(form, left, right):
    return jnp.einsum(form, left, right, precision=lax.Precision.HIGHEST)

def layer_norm(values, gain, shift):
    center = values - lax.optimization_barrier(jnp.mean(values, axis=-1, keepdims=True))
    inverse = lax.rsqrt(lax.optimization_barrier(jnp.mean(center * center, axis=-1, keepdims=True)) + EPSILON)
    return center * inverse * gain + shift

def block_forward(weights, inputs, cell_lens):
    gain_one, shift_one, query_w, query_b, key_w, value_w, value_b, out_w, out_b, gain_two, shift_two, up_w, up_b, down_w, down_b = weights
    group = inputs.shape[0]
    seq_length = inputs.shape[1]
    factor = HEAD_DIM ** (-0.5)
    attn_in = low(layer_norm(inputs, gain_one, shift_one))
    queries = low(low_back(product('csd,de->cse', attn_in, query_w) + query_b))
    key_rows = low(low_back(product('csd,de->cse', attn_in, key_w)))
    value_rows = low(low_back(product('csd,de->cse', attn_in, value_w) + value_b))
    queries = queries.reshape(group, seq_length, HEADS, HEAD_DIM)
    key_rows = key_rows.reshape(group, seq_length, HEADS, HEAD_DIM)
    value_rows = value_rows.reshape(group, seq_length, HEADS, HEAD_DIM)
    key_live = jnp.arange(seq_length)[None, :] < cell_lens[:, None]
    block_rows = min(512, seq_length)
    blocks = seq_length // block_rows
    query_blocks = jnp.moveaxis(queries.reshape(group, blocks, block_rows, HEADS, HEAD_DIM), 1, 0)

    def attend(query_block):
        scores = product('cqhe,ckhe->chqk', query_block, key_rows) * factor
        scores = jnp.where(key_live[:, None, None, :], low_back(scores), NEGATIVE)
        shares = jax.nn.softmax(scores, axis=-1)
        return product('chqk,ckhe->cqhe', low(shares), value_rows)
    blended = lax.map(jax.checkpoint(attend), query_blocks)
    blended = jnp.moveaxis(blended, 0, 1).reshape(group, seq_length, HEADS * HEAD_DIM)
    attn_out = low(low_back(blended))
    residual = inputs + low_back(product('csd,de->cse', attn_out, out_w) + out_b)
    ffn_in = low(layer_norm(residual, gain_two, shift_two))
    pre_act = low_back(product('csd,df->csf', ffn_in, up_w) + up_b)
    hidden = low(jax.nn.gelu(pre_act, approximate=False))
    return residual + product('csf,fd->csd', hidden, down_w) + down_b

def reference(cells_in, out_grad, cell_length, cell_place, gene_ids, attn_norm_gain, attn_norm_bias, query_weight, query_bias, key_weight, value_weight, value_bias, out_weight, out_bias, ffn_norm_gain, ffn_norm_bias, up_weight, up_bias, down_weight, down_bias):
    weights = tuple((member.astype(jnp.float32) for member in (attn_norm_gain, attn_norm_bias, query_weight, query_bias, key_weight, value_weight, value_bias, out_weight, out_bias, ffn_norm_gain, ffn_norm_bias, up_weight, up_bias, down_weight, down_bias)))
    slot_lens = cell_length[cell_place]
    group = math.gcd(CELLS, max(1, 4096 // SEQ))
    rounds_count = CELLS // group
    inputs = cells_in.astype(jnp.float32).reshape(rounds_count, group, SEQ, D)
    cotangent = out_grad.astype(jnp.float32).reshape(rounds_count, group, SEQ, D)
    part_lens = slot_lens.reshape(rounds_count, group)

    def advance(running, batch_part):
        inputs_part, grad_part, lens_part = batch_part
        result, backward = jax.vjp(lambda params, values: block_forward(params, values, lens_part), weights, inputs_part)
        grad_weights, grad_inputs = backward(grad_part)
        running = jax.tree.map(jnp.add, running, grad_weights)
        return (running, (result.astype(jnp.bfloat16), grad_inputs.astype(jnp.bfloat16)))
    zeros = jax.tree.map(jnp.zeros_like, weights)
    totals, (results, grad_inputs) = lax.scan(advance, zeros, (inputs, cotangent, part_lens))
    block_out = results.reshape(CELLS, SEQ, D)
    input_grad = grad_inputs.reshape(CELLS, SEQ, D)
    live_rows = (jnp.arange(SEQ)[None, :] < slot_lens[:, None]).astype(jnp.int32)
    gene_counts = jax.ops.segment_sum(live_rows.reshape(-1), gene_ids.reshape(-1).astype(jnp.int32), num_segments=VOCAB)
    return (block_out, input_grad, totals[0], totals[1], totals[2], totals[3], totals[4], totals[5], totals[6], totals[7], totals[8], totals[9], totals[10], totals[11], totals[12], totals[13], totals[14], gene_counts)
```

```python
from functools import partial

import jax
import jax.numpy as jnp
from jax import lax
from jax.experimental import pallas as pl
from jax.experimental.pallas import tpu as pltpu
from jax.sharding import PartitionSpec as P

HEADS = 12
HEAD_DIM = 64
VOCAB = 36000


EPSILON = 1e-05
NEGATIVE = -1e30


def normalize(values):
    center = values - jnp.mean(values, axis=-1, keepdims=True)
    inverse = lax.rsqrt(jnp.mean(center * center, axis=-1, keepdims=True) + EPSILON)
    return (center * inverse, inverse)


def norm_back(grad_out, normed, inverse, gain):
    scaled = grad_out * gain
    return inverse * (
        scaled
        - jnp.mean(scaled, axis=-1, keepdims=True)
        - normed * jnp.mean(scaled * normed, axis=-1, keepdims=True)
    )


def project(rows, matrix):
    return jnp.einsum("csd,de->cse", rows, matrix, preferred_element_type=jnp.float32)


def project_back(grads, matrix):
    return jnp.einsum("cse,de->csd", grads, matrix, preferred_element_type=jnp.float32)


def outer_sum(rows, grads):
    return jnp.einsum("csd,cse->de", rows, grads, preferred_element_type=jnp.float32)


def row_total(values):
    return jnp.sum(values.astype(jnp.float32), axis=(0, 1))


def fwd_kernel(qb, len_ref, q_ref, k_ref, v_ref, o_ref, e_ref, r_ref):
    S=k_ref.shape[0]
    lane = lax.broadcasted_iota(jnp.int32,(S,128),1)
    kpos = lax.broadcasted_iota(jnp.int32,(1,S),1)
    bias = jnp.where(kpos < len_ref[0], 0.0, -1e30).astype(jnp.float32)
    k = k_ref[...]
    v = v_ref[...]
    first = lane < 64
    k0 = jnp.where(first, k, jnp.zeros_like(k)); k1 = jnp.where(first, jnp.zeros_like(k), k)
    fq = lax.broadcasted_iota(jnp.int32,(qb,128),1) < 64
    for b in range(S//qb):
        rows = pl.ds(b*qb, qb)
        q = q_ref[rows,:]
        outs=[]; rs=[]
        for h,kh in ((0,k0),(1,k1)):
            s = lax.dot_general(q, kh, (((1,),(1,)),((),())), preferred_element_type=jnp.float32) + bias
            m = jnp.max(s, axis=1, keepdims=True)
            e = jnp.exp(s-m)
            l = jnp.sum(e, axis=1, keepdims=True)
            eb = e.astype(jnp.bfloat16)
            e_ref[h, rows, :] = eb
            o = jnp.dot(eb, v, preferred_element_type=jnp.float32)
            outs.append(o); rs.append(1.0/l)
        r = jnp.where(fq, rs[0], rs[1])
        r_ref[rows,:] = r
        o_ref[rows,:] = (jnp.where(fq, outs[0], outs[1])*r).astype(jnp.bfloat16)
def attn_fwd(length, q, k, v, qb=256):
    S,D=q.shape; pairs=D//128
    blk=pl.BlockSpec((S,128), lambda p: (0,p))
    return pl.pallas_call(partial(fwd_kernel,qb), grid=(pairs,),
        in_specs=[pl.BlockSpec(memory_space=pltpu.SMEM), blk, blk, blk],
        out_specs=[blk, pl.BlockSpec((2,S,S), lambda p:(p,0,0)), blk],
        out_shape=[jax.ShapeDtypeStruct((S,D),jnp.bfloat16), jax.ShapeDtypeStruct((2*pairs,S,S),jnp.bfloat16), jax.ShapeDtypeStruct((S,D),jnp.float32)],
        compiler_params=pltpu.CompilerParams(vmem_limit_bytes=56<<20), name="attn_fwd")(length,q,k,v)

def bwd_kernel(qb, q_ref, k_ref, v_ref, do_ref, o_ref, r_ref, e_ref, dq_ref, dk_ref, dv_ref, kt_acc, vt_acc):
    S=k_ref.shape[0]
    lane = lax.broadcasted_iota(jnp.int32,(S,128),1); first = lane<64
    fq = lax.broadcasted_iota(jnp.int32,(qb,128),1) < 64
    k=k_ref[...]; v=v_ref[...]
    z=jnp.zeros_like(k)
    v0=jnp.where(first,v,z); v1=jnp.where(first,z,v)
    for b in range(S//qb):
        rows=pl.ds(b*qb,qb)
        do = do_ref[rows,:].astype(jnp.float32)*r_ref[rows,:]
        dob = do.astype(jnp.bfloat16)
        prod = dob.astype(jnp.float32)*o_ref[rows,:].astype(jnp.float32)
        dall = jnp.sum(prod,axis=1,keepdims=True)
        d0 = jnp.sum(jnp.where(fq,prod,0.0),axis=1,keepdims=True); d1=dall-d0
        dot_ = dob.T
        qt = q_ref[rows,:].T
        dqs=[]
        for h,vh,d in ((0,v0,d0),(1,v1,d1)):
            e = e_ref[h,rows,:]
            dp = lax.dot_general(dob, vh, (((1,),(1,)),((),())), preferred_element_type=jnp.float32)
            ds = (e.astype(jnp.float32)*(dp-d)).astype(jnp.bfloat16)
            dqs.append(jnp.dot(ds,k,preferred_element_type=jnp.float32))
            hr = slice(h*64,h*64+64)
            dv_t = jnp.dot(dot_[hr], e, preferred_element_type=jnp.float32)
            dk_t = jnp.dot(qt[hr], ds, preferred_element_type=jnp.float32)
            if b==0:
                vt_acc[hr,:]=dv_t; kt_acc[hr,:]=dk_t
            else:
                vt_acc[hr,:]+=dv_t; kt_acc[hr,:]+=dk_t
        dq_ref[rows,:] = (jnp.where(fq,dqs[0],dqs[1])*0.125).astype(jnp.bfloat16)
    dk_ref[...] = kt_acc[...].astype(jnp.bfloat16).T
    dv_ref[...] = vt_acc[...].astype(jnp.bfloat16).T
def attn_bwd(q,k,v,do,o,r,e,qb=256):
    S,D=q.shape; pairs=D//128
    blk=pl.BlockSpec((S,128), lambda p: (0,p))
    return pl.pallas_call(partial(bwd_kernel,qb), grid=(pairs,),
        in_specs=[blk]*6+[pl.BlockSpec((2,S,S), lambda p:(p,0,0))],
        out_specs=[blk]*3, out_shape=[jax.ShapeDtypeStruct((S,D),jnp.bfloat16)]*3,
        scratch_shapes=[pltpu.VMEM((128,S),jnp.float32)]*2,
        compiler_params=pltpu.CompilerParams(vmem_limit_bytes=56<<20), name="attn_bwd")(q,k,v,do,o,r,e)


def body(
    cells_in,
    out_grad,
    cell_length,
    cell_place,
    gene_ids,
    attn_norm_gain,
    attn_norm_bias,
    query_weight,
    query_bias,
    key_weight,
    value_weight,
    value_bias,
    out_weight,
    out_bias,
    ffn_norm_gain,
    ffn_norm_bias,
    up_weight,
    up_bias,
    down_weight,
    down_bias,
):
    shards = (
        attn_norm_gain,
        attn_norm_bias,
        query_weight,
        query_bias,
        key_weight,
        value_weight,
        value_bias,
        out_weight,
        out_bias,
        ffn_norm_gain,
        ffn_norm_bias,
        up_weight,
        up_bias,
        down_weight,
        down_bias,
    )
    gathered = (
        lax.all_gather(shards[0], "fsdp", axis=0, tiled=True),
        lax.all_gather(shards[1], "fsdp", axis=0, tiled=True),
        lax.all_gather(shards[2], "fsdp", axis=0, tiled=True),
        lax.all_gather(shards[3], "fsdp", axis=0, tiled=True),
        lax.all_gather(shards[4], "fsdp", axis=0, tiled=True),
        lax.all_gather(shards[5], "fsdp", axis=0, tiled=True),
        lax.all_gather(shards[6], "fsdp", axis=0, tiled=True),
        lax.all_gather(shards[7], "fsdp", axis=0, tiled=True),
        lax.all_gather(shards[8], "fsdp", axis=0, tiled=True),
        lax.all_gather(shards[9], "fsdp", axis=0, tiled=True),
        lax.all_gather(shards[10], "fsdp", axis=0, tiled=True),
        lax.all_gather(shards[11], "fsdp", axis=0, tiled=True),
        lax.all_gather(shards[12], "fsdp", axis=0, tiled=True),
        lax.all_gather(shards[13], "fsdp", axis=0, tiled=True),
        lax.all_gather(shards[14], "fsdp", axis=0, tiled=True),
    )
    (
        gain_one,
        shift_one,
        query_w,
        query_b,
        key_w,
        value_w,
        value_b,
        out_w,
        out_b,
        gain_two,
        shift_two,
        up_w,
        up_b,
        down_w,
        down_b,
    ) = gathered
    cell_count = cells_in.shape[0]
    seq_length = cells_in.shape[1]
    model_width = cells_in.shape[2]
    factor = HEAD_DIM ** (-0.5)
    head_shape = (cell_count, seq_length, HEADS, HEAD_DIM)
    slot_index = lax.axis_index(("dp", "fsdp")) * cell_count + jnp.arange(cell_count)
    cell_lens = cell_length[cell_place[slot_index]]
    key_live = jnp.arange(seq_length)[None, :] < cell_lens[:, None]
    block_rows = min(512, seq_length)
    inputs = cells_in.astype(jnp.float32)
    normed_one, inverse_one = normalize(inputs)
    attn_in = (normed_one * gain_one.astype(jnp.float32) + shift_one.astype(jnp.float32)).astype(
        jnp.bfloat16
    )
    query_rows = (
        (project(attn_in, query_w) + query_b.astype(jnp.float32))
        .astype(jnp.bfloat16)
        .reshape(head_shape)
    )
    key_rows = project(attn_in, key_w).astype(jnp.bfloat16).reshape(head_shape)
    value_rows = (
        (project(attn_in, value_w) + value_b.astype(jnp.float32))
        .astype(jnp.bfloat16)
        .reshape(head_shape)
    )
    query_flat = query_rows.reshape(seq_length, model_width) * jnp.asarray(factor, jnp.bfloat16)
    key_flat = key_rows.reshape(seq_length, model_width)
    value_flat = value_rows.reshape(seq_length, model_width)
    attn_flat, raised, inverse_sum = attn_fwd(cell_lens.astype(jnp.int32), query_flat, key_flat, value_flat, 512)
    attn_out = attn_flat[None]
    residual = inputs + project(attn_out, out_w) + out_b.astype(jnp.float32)
    normed_two, inverse_two = normalize(residual)
    ffn_in = (normed_two * gain_two.astype(jnp.float32) + shift_two.astype(jnp.float32)).astype(
        jnp.bfloat16
    )
    pre_act = project(ffn_in, up_w) + up_b.astype(jnp.float32)
    hidden = jax.nn.gelu(pre_act, approximate=False).astype(jnp.bfloat16)
    result = residual + project(hidden, down_w) + down_b.astype(jnp.float32)
    block_out = result.astype(jnp.bfloat16)
    again = (
        lax.all_gather(shards[0], "fsdp", axis=0, tiled=True),
        lax.all_gather(shards[1], "fsdp", axis=0, tiled=True),
        lax.all_gather(shards[2], "fsdp", axis=0, tiled=True),
        lax.all_gather(shards[3], "fsdp", axis=0, tiled=True),
        lax.all_gather(shards[4], "fsdp", axis=0, tiled=True),
        lax.all_gather(shards[5], "fsdp", axis=0, tiled=True),
        lax.all_gather(shards[6], "fsdp", axis=0, tiled=True),
        lax.all_gather(shards[7], "fsdp", axis=0, tiled=True),
        lax.all_gather(shards[8], "fsdp", axis=0, tiled=True),
        lax.all_gather(shards[9], "fsdp", axis=0, tiled=True),
        lax.all_gather(shards[10], "fsdp", axis=0, tiled=True),
        lax.all_gather(shards[11], "fsdp", axis=0, tiled=True),
        lax.all_gather(shards[12], "fsdp", axis=0, tiled=True),
        lax.all_gather(shards[13], "fsdp", axis=0, tiled=True),
        lax.all_gather(shards[14], "fsdp", axis=0, tiled=True),
    )
    (
        gain_one_b,
        shift_one_b,
        query_wb,
        query_bb,
        key_wb,
        value_wb,
        value_bb,
        out_wb,
        out_bb,
        gain_two_b,
        shift_two_b,
        up_wb,
        up_bb,
        down_wb,
        down_bb,
    ) = again
    grad_down_w = outer_sum(hidden, out_grad)
    grad_down_b = row_total(out_grad)
    grad_hidden = project_back(out_grad, down_wb)
    unused_value, gelu_back = jax.vjp(partial(jax.nn.gelu, approximate=False), pre_act)
    grad_pre = gelu_back(grad_hidden)[0].astype(jnp.bfloat16)
    grad_up_w = outer_sum(ffn_in, grad_pre)
    grad_up_b = row_total(grad_pre)
    grad_ffn_in = project_back(grad_pre, up_wb)
    grad_gain_two = jnp.sum(grad_ffn_in * normed_two, axis=(0, 1))
    grad_shift_two = jnp.sum(grad_ffn_in, axis=(0, 1))
    grad_residual = out_grad.astype(jnp.float32) + norm_back(
        grad_ffn_in, normed_two, inverse_two, gain_two_b.astype(jnp.float32)
    )
    grad_branch = grad_residual.astype(jnp.bfloat16)
    grad_out_w = outer_sum(attn_out, grad_branch)
    grad_out_b = row_total(grad_branch)
    grad_mixed = project_back(grad_branch, out_wb).astype(jnp.bfloat16).reshape(head_shape)
    grad_query_rows, grad_key_rows, grad_value_rows = (
        part[None]
        for part in attn_bwd(
            query_flat, key_flat, value_flat, grad_mixed.reshape(seq_length, model_width),
            attn_flat, inverse_sum, raised, 512,
        )
    )
    grad_query_w = outer_sum(attn_in, grad_query_rows)
    grad_query_b = row_total(grad_query_rows)
    grad_key_w = outer_sum(attn_in, grad_key_rows)
    grad_value_w = outer_sum(attn_in, grad_value_rows)
    grad_value_b = row_total(grad_value_rows)
    grad_attn_in = (
        project_back(grad_query_rows, query_wb)
        + project_back(grad_key_rows, key_wb)
        + project_back(grad_value_rows, value_wb)
    )
    grad_gain_one = jnp.sum(grad_attn_in * normed_one, axis=(0, 1))
    grad_shift_one = jnp.sum(grad_attn_in, axis=(0, 1))
    input_grad = (
        grad_residual
        + norm_back(grad_attn_in, normed_one, inverse_one, gain_one_b.astype(jnp.float32))
    ).astype(jnp.bfloat16)
    local_grads = (
        grad_gain_one,
        grad_shift_one,
        grad_query_w,
        grad_query_b,
        grad_key_w,
        grad_value_w,
        grad_value_b,
        grad_out_w,
        grad_out_b,
        grad_gain_two,
        grad_shift_two,
        grad_up_w,
        grad_up_b,
        grad_down_w,
        grad_down_b,
    )
    shard_grads = (
        lax.psum_scatter(
            local_grads[0].astype(jnp.bfloat16), "fsdp", scatter_dimension=0, tiled=True
        ).astype(jnp.float32),
        lax.psum_scatter(
            local_grads[1].astype(jnp.bfloat16), "fsdp", scatter_dimension=0, tiled=True
        ).astype(jnp.float32),
        lax.psum_scatter(
            local_grads[2].astype(jnp.bfloat16), "fsdp", scatter_dimension=0, tiled=True
        ).astype(jnp.float32),
        lax.psum_scatter(
            local_grads[3].astype(jnp.bfloat16), "fsdp", scatter_dimension=0, tiled=True
        ).astype(jnp.float32),
        lax.psum_scatter(
            local_grads[4].astype(jnp.bfloat16), "fsdp", scatter_dimension=0, tiled=True
        ).astype(jnp.float32),
        lax.psum_scatter(
            local_grads[5].astype(jnp.bfloat16), "fsdp", scatter_dimension=0, tiled=True
        ).astype(jnp.float32),
        lax.psum_scatter(
            local_grads[6].astype(jnp.bfloat16), "fsdp", scatter_dimension=0, tiled=True
        ).astype(jnp.float32),
        lax.psum_scatter(
            local_grads[7].astype(jnp.bfloat16), "fsdp", scatter_dimension=0, tiled=True
        ).astype(jnp.float32),
        lax.psum_scatter(
            local_grads[8].astype(jnp.bfloat16), "fsdp", scatter_dimension=0, tiled=True
        ).astype(jnp.float32),
        lax.psum_scatter(
            local_grads[9].astype(jnp.bfloat16), "fsdp", scatter_dimension=0, tiled=True
        ).astype(jnp.float32),
        lax.psum_scatter(
            local_grads[10].astype(jnp.bfloat16), "fsdp", scatter_dimension=0, tiled=True
        ).astype(jnp.float32),
        lax.psum_scatter(
            local_grads[11].astype(jnp.bfloat16), "fsdp", scatter_dimension=0, tiled=True
        ).astype(jnp.float32),
        lax.psum_scatter(
            local_grads[12].astype(jnp.bfloat16), "fsdp", scatter_dimension=0, tiled=True
        ).astype(jnp.float32),
        lax.psum_scatter(
            local_grads[13].astype(jnp.bfloat16), "fsdp", scatter_dimension=0, tiled=True
        ).astype(jnp.float32),
        lax.psum_scatter(
            local_grads[14].astype(jnp.bfloat16), "fsdp", scatter_dimension=0, tiled=True
        ).astype(jnp.float32),
    )
    total_grads = lax.psum(
        (
            shard_grads[0],
            shard_grads[1],
            shard_grads[2],
            shard_grads[3],
            shard_grads[4],
            shard_grads[5],
            shard_grads[6],
            shard_grads[7],
            shard_grads[8],
            shard_grads[9],
            shard_grads[10],
            shard_grads[11],
            shard_grads[12],
            shard_grads[13],
            shard_grads[14],
        ),
        "dp",
    )
    live_rows = key_live.astype(jnp.int32).reshape(-1)
    local_tally = jax.ops.segment_sum(live_rows, gene_ids.reshape(-1), num_segments=VOCAB)
    gene_counts = lax.psum(local_tally, ("dp", "fsdp"))
    return (block_out, input_grad) + tuple(total_grads) + (gene_counts,)


def solution(mesh):
    in_specs = (
        P(("dp", "fsdp"), None, None),
        P(("dp", "fsdp"), None, None),
        P(),
        P(),
        P(("dp", "fsdp"), None),
        P("fsdp"),
        P("fsdp"),
        P("fsdp", None),
        P("fsdp"),
        P("fsdp", None),
        P("fsdp", None),
        P("fsdp"),
        P("fsdp", None),
        P("fsdp"),
        P("fsdp"),
        P("fsdp"),
        P("fsdp", None),
        P("fsdp"),
        P("fsdp", None),
        P("fsdp"),
    )
    out_specs = (
        P(("dp", "fsdp"), None, None),
        P(("dp", "fsdp"), None, None),
        P("fsdp"),
        P("fsdp"),
        P("fsdp", None),
        P("fsdp"),
        P("fsdp", None),
        P("fsdp", None),
        P("fsdp"),
        P("fsdp", None),
        P("fsdp"),
        P("fsdp"),
        P("fsdp"),
        P("fsdp", None),
        P("fsdp"),
        P("fsdp", None),
        P("fsdp"),
        P(),
    )
    return jax.shard_map(body, mesh=mesh, in_specs=in_specs, out_specs=out_specs, check_vma=False)
```

```python
from functools import partial

import jax
import jax.numpy as jnp
from jax import lax
from jax.experimental import pallas as pl
from jax.experimental.pallas import tpu as pltpu
from jax.sharding import PartitionSpec as P

HEADS = 12
HEAD_DIM = 64
VOCAB = 36000
EPSILON = 1e-05
NEGATIVE = -1e30
PAIR = 2 * HEAD_DIM
TALLY_ROWS = 288

F32 = jnp.float32
BF16 = jnp.bfloat16
VMEM_LIMIT = 60 << 20

GAIN_ONE, SHIFT_ONE, OUT_B, GAIN_TWO, SHIFT_TWO, DOWN_B, QUERY_B, VALUE_B, UP_B = range(9)
SUM_ROWS = 16

WHOLE = pl.BlockSpec(memory_space=pl.ANY)
SCALARS = pl.BlockSpec(memory_space=pltpu.SMEM)


LIGHT = pl.CostEstimate(flops=1024, transcendentals=0, bytes_accessed=1024)


def call(kernel, name, grid, in_specs, out_specs, out_shape, scratch=(), prefetch=0, aliases=None):
    return pl.pallas_call(
        kernel,
        grid_spec=pltpu.PrefetchScalarGridSpec(
            num_scalar_prefetch=prefetch,
            grid=grid,
            in_specs=in_specs,
            out_specs=out_specs,
            scratch_shapes=scratch,
        ),
        out_shape=out_shape,
        input_output_aliases=aliases or {},
        compiler_params=pltpu.CompilerParams(vmem_limit_bytes=VMEM_LIMIT),
        cost_estimate=LIGHT,
        name=name,
    )


def shape(dims, dtype):
    return jax.ShapeDtypeStruct(dims, dtype)


def dot(left, right):
    return jnp.dot(left, right, preferred_element_type=F32)


def dot_nt(left, right):
    return lax.dot_general(left, right, (((1,), (1,)), ((), ())), preferred_element_type=F32)


def moments(values):
    width = values.shape[-1]
    center = values - jnp.sum(values, axis=-1, keepdims=True) * (1.0 / width)
    spread = jnp.sum(center * center, axis=-1, keepdims=True) * (1.0 / width)
    inverse = lax.rsqrt(spread + EPSILON)
    return center * inverse, inverse


def norm_back(grad_out, normed, inverse, gain):
    width = normed.shape[-1]
    scaled = grad_out * gain
    mean = jnp.sum(scaled, axis=-1, keepdims=True) * (1.0 / width)
    along = jnp.sum(scaled * normed, axis=-1, keepdims=True) * (1.0 / width)
    return inverse * (scaled - mean - normed * along)


def start_all(copies):
    for copy in copies:
        copy.start()


def wait_all(copies):
    for copy in copies:
        copy.wait()


def aligned(begin, size, unit):
    return pl.ds(pl.multiple_of(begin, unit), size)


def pack_kernel(slots, where, *refs):
    pairs, (o, up, down), small, (first, second) = (
        refs[: 3 * slots], refs[3 * slots : 3 * slots + 3], refs[3 * slots + 3 : -2], refs[-2:],
    )
    rows, half = o.shape
    deep, width = down.shape
    for number, ref in enumerate(pairs):
        first[0:rows, number * PAIR : (number + 1) * PAIR] = ref[...]
    first[rows:, :] = jnp.zeros((first.shape[0] - rows, first.shape[1]), BF16)
    for number, ref in enumerate(small):
        value = ref[...].astype(F32).reshape(1, -1).astype(BF16)
        first[rows + number : rows + number + 1, 0 : ref.shape[0]] = value
    second[0:deep, :] = down[...]
    row = deep
    for begin in range(0, up.shape[1], width):
        second[row : row + rows, :] = up[:, begin : begin + width]
        row += rows
    second[row : row + rows, 0:half] = o[...]
    second[row : row + rows, half:width] = jnp.zeros((rows, width - half), BF16)


def pack(where, q, k, v, o, up, down, small):
    rows, width = q.shape[0] // 4, q.shape[1]
    slots = width // PAIR // 2
    deep = down.shape[0] // 8
    first = (rows + SUM_ROWS, 3 * PAIR * slots)
    second = (deep + rows * (up.shape[1] // 2 // width + 1), width)
    return call(
        partial(pack_kernel, slots),
        "pack",
        (1,),
        [
            pl.BlockSpec((rows, PAIR), lambda i, w, s=slot: (w[1], slots * w[2] + s))
            for slot in range(slots)
            for _ in range(3)
        ]
        + [
            pl.BlockSpec((rows, o.shape[1] // 2), lambda i, w: (w[1], w[2])),
            pl.BlockSpec((rows, up.shape[1] // 2), lambda i, w: (w[1], w[2])),
            pl.BlockSpec((deep, width), lambda i, w: (4 * w[2] + w[1], 0)),
        ]
        + [pl.BlockSpec(part.shape, lambda i, w: (0,)) for part in small],
        [pl.BlockSpec(first, lambda i, w: (0, 0)), pl.BlockSpec(second, lambda i, w: (0, 0))],
        [shape(first, BF16), shape(second, BF16)],
        prefetch=1,
    )(where, *([q, k, v] * slots), o, up, down, *small)


def split_kernel(parts, *refs):
    ins, outs = refs[: -len(parts)], refs[-len(parts) :]
    for (row, column), out in zip(parts, outs):
        rows, columns = out.shape[1:]
        for number, ref in enumerate(ins):
            out[number] = ref[row : row + rows, column : column + columns]


def split(arrays, parts):
    full = arrays[0].shape
    return call(
        partial(split_kernel, [part[:2] for part in parts]),
        "split",
        (1,),
        [pl.BlockSpec(full, lambda i: (0, 0))] * len(arrays),
        [pl.BlockSpec((len(arrays), *part[2:]), lambda i: (0, 0, 0)) for part in parts],
        [shape((len(arrays), *part[2:]), BF16) for part in parts],
    )(*arrays)


def remote_places(where, pieces, count):
    z, quad, core = where[0], where[1], where[2]
    for number, piece in enumerate(pieces):
        turn, side = number % 4, number // 4
        for step in range(1, count):
            yield piece, step - 1, z ^ step, quad ^ turn, core ^ side


def pair_copies(where, own, pieces, full, sems, count, slot):
    shard = own[0].shape[0]
    slots = own[0].shape[1] // PAIR // 2
    rows, half = pieces[0].shape[1:]
    copies = []
    for kind, ref in enumerate(own):
        for core in range(2):
            for number in range(half // (3 * PAIR)):
                source = (core * slots + slot + number) * PAIR
                target = core * half + (3 * number + kind) * PAIR
                copies.append(
                    pltpu.make_async_copy(
                        ref.at[:, source : source + PAIR],
                        full.at[aligned(where[0] * shard, shard, 16), target : target + PAIR],
                        sems.at[len(copies)],
                    )
                )
    for piece, step, z, quad, core in remote_places(where, pieces, count):
        copies.append(
            pltpu.make_async_copy(
                piece.at[step],
                full.at[aligned(z * shard + quad * rows, rows, 16), aligned(core * half, half, 128)],
                sems.at[len(copies)],
            )
        )
    return copies


def column_copies(where, own, pieces, full, sems, count, row):
    shard = own.shape[0]
    rows, half = shard // 4, own.shape[1] // 2
    width = pieces[0].shape[2]
    copies = [pltpu.make_async_copy(own, full.at[aligned(where[0] * shard, shard, 16)], sems.at[0])]
    for piece, step, z, quad, core in remote_places(where, pieces, count):
        for number, begin in enumerate(range(0, half, width)):
            size = min(width, half - begin)
            copies.append(
                pltpu.make_async_copy(
                    piece.at[step, row + number * rows : row + (number + 1) * rows, 0:size],
                    full.at[
                        aligned(z * shard + quad * rows, rows, 16),
                        aligned(core * half + begin, size, 128),
                    ],
                    sems.at[len(copies)],
                )
            )
    return copies


def row_copies(where, own, pieces, full, sems, count):
    shard = own.shape[0]
    rows = pieces[0].shape[1]
    copies = [
        pltpu.make_async_copy(own, full.at[aligned(where[0] * shard, shard, 16)], sems.at[0])
    ]
    for piece, step, z, quad, core in remote_places(where, pieces, count):
        copies.append(
            pltpu.make_async_copy(
                piece.at[step],
                full.at[aligned(z * shard + core * 4 * rows + quad * rows, rows, 16)],
                sems.at[len(copies)],
            )
        )
    return copies


def copy_count(count):
    return 1 + 8 * (count - 1)


def norm_kernel(count, shard, where, x_ref, *rest):
    small, (a_ref, t_ref, vec_ref, up_ref, bias_ref) = rest[:count], rest[count:]

    @pl.when(pl.program_id(0) == 0)
    def _():
        wide = up_ref.shape[1] // count
        for owner in range(count):
            value = small[0][...].astype(F32)
            for step in range(1, count):
                here = (where[0] ^ step) == owner
                value = jnp.where(here, small[step][...].astype(F32), value)
            vec_ref[:, owner * shard : (owner + 1) * shard] = value[0:8, 0:shard]
            up_ref[:, owner * wide : (owner + 1) * wide] = value[UP_B : UP_B + 1, 0:wide]
        slots = vec_ref.shape[1] // PAIR // 2
        for core in range(2):
            for slot in range(slots):
                span = slice((core * slots + slot) * PAIR, (core * slots + slot + 1) * PAIR)
                begin = 3 * PAIR * spot(slot, core, slots)
                bias_ref[:, begin : begin + PAIR] = vec_ref[QUERY_B : QUERY_B + 1, span]
                bias_ref[:, begin + PAIR : begin + 2 * PAIR] = jnp.zeros((1, PAIR), F32)
                bias_ref[:, begin + 2 * PAIR : begin + 3 * PAIR] = vec_ref[
                    VALUE_B : VALUE_B + 1, span
                ]

    normed, _ = moments(x_ref[...].astype(F32))
    rows = normed * vec_ref[GAIN_ONE : GAIN_ONE + 1, :] + vec_ref[SHIFT_ONE : SHIFT_ONE + 1, :]
    rows = rows.astype(BF16)
    a_ref[...] = rows
    t_ref[...] = rows.T


def spot(slot, core, slots):
    return jnp.where(slot == 0, core, 1 + core * (slots - 1) + slot) if not isinstance(
        slot, int
    ) else (core if slot == 0 else 1 + core * (slots - 1) + slot)


def first_norm(where, inputs, small, shard, wide, block=256):
    seq, width = inputs.shape
    count = len(small)
    fixed = lambda a, b: pl.BlockSpec((a, b), lambda i: (0, 0))
    last = small[0].shape[0] // SUM_ROWS - 1
    return call(
        partial(norm_kernel, count, shard),
        "first_norm",
        (seq // block,),
        [SCALARS, pl.BlockSpec((block, width), lambda i: (i, 0))]
        + [pl.BlockSpec((SUM_ROWS, part.shape[1]), lambda i: (last, 0)) for part in small],
        [
            pl.BlockSpec((block, width), lambda i: (i, 0)),
            pl.BlockSpec((width, block), lambda i: (0, i)),
            fixed(8, width),
            fixed(1, wide),
            fixed(1, 3 * width),
        ],
        [
            shape((seq, width), BF16),
            shape((width, seq), BF16),
            shape((8, width), F32),
            shape((1, wide), F32),
            shape((1, 3 * width), F32),
        ],
    )(where, inputs, *small)


def qkv_kernel(count, slot, slots, where, a_ref, bias_ref, q, k, v, *rest):
    pieces = rest[:8]
    out_ref, kept_ref, full, sems, out_sems = rest[-5:]
    step, part = pl.program_id(0), pl.program_id(1)
    half = pieces[0].shape[2]

    def keep():
        return [
            pltpu.make_async_copy(
                full.at[:, core * half : (core + 1) * half],
                kept_ref.at[
                    :, (core * slots + slot) * 3 * PAIR : (core * slots + slot) * 3 * PAIR + half
                ],
                out_sems.at[core],
            )
            for core in range(2)
        ]

    @pl.when((step == 0) & (part == 0))
    def _():
        copies = pair_copies(where, (q, k, v), pieces, full, sems, count, slot)
        start_all(copies)
        wait_all(copies)
        start_all(keep())

    wide = out_ref.shape[1]
    column = pl.multiple_of(part * wide, wide)
    rows = (dot(a_ref[...], full[:, pl.ds(column, wide)]) + bias_ref[...]).astype(BF16)
    for begin in range(0, wide, PAIR):
        value = rows[:, begin : begin + PAIR]
        if begin // PAIR % 3 == 0:
            value = value * jnp.asarray(HEAD_DIM**-0.5, BF16)
        out_ref[:, begin : begin + PAIR] = value

    @pl.when((step == pl.num_programs(0) - 1) & (part == pl.num_programs(1) - 1))
    def _():
        wait_all(keep())


def project_qkv(where, attn_in, bias, own, pieces, count, slot, kept=(), block=512):
    seq, width = attn_in.shape
    slots = own[0].shape[1] // PAIR // 2
    half = pieces[0].shape[2]
    wide, parts = (2 * half, 1) if slot == 0 else (half, 2)
    first = 0 if slot == 0 else 1
    copies = copy_count(count) - 1 + 2 * half // PAIR
    return call(
        partial(qkv_kernel, count, slot, slots),
        "project_qkv",
        (seq // block, parts),
        [
            SCALARS,
            pl.BlockSpec((block, width), lambda i, n: (i, 0)),
            pl.BlockSpec((1, wide), lambda i, n: (0, first + n)),
        ]
        + [WHOLE] * (11 + len(kept)),
        [pl.BlockSpec((block, wide), lambda i, n: (i, first + n)), WHOLE],
        [shape((seq, 3 * width), BF16), shape((width, 3 * width), BF16)],
        [
            pltpu.VMEM((width, 2 * half), BF16),
            pltpu.SemaphoreType.DMA((copies,)),
            pltpu.SemaphoreType.DMA((2,)),
        ],
        aliases={14 + i: i for i in range(len(kept))},
    )(where, attn_in, bias, *own, *pieces, *kept)


def attend_kernel(where, lengths, places, q_ref, k_ref, v_ref, *rest):
    o_ref, t_ref, e_ref, r_ref = rest[-4:]
    seq, block = k_ref.shape[0], q_ref.shape[0]
    first = lax.broadcasted_iota(jnp.int32, (seq, PAIR), 1) < HEAD_DIM
    here = lax.broadcasted_iota(jnp.int32, (block, PAIR), 1) < HEAD_DIM
    place = lax.broadcasted_iota(jnp.int32, (1, seq), 1)
    bias = jnp.where(place < lengths[places[where[3]]], 0.0, NEGATIVE).astype(F32)
    queries, keys, values = q_ref[...], k_ref[...], v_ref[...]
    zeros = jnp.zeros_like(keys)
    blended, shares = [], []
    for head in range(2):
        head_keys = jnp.where(first, keys, zeros) if head == 0 else jnp.where(first, zeros, keys)
        scores = dot_nt(queries, head_keys) + bias
        raised = jnp.exp(scores - jnp.max(scores, axis=1, keepdims=True))
        shares.append(1.0 / jnp.sum(raised, axis=1, keepdims=True))
        raised = raised.astype(BF16)
        e_ref[head] = raised
        blended.append(dot(raised, values))
    share = jnp.where(here, shares[0], shares[1])
    r_ref[...] = share
    mixed = (jnp.where(here, blended[0], blended[1]) * share).astype(BF16)
    o_ref[...] = mixed
    t_ref[...] = mixed.T


def attend(cell, qkv, spots, pairs, kept=(), block=512):
    seq, wide = qkv.shape
    total = wide // (3 * PAIR)
    there = lambda p: spots[0] + (spots[1] - spots[0]) * p
    here = lambda p: pairs[0] + (pairs[1] - pairs[0]) * p
    return call(
        attend_kernel,
        "attend",
        (2, seq // block),
        [
            SCALARS,
            SCALARS,
            SCALARS,
            pl.BlockSpec((block, PAIR), lambda p, b: (b, 3 * there(p))),
            pl.BlockSpec((seq, PAIR), lambda p, b: (0, 3 * there(p) + 1)),
            pl.BlockSpec((seq, PAIR), lambda p, b: (0, 3 * there(p) + 2)),
        ]
        + [WHOLE] * len(kept),
        [
            pl.BlockSpec((block, PAIR), lambda p, b: (b, here(p))),
            pl.BlockSpec((PAIR, block), lambda p, b: (here(p), b)),
            pl.BlockSpec((2, block, seq), lambda p, b: (here(p), b, 0)),
            pl.BlockSpec((block, PAIR), lambda p, b: (b, here(p))),
        ],
        [
            shape((seq, total * PAIR), BF16),
            shape((total * PAIR, seq), BF16),
            shape((2 * total, seq, seq), BF16),
            shape((seq, total * PAIR), F32),
        ],
        aliases={6 + i: i for i in range(len(kept))},
    )(*cell, qkv, qkv, qkv, *kept)


ERF_P = 0.3275911 * 2.0**-0.5
ERF_A = (0.254829592, -0.284496736, 1.421413741, -1.453152027, 1.061405429)


def gelu_parts(values):
    bell = jnp.exp(values * values * -0.5)
    ratio = 1.0 / (1.0 + ERF_P * jnp.abs(values))
    tail = 0.5 * ERF_A[4]
    for term in ERF_A[3::-1]:
        tail = tail * ratio + 0.5 * term
    tail = tail * ratio * bell
    under = jnp.where(values > 0, 1.0 - tail, tail)
    return values * under, under + values * bell * 0.3989422804014327


def up_kernel(count, where, x_ref, mix_ref, vec_ref, bias_ref, out_own, up_own, *rest):
    pieces = rest[:8]
    res_ref, fit_ref, hid_ref, hidt_ref, slope_ref, out_full, up_full, sem_a, sem_b = rest[8:]

    @pl.when(pl.program_id(0) == 0)
    def _():
        rows = up_own.shape[0] // 4
        blocks = up_own.shape[1] // 2 // pieces[0].shape[2]
        copies = column_copies(where, out_own, pieces, out_full, sem_a, count, blocks * rows)
        copies += column_copies(where, up_own, pieces, up_full, sem_b, count, 0)
        start_all(copies)
        wait_all(copies)

    mixed = x_ref[...].astype(F32) + vec_ref[OUT_B : OUT_B + 1, :]
    mixed = mixed + dot(mix_ref[...], out_full[...])
    res_ref[...] = mixed
    normed, _ = moments(mixed)
    rows = normed * vec_ref[GAIN_TWO : GAIN_TWO + 1, :] + vec_ref[SHIFT_TWO : SHIFT_TWO + 1, :]
    rows = rows.astype(BF16)
    fit_ref[...] = rows.T
    chunk = 768
    for begin in range(0, up_full.shape[1], chunk):
        span = slice(begin, begin + chunk)
        value, slope = gelu_parts(dot(rows, up_full[:, span]) + bias_ref[:, span])
        value = value.astype(BF16)
        hid_ref[:, span] = value
        hidt_ref[span, :] = value.T
        slope_ref[:, span] = slope.astype(BF16)


def feed_up(where, inputs, mixed, vectors, bias, out_own, up_own, pieces, count, block=256):
    seq, width = inputs.shape
    wide = up_own.shape[1]
    row = lambda n: pl.BlockSpec((block, n), lambda i: (i, 0))
    fixed = lambda a, b: pl.BlockSpec((a, b), lambda i: (0, 0))
    return call(
        partial(up_kernel, count),
        "feed_up",
        (seq // block,),
        [SCALARS, row(width), row(width), fixed(*vectors.shape), fixed(1, wide)] + [WHOLE] * 10,
        [
            row(width),
            pl.BlockSpec((width, block), lambda i: (0, i)),
            row(wide),
            pl.BlockSpec((wide, block), lambda i: (0, i)),
            row(wide),
            fixed(width, width),
            fixed(width, wide),
        ],
        [
            shape((seq, width), F32),
            shape((width, seq), BF16),
            shape((seq, wide), BF16),
            shape((wide, seq), BF16),
            shape((seq, wide), BF16),
            shape((width, width), BF16),
            shape((width, wide), BF16),
        ],
        [pltpu.SemaphoreType.DMA((2 * copy_count(count),))] * 2,
    )(where, inputs, mixed, vectors, bias, out_own, up_own, *pieces)


def down_kernel(count, where, res_ref, hid_ref, slope_ref, grad_ref, vec_ref, own, *rest):
    pieces, (out_ref, pre_ref, presum_ref, gradsum_ref, full, sems) = rest[:8], rest[8:]

    @pl.when(pl.program_id(0) == 0)
    def _():
        copies = row_copies(where, own, pieces, full, sems, count)
        start_all(copies)
        presum_ref[...] = jnp.zeros_like(presum_ref)
        gradsum_ref[...] = jnp.zeros_like(gradsum_ref)
        wait_all(copies)

    result = res_ref[...] + vec_ref[DOWN_B : DOWN_B + 1, :] + dot(hid_ref[...], full[...])
    out_ref[...] = result.astype(BF16)
    grads = grad_ref[...]
    gradsum_ref[...] += jnp.sum(grads.astype(F32), axis=0, keepdims=True)
    chunk = 768
    for begin in range(0, full.shape[0], chunk):
        span = slice(begin, begin + chunk)
        pre = dot_nt(grads, full[span, :]) * slope_ref[:, span].astype(F32)
        pre = pre.astype(BF16)
        pre_ref[:, span] = pre
        presum_ref[:, span] += jnp.sum(pre.astype(F32), axis=0, keepdims=True)


def feed_down(where, residual, hidden, slope, out_grad, vectors, own, pieces, count, block=256):
    seq, width = residual.shape
    wide = hidden.shape[1]
    row = lambda n: pl.BlockSpec((block, n), lambda i: (i, 0))
    fixed = lambda a, b: pl.BlockSpec((a, b), lambda i: (0, 0))
    return call(
        partial(down_kernel, count),
        "feed_down",
        (seq // block,),
        [SCALARS, row(width), row(wide), row(wide), row(width), fixed(*vectors.shape)]
        + [WHOLE] * 9,
        [row(width), row(wide), fixed(1, wide), fixed(1, width)],
        [
            shape((seq, width), BF16),
            shape((seq, wide), BF16),
            shape((1, wide), F32),
            shape((1, width), F32),
        ],
        [pltpu.VMEM((wide, width), BF16), pltpu.SemaphoreType.DMA((copy_count(count),))],
    )(where, residual, hidden, slope, out_grad, vectors, own, *pieces)


def residual_kernel(
    pre_ref, res_ref, grad_ref, vec_ref, up_ref, out_ref, gres_ref, gb_ref, gao_ref, sums_ref
):
    @pl.when(pl.program_id(0) == 0)
    def _():
        sums_ref[...] = jnp.zeros_like(sums_ref)

    grad_in = dot_nt(pre_ref[...], up_ref[...])
    normed, inverse = moments(res_ref[...])
    gain = vec_ref[GAIN_TWO : GAIN_TWO + 1, :]
    grad_res = grad_ref[...].astype(F32) + norm_back(grad_in, normed, inverse, gain)
    gres_ref[...] = grad_res
    branch = grad_res.astype(BF16)
    gb_ref[...] = branch
    gao_ref[...] = dot_nt(branch, out_ref[...]).astype(BF16)
    sums_ref[0:1, :] += jnp.sum(grad_in * normed, axis=0, keepdims=True)
    sums_ref[1:2, :] += jnp.sum(grad_in, axis=0, keepdims=True)
    sums_ref[2:3, :] += jnp.sum(branch.astype(F32), axis=0, keepdims=True)


def residual_back(grad_pre, residual, out_grad, vectors, up_full, out_full, block=256):
    seq, width = residual.shape
    wide = grad_pre.shape[1]
    row = lambda n: pl.BlockSpec((block, n), lambda i: (i, 0))
    fixed = lambda a, b: pl.BlockSpec((a, b), lambda i: (0, 0))
    return call(
        residual_kernel,
        "residual_back",
        (seq // block,),
        [row(wide), row(width), row(width), fixed(*vectors.shape), fixed(width, wide), fixed(width, width)],
        [row(width), row(width), row(width), fixed(8, width)],
        [
            shape((seq, width), F32),
            shape((seq, width), BF16),
            shape((seq, width), BF16),
            shape((8, width), F32),
        ],
    )(grad_pre, residual, out_grad, vectors, up_full, out_full)


def attend_back_kernel(
    where, q_ref, k_ref, v_ref, do_ref, o_ref, r_ref, e_ref, *rest
):
    out_ref, sum_ref, k_acc, v_acc = rest[-4:]
    seq, block = k_ref.shape[0], q_ref.shape[0]
    step, last = pl.program_id(1), pl.num_programs(1) - 1
    first = lax.broadcasted_iota(jnp.int32, (seq, PAIR), 1) < HEAD_DIM
    here = lax.broadcasted_iota(jnp.int32, (block, PAIR), 1) < HEAD_DIM
    keys, values, queries = k_ref[...], v_ref[...], q_ref[...]
    zeros = jnp.zeros_like(values)

    @pl.when(step == 0)
    def _():
        k_acc[...] = jnp.zeros_like(k_acc)
        v_acc[...] = jnp.zeros_like(v_acc)

    grads = (do_ref[...].astype(F32) * r_ref[...]).astype(BF16)
    product = grads.astype(F32) * o_ref[...].astype(F32)
    whole = jnp.sum(product, axis=1, keepdims=True)
    part = jnp.sum(jnp.where(here, product, 0.0), axis=1, keepdims=True)
    inner = (part, whole - part)
    grads_t, queries_t = grads.T, queries.T
    grad_queries = []
    for head in range(2):
        head_values = (
            jnp.where(first, values, zeros) if head == 0 else jnp.where(first, zeros, values)
        )
        raised = e_ref[head]
        grad_shares = dot_nt(grads, head_values)
        grad_scores = (raised.astype(F32) * (grad_shares - inner[head])).astype(BF16)
        grad_queries.append(dot(grad_scores, keys))
        span = slice(head * HEAD_DIM, (head + 1) * HEAD_DIM)
        v_acc[span, :] += dot(grads_t[span], raised)
        k_acc[span, :] += dot(queries_t[span], grad_scores)
    rows = pl.ds(pl.multiple_of(step * block, block), block)
    mine = jnp.where(here, grad_queries[0], grad_queries[1]) * (HEAD_DIM**-0.5)
    out_ref[rows, 0:PAIR] = mine.astype(BF16)

    @pl.when(step == last)
    def _():
        out_ref[:, PAIR : 2 * PAIR] = k_acc[...].astype(BF16).T
        out_ref[:, 2 * PAIR : 3 * PAIR] = v_acc[...].astype(BF16).T
        sum_ref[...] = jnp.sum(out_ref[...].astype(F32), axis=0, keepdims=True)


def attend_back(where, qkv, grad_mixed, mixed, shares, raised, other, slots, kept=(), block=512):
    seq = qkv.shape[0]
    pairs = qkv.shape[1] // (3 * PAIR) // 2

    begin, end = slots

    def pair(p, w):
        return side(w, other) * pairs + begin + p

    def there(p, w):
        return spot(begin + p, side(w, other), pairs)

    return call(
        attend_back_kernel,
        "attend_back",
        (end - begin, seq // block),
        [
            pl.BlockSpec((block, PAIR), lambda p, b, w: (b, 3 * there(p, w))),
            pl.BlockSpec((seq, PAIR), lambda p, b, w: (0, 3 * there(p, w) + 1)),
            pl.BlockSpec((seq, PAIR), lambda p, b, w: (0, 3 * there(p, w) + 2)),
            pl.BlockSpec((block, PAIR), lambda p, b, w: (b, pair(p, w))),
            pl.BlockSpec((block, PAIR), lambda p, b, w: (b, pair(p, w))),
            pl.BlockSpec((block, PAIR), lambda p, b, w: (b, pair(p, w))),
            pl.BlockSpec((2, block, seq), lambda p, b, w: (pair(p, w), b, 0)),
        ]
        + [WHOLE] * len(kept),
        [
            pl.BlockSpec((seq, 3 * PAIR), lambda p, b, w: (0, begin + p)),
            pl.BlockSpec((1, 3 * PAIR), lambda p, b, w: (0, begin + p)),
        ],
        [shape((seq, 3 * PAIR * pairs), BF16), shape((1, 3 * PAIR * pairs), F32)],
        [pltpu.VMEM((PAIR, seq), F32)] * 2,
        prefetch=1,
        aliases={8 + i: i for i in range(len(kept))},
    )(where, qkv, qkv, qkv, grad_mixed, mixed, shares, raised, *kept)


def input_kernel(
    where, other_ref, mine_ref, x_ref, gres_ref, vec_ref, w_other, w_mine,
    two_ref, pre_ref, down_ref, sum_other, sum_mine, out_ref, sums_ref,
):
    width = x_ref.shape[1]

    @pl.when(pl.program_id(0) == 0)
    def _():
        sums_ref[...] = jnp.zeros_like(sums_ref)
        sums_ref[OUT_B : OUT_B + 1, :] = two_ref[2:3, :]
        sums_ref[GAIN_TWO : SHIFT_TWO + 1, :] = two_ref[0:2, :]
        sums_ref[DOWN_B : DOWN_B + 1, :] = down_ref[...]
        half = sum_mine.shape[1]
        for core in range(2):
            pick = jnp.where(where[2] == core, sum_mine[...], sum_other[...])
            for slot in range(half // (3 * PAIR)):
                column = (core * (half // (3 * PAIR)) + slot) * PAIR
                for row, kind in ((QUERY_B, 0), (VALUE_B, 2)):
                    begin = (3 * slot + kind) * PAIR
                    sums_ref[row : row + 1, column : column + PAIR] = pick[:, begin : begin + PAIR]
        for row in range(pre_ref.shape[1] // width):
            sums_ref[UP_B + row : UP_B + row + 1, :] = pre_ref[:, row * width : (row + 1) * width]

    grad_in = dot_nt(other_ref[...], w_other[...]) + dot_nt(mine_ref[...], w_mine[...])
    normed, inverse = moments(x_ref[...].astype(F32))
    gain = vec_ref[GAIN_ONE : GAIN_ONE + 1, :]
    out_ref[...] = (gres_ref[...] + norm_back(grad_in, normed, inverse, gain)).astype(BF16)
    sums_ref[GAIN_ONE : GAIN_ONE + 1, :] += jnp.sum(grad_in * normed, axis=0, keepdims=True)
    sums_ref[SHIFT_ONE : SHIFT_ONE + 1, :] += jnp.sum(grad_in, axis=0, keepdims=True)


def input_back(where, other, mine, inputs, grad_res, vectors, full, sums, block=256):
    seq, width = inputs.shape
    wide = other.shape[1]
    row = lambda n: pl.BlockSpec((block, n), lambda i, w: (i, 0))
    fixed = lambda a, b: pl.BlockSpec((a, b), lambda i, w: (0, 0))
    return call(
        input_kernel,
        "input_back",
        (seq // block,),
        [
            row(wide),
            row(wide),
            row(width),
            row(width),
            fixed(*vectors.shape),
            pl.BlockSpec((width, wide), lambda i, w: (0, 1 - w[2])),
            pl.BlockSpec((width, wide), lambda i, w: (0, w[2])),
        ]
        + [fixed(*part.shape) for part in sums],
        [row(width), fixed(SUM_ROWS, width)],
        [shape((seq, width), BF16), shape((SUM_ROWS, width), F32)],
        prefetch=1,
    )(where, other, mine, inputs, grad_res, vectors, full, full, *sums)


def outer_call(kernel, name, where, grid, in_specs, out_specs, out_shape, scratch, arrays):
    return call(kernel, name, grid, in_specs, out_specs, out_shape, scratch, 1)(where, *arrays)


def theirs_kernel(where, left_ref, grad_ref, out_ref):
    out_ref[...] = dot(left_ref[...], grad_ref[...]).astype(BF16)


def part_rows(where, total, outs, shards, column=0):
    rows = total.shape[0] // shards // 4
    span = slice(column, column + total.shape[1])
    for turn, out in enumerate(outs):
        for z in range(shards):
            begin = (z * 4 + (where[1] ^ turn)) * rows
            out[z, :, span] = total[aligned(begin, rows, 16), :].astype(BF16)


def mine_kernel(shards, where, left_ref, grad_ref, got_ref, *rest):
    outs, total = rest[:4], rest[4]
    total[...] = dot(left_ref[...], grad_ref[...]) + got_ref[...].astype(F32)
    part_rows(where, total, outs, shards)


def side(w, other):
    return (1 - w[2]) if other else w[2]


def rows_outer(where, left, grad, count, got=None):
    (deep, seq), width = left.shape, grad.shape[1]
    block = deep // count // 2
    specs = [
        pl.BlockSpec((block, seq), lambda i, w: (2 * i + side(w, got is None), 0)),
        pl.BlockSpec((seq, width), lambda i, w: (0, 0)),
    ]
    kept = pl.BlockSpec((block, width), lambda i, w: (i, 0))
    if got is None:
        return outer_call(
            theirs_kernel, "rows_theirs", where, (count,), specs, kept,
            shape((deep // 2, width), BF16), (), (left, grad),
        )
    out = pl.BlockSpec((1, block // 4, width), lambda i, w: (i, 0, 0))
    return outer_call(
        partial(mine_kernel, 1), "rows_mine", where, (count,), specs + [kept], [out] * 4,
        [shape((count, block // 4, width), BF16)] * 4,
        [pltpu.VMEM((block, width), F32)], (left, grad, got),
    )


def columns_outer(where, left, grad, count, tiles, got=None, halves=True):
    (deep, seq), wide = left.shape, grad.shape[1]
    half = wide // 2 if halves else wide
    tile = half // tiles
    other = got is None
    specs = [
        pl.BlockSpec((deep, seq), lambda i, w: (0, 0)),
        pl.BlockSpec((seq, tile), lambda i, w: (0, (side(w, other) * tiles if halves else 0) + i)),
    ]
    kept = pl.BlockSpec((deep, tile), lambda i, w: (0, i))
    if other:
        return outer_call(
            theirs_kernel, "columns_theirs", where, (tiles,), specs, kept,
            shape((deep, half), BF16), (), (left, grad),
        )
    rows = deep // count // 4
    out = pl.BlockSpec((count, rows, tile), lambda i, w: (0, 0, i))
    return outer_call(
        partial(mine_kernel, count), "columns_mine", where, (tiles,), specs + [kept], [out] * 4,
        [shape((count, rows, half), BF16)] * 4,
        [pltpu.VMEM((deep, tile), F32)], (left, grad, got),
    )


def two_mine_kernel(shards, where, a_left, a_grad, b_left, b_grad, a_got, b_got, *rest):
    outs, a_total, b_total = rest[:4], rest[4], rest[5]
    step, half, tile = pl.program_id(0), a_grad.shape[1], b_grad.shape[1]

    @pl.when(step == 0)
    def _():
        a_total[...] = dot(a_left[...], a_grad[...]) + a_got[...].astype(F32)
        part_rows(where, a_total, outs, shards)

    for number in range((outs[0].shape[2] - half) // tile):

        @pl.when(step == number + 1)
        def _(begin=half + number * tile):
            b_total[...] = dot(b_left[...], b_grad[...]) + b_got[...].astype(F32)
            part_rows(where, b_total, outs, shards, begin)


def two_mine(where, a_left, a_grad, b_left, b_grad, count, a_got, b_got, tile=768):
    (deep, seq) = a_left.shape
    a_half, b_half = a_grad.shape[1] // 2, b_grad.shape[1] // 2
    tiles = b_half // tile
    late = lambda i: jnp.maximum(i - 1, 0)
    fixed = lambda *dims: pl.BlockSpec(dims, lambda i, w: (0,) * len(dims))
    rows = deep // count // 4
    return outer_call(
        partial(two_mine_kernel, count),
        "two_mine",
        where,
        (1 + tiles,),
        [
            fixed(deep, seq),
            pl.BlockSpec((seq, a_half), lambda i, w: (0, w[2])),
            fixed(deep, seq),
            pl.BlockSpec((seq, tile), lambda i, w: (0, w[2] * tiles + late(i))),
            fixed(deep, a_half),
            pl.BlockSpec((deep, tile), lambda i, w: (0, late(i))),
        ],
        [fixed(count, rows, a_half + b_half)] * 4,
        [shape((count, rows, a_half + b_half), BF16)] * 4,
        [pltpu.VMEM((deep, a_half), F32), pltpu.VMEM((deep, tile), F32)],
        (a_left, a_grad, b_left, b_grad, a_got, b_got),
    )


def total_of(refs, z):
    total = refs[0][z].astype(F32)
    for ref in refs[1:]:
        total = total + ref[z].astype(F32)
    return total.astype(BF16)


def quad_kernel(count, where, *refs):
    for step in range(count):
        refs[4 + step][...] = total_of(refs[:4], where[0] ^ step)


def quad_sum(where, parts, count):
    full = parts[0].shape
    return call(
        partial(quad_kernel, count),
        "quad_sum",
        (1,),
        [SCALARS] + [pl.BlockSpec(full, lambda i: (0, 0, 0))] * 4,
        [pl.BlockSpec(full[1:], lambda i: (0, 0))] * count,
        [shape(full[1:], BF16)] * count,
    )(where, *parts)


def quad_pairs_kernel(half, where, *refs):
    near, far = refs[4:]
    for step in range(half):
        near[step] = total_of(refs[:4], where[0] ^ step)
        far[step] = total_of(refs[:4], where[0] ^ step ^ half)


def quad_pairs(where, parts, count):
    full = parts[0].shape
    half = count // 2
    return call(
        partial(quad_pairs_kernel, half),
        "quad_pairs",
        (1,),
        [SCALARS] + [pl.BlockSpec(full, lambda i: (0, 0, 0))] * 4,
        [pl.BlockSpec((half, *full[1:]), lambda i: (0, 0, 0))] * 2,
        [shape((half, *full[1:]), BF16)] * 2,
    )(where, *parts)


def halve_kernel(a, b, mine, other):
    total = (a[...].astype(F32) + b[...].astype(F32)).astype(BF16)
    mine[...] = total[0]
    other[...] = total[1]


def halve(near, got):
    full = near.shape
    spec = pl.BlockSpec(full, lambda i: (0, 0, 0))
    return call(
        halve_kernel,
        "halve",
        (1,),
        [spec] * 2,
        [pl.BlockSpec(full[1:], lambda i: (0, 0))] * 2,
        [shape(full[1:], BF16)] * 2,
    )(near, got)


def blocks_of(rows, wide, width):
    return [
        (rows * number, begin, min(width, wide - begin))
        for number, begin in enumerate(range(0, wide, width))
    ]


def merge_kernel(down, down_got, two, two_got, out):
    deep, width = down.shape
    rows, wide = two.shape
    out[0:deep, :] = (down[...].astype(F32) + down_got[...].astype(F32)).astype(BF16)
    total = (two[...].astype(F32) + two_got[...].astype(F32)).astype(BF16)
    for row, begin, size in blocks_of(rows, wide, width):
        row += deep
        out[row : row + rows, 0:size] = total[:, begin : begin + size]
        if size < width:
            out[row : row + rows, size:width] = jnp.zeros((rows, width - size), BF16)


def merge(down, down_got, two, two_got):
    deep, width = down.shape
    rows, wide = two.shape
    tall = deep + rows * len(blocks_of(rows, wide, width))
    whole = lambda part: pl.BlockSpec(part.shape, lambda i: (0, 0))
    return call(
        merge_kernel,
        "merge",
        (1,),
        [whole(part) for part in (down, down_got, two, two_got)],
        pl.BlockSpec((tall, width), lambda i: (0, 0)),
        shape((tall, width), BF16),
    )(down, down_got, two, two_got)


def add_kernel(*refs):
    total = refs[0][...].astype(F32)
    for ref in refs[1:-1]:
        total = total + ref[...].astype(F32)
    refs[-1][...] = total.astype(refs[-1].dtype)


def add_all(parts):
    full = parts[0].shape
    spec = pl.BlockSpec(full, lambda i: (0,) * len(full))
    return call(
        add_kernel, "add_all", (1,), [spec] * len(parts), spec, shape(full, parts[0].dtype)
    )(*parts)


def halves_of(where, pieces, turn):
    low = where[2] == 0
    near, far = pieces[turn][...].astype(F32), pieces[4 + turn][...].astype(F32)
    return jnp.where(low, near, far), jnp.where(low, far, near)


def lay_merged_kernel(where, *refs):
    pieces, (down, out, up) = refs[:8], refs[8:]
    width, half = down.shape[1], out.shape[1] // 2
    deep = down.shape[0] // 8
    rows, wide = up.shape[0] // 4, half + up.shape[1] // 2
    for turn in range(4):
        quad = where[1] ^ turn
        for core, value in enumerate(halves_of(where, pieces, turn)):
            down[aligned((4 * core + quad) * deep, deep, 16), :] = value[0:deep]
            for row, begin, size in blocks_of(rows, wide, width):
                part = value[deep + row : deep + row + rows, 0:size]
                place = aligned(quad * rows, rows, 16)
                if begin < half:
                    out[place, core * half : (core + 1) * half] = part[:, 0:half]
                    part, begin = part[:, half:], half
                column = core * (wide - half) + begin - half
                up[place, column : column + part.shape[1]] = part


def lay_pairs_kernel(where, *refs):
    pieces, outs = refs[:8], refs[8:]
    rows, half = pieces[0].shape
    for turn in range(4):
        place = aligned((where[1] ^ turn) * rows, rows, 16)
        for core, value in enumerate(halves_of(where, pieces, turn)):
            for slot in range(half // (3 * PAIR)):
                begin = (core * (half // (3 * PAIR)) + slot) * PAIR
                for kind, out in enumerate(outs):
                    column = (3 * slot + kind) * PAIR
                    out[place, begin : begin + PAIR] = value[:, column : column + PAIR]


def lay(kernel, name, where, pieces, outs):
    spec = pl.BlockSpec(pieces[0].shape, lambda i: (0, 0))
    return call(
        kernel,
        name,
        (1,),
        [SCALARS] + [spec] * 8,
        [pl.BlockSpec(dims, lambda i: (0, 0)) for dims in outs],
        [shape(dims, F32) for dims in outs],
    )(where, *pieces)


def tally_kernel(where, lengths, places, ids_ref, out_ref):
    ids = ids_ref[...]
    seq = ids.shape[1]
    live = lax.broadcasted_iota(jnp.int32, (1, seq), 1) < lengths[places[where[3]]]
    high, low = ids // 128, jnp.where(live, ids % 128, -1)
    tall = (lax.broadcasted_iota(jnp.int32, (TALLY_ROWS, seq), 0) == high).astype(F32).astype(BF16)
    wide = (lax.broadcasted_iota(jnp.int32, (128, seq), 0) == low).astype(F32).astype(BF16)
    out_ref[...] = dot_nt(tall, wide).astype(jnp.int32)


def tally(cell, ids):
    return call(
        tally_kernel,
        "tally",
        (1,),
        [SCALARS] * 3 + [pl.BlockSpec(ids.shape, lambda i: (0, 0))],
        pl.BlockSpec((TALLY_ROWS, 128), lambda i: (0, 0)),
        shape((TALLY_ROWS, 128), jnp.int32),
    )(*cell, ids)


def body(
    dp_size,
    fsdp_size,
    cells_in,
    out_grad,
    cell_length,
    cell_place,
    gene_ids,
    attn_norm_gain,
    attn_norm_bias,
    query_weight,
    query_bias,
    key_weight,
    value_weight,
    value_bias,
    out_weight,
    out_bias,
    ffn_norm_gain,
    ffn_norm_bias,
    up_weight,
    up_bias,
    down_weight,
    down_bias,
):
    count = fsdp_size
    seq, width = cells_in.shape[1:]
    place = lax.axis_index("dp")
    z = lax.axis_index("fsdp")
    core, quad = place & 1, (place >> 1) & 3
    where = jnp.stack([z, quad, core, place * fsdp_size + z]).astype(jnp.int32)
    cell = (where, cell_length.astype(jnp.int32), cell_place.astype(jnp.int32))

    def swap(value, mask):
        return lax.ppermute(value, "dp", [(i, i ^ mask) for i in range(dp_size)])

    def turn(value, step):
        return lax.ppermute(value, "fsdp", [(i, i ^ step) for i in range(count)])

    def from_quad(value):
        return [swap(value, 2 * mask) for mask in (1, 2, 3)]

    def to_quad(parts):
        return [swap(parts[mask], 2 * mask) for mask in (1, 2, 3)]

    def from_column(value):
        return [turn(value, step) for step in range(1, count)]

    def to_column(parts):
        return [turn(parts[step], step) for step in range(1, count)]

    def to_core(parts, beside=None):
        first = lambda: ([swap(part, 1) for part in parts[:2]], beside() if beside else ())
        got, result = during(first)
        got = got + during(lambda: [swap(part, 1) for part in parts[2:]])
        return (got, result) if beside else got

    def halfway(near, far):
        return turn(far, count // 2)

    def beyond(total):
        mask = 8
        while mask < dp_size:
            total = add_all([total, swap(total, mask)])
            mask *= 2
        return total

    inputs = cells_in.reshape(seq, width)
    grads = out_grad.reshape(seq, width)
    live = cell_length[0] > 0

    def during(run):
        outs = jax.eval_shape(run)
        blank = lambda: jax.tree.map(lambda out: jnp.zeros(out.shape, out.dtype), outs)
        return lax.cond(live, run, blank)

    shard = attn_norm_gain.shape[0]
    small = [
        attn_norm_gain,
        attn_norm_bias,
        out_bias,
        ffn_norm_gain,
        ffn_norm_bias,
        down_bias,
        query_bias,
        value_bias,
        up_bias,
    ]
    own = (query_weight, key_weight, value_weight)
    pairs = width // PAIR
    deep = down_weight.shape[0] // 8
    first, second = pack(where, *own, out_weight, up_weight, down_weight, small)

    rows, wide = first.shape[0] - SUM_ROWS, first.shape[1]
    group = 3 * PAIR
    tall = second.shape[0]

    far, side_rest, counts = during(
        lambda: (from_column(first), turn(second, 1), tally(cell, gene_ids))
    )
    early, later = split(far, [(0, 0, rows, group), (0, group, rows, wide - group)])
    small = [first] + far

    def stage():
        near, norm = during(
            lambda: (
                from_quad(early),
                first_norm(where, inputs, small, shard, count * up_bias.shape[0]),
            )
        )
        near = [early] + near
        pieces = near + to_core(near)

        def inner():
            kept = project_qkv(where, norm[0], norm[4], own, pieces, count, 0)
            return from_quad(later), kept, attend(cell, kept[0], (0, 1), (0, pairs // 2))

        return norm, during(inner)

    rest, ((attn_in, attn_in_t, vectors, up_b, bias), (far, kept, mixed)) = during(
        lambda: ([turn(second, 2), turn(side_rest, 2)], during(stage))
    )
    later = [later] + far
    third, second = split(
        [side_rest] + rest, [(0, 0, deep, width), (deep, 0, tall - deep, width)]
    )

    def stage():
        pieces = later + to_core(later)
        out = project_qkv(where, attn_in, bias, own, pieces, count, 1, kept)
        return out, attend(cell, out[0], (2, 3), (1, 2), mixed)

    far, ((qkv, qkv_full), mixed) = during(lambda: (from_quad(second), during(stage)))
    second = [second] + far
    far, (other, (mixed, mixed_t, raised, shares)) = during(
        lambda: (
            from_quad(third),
            to_core(
                second,
                lambda: attend(cell, qkv, (4, 5), (pairs // 2 + 1, pairs // 2 + 2), mixed),
            ),
        )
    )
    second, third = second + other, [third] + far
    other, (residual, ffn_in_t, hidden, hidden_t, slope, out_full, up_full) = to_core(
        third,
        lambda: feed_up(
            where, inputs, mixed, vectors, up_b, out_weight, up_weight, second, count
        ),
    )
    third = third + other
    down_theirs = rows_outer(where, hidden_t, grads, count)

    def stage():
        got = swap(down_theirs, 1)
        down = feed_down(
            where, residual, hidden, slope, grads, vectors, down_weight, third, count
        )
        return got, down, columns_outer(where, ffn_in_t, down[1], count, 2)

    down_got, (block_out, grad_pre, pre_sum, grad_sum), up_theirs = during(stage)
    down_parts = rows_outer(where, hidden_t, grads, count, down_got)

    def stage():
        up_got = swap(up_theirs, 1)
        back = residual_back(grad_pre, residual, grads, vectors, up_full, out_full)
        out_got = swap(columns_outer(where, mixed_t, back[1], count, 1), 1)
        return back, two_mine(
            where, mixed_t, back[1], ffn_in_t, grad_pre, count, out_got, up_got
        )

    got, ((grad_res, branch, grad_mixed, two_sums), two_parts) = during(
        lambda: (to_quad(down_parts), during(stage))
    )
    down_near, down_far = quad_pairs(where, [down_parts[0]] + got, count)
    last = pairs // 2

    def stage():
        def inner():
            back, sums = attend_back(
                where, qkv, grad_mixed, mixed, shares, raised, True, (0, last)
            )
            return back, sums, columns_outer(where, attn_in_t, back, count, 1, halves=False)

        other, sums, theirs = during(inner)
        got, far, kept = during(
            lambda: (
                swap(theirs, 1),
                turn(down_far, 2),
                attend_back(
                    where, qkv, grad_mixed, mixed, shares, raised, False, (0, last - 1)
                ),
            )
        )
        return other, sums, got, far, kept

    got, (grads_other, sums_other, qkv_got, far, kept) = during(
        lambda: (to_quad(two_parts), during(stage))
    )
    two_near, two_far = quad_pairs(where, [two_parts[0]] + got, count)
    down_piece, down_next = halve(down_near, far)

    def stage():
        grads_mine, sums_mine = attend_back(
            where, qkv, grad_mixed, mixed, shares, raised, False, (last - 1, last), kept
        )
        parts = columns_outer(where, attn_in_t, grads_mine, count, 1, qkv_got, halves=False)
        return turn(two_far, 2), turn(down_next, 1), swap(counts, 1), grads_mine, sums_mine, parts

    far, down_got, tally_got, grads_mine, sums_mine, qkv_parts = during(stage)
    counts = counts + tally_got
    two_piece, two_next = halve(two_near, far)

    def stage():
        two_got, tally_got, (back, sums) = during(
            lambda: (
                turn(two_next, 1),
                swap(counts, 2),
                input_back(
                    where, grads_other, grads_mine, inputs, grad_res, vectors, qkv_full,
                    (two_sums, pre_sum, grad_sum, sums_other, sums_mine),
                ),
            )
        )
        merged = beyond(merge(down_piece, down_got, two_piece, two_got))
        total = counts + tally_got
        more, tally_got = during(lambda: (swap(sums, 1), swap(total, 4)))
        return merged, back, add_all([sums, more]), total + tally_got

    got, (merged, input_grad, sums, counts) = during(
        lambda: (to_quad(qkv_parts), during(stage))
    )
    qkv_parts = quad_sum(where, [qkv_parts[0]] + got, count)
    got, far, more, tally_got = during(
        lambda: (
            to_column(qkv_parts),
            from_quad(merged),
            swap(sums, 2),
            turn(counts, 1),
        )
    )
    counts = counts + tally_got
    qkv_piece = beyond(add_all([qkv_parts[0]] + got))
    merged, sums = [merged] + far, add_all([sums, more])

    def stage():
        pieces = merged + to_core(merged)
        return lay(
            lay_merged_kernel, "lay_merged", where, pieces,
            [down_weight.shape, out_weight.shape, up_weight.shape],
        )

    far, more, (grad_down, grad_out, grad_up) = during(
        lambda: (from_quad(qkv_piece), swap(sums, 4), during(stage))
    )
    qkv_pieces, sums = [qkv_piece] + far, sums + more
    mask = 8
    while mask < dp_size:
        sums, counts = sums + swap(sums, mask), counts + swap(counts, mask)
        mask *= 2

    def stage():
        pieces = qkv_pieces + to_core(qkv_pieces)
        return lay(lay_pairs_kernel, "lay_qkv", where, pieces, [query_weight.shape] * 3)

    more, tally_got, (grad_query, grad_key, grad_value) = during(
        lambda: (from_column(sums), turn(counts, 2), during(stage))
    )
    sums = sums + sum(more)
    counts = counts + tally_got
    pieces = lax.dynamic_slice(sums, (0, z * shard), (8, shard))
    vec = [pieces[i] for i in range(8)]
    size = up_bias.shape[0]
    grad_up_b = lax.dynamic_slice(sums[UP_B:].reshape(-1), (z * size,), (size,))

    gene_counts = counts.reshape(-1)[:VOCAB]

    return (
        block_out.reshape(cells_in.shape),
        input_grad.reshape(cells_in.shape),
        vec[0],
        vec[1],
        grad_query,
        vec[6],
        grad_key,
        grad_value,
        vec[7],
        grad_out,
        vec[2],
        vec[3],
        vec[4],
        grad_up,
        grad_up_b,
        grad_down,
        vec[5],
        gene_counts,
    )


def solution(mesh):
    cells = P(("dp", "fsdp"), None, None)
    vector = P("fsdp")
    matrix = P("fsdp", None)
    in_specs = (
        cells,
        cells,
        P(),
        P(),
        P(("dp", "fsdp"), None),
        vector,
        vector,
        matrix,
        vector,
        matrix,
        matrix,
        vector,
        matrix,
        vector,
        vector,
        vector,
        matrix,
        vector,
        matrix,
        vector,
    )
    out_specs = (
        cells,
        cells,
        vector,
        vector,
        matrix,
        vector,
        matrix,
        matrix,
        vector,
        matrix,
        vector,
        vector,
        vector,
        matrix,
        vector,
        matrix,
        vector,
        P(),
    )
    return jax.shard_map(
        partial(body, mesh.shape["dp"], mesh.shape["fsdp"]),
        mesh=mesh,
        in_specs=in_specs,
        out_specs=out_specs,
        check_vma=False,
    )
```

```python
from functools import partial

import jax
import jax.numpy as jnp
from jax import lax
from jax.experimental import pallas as pl
from jax.experimental.pallas import tpu as pltpu
from jax.sharding import PartitionSpec as P

HEADS = 12
HEAD_DIM = 64
VOCAB = 36000
EPSILON = 1e-05
NEGATIVE = -1e30
PAIR = 2 * HEAD_DIM
CHUNK = 1536
TALLY_ROWS = 288

F32 = jnp.float32
BF16 = jnp.bfloat16
VMEM_LIMIT = 60 << 20

GAIN_ONE, SHIFT_ONE, OUT_B, GAIN_TWO, SHIFT_TWO, DOWN_B, QUERY_B, VALUE_B, UP_B = range(9)
SUM_ROWS = 16

WHOLE = pl.BlockSpec(memory_space=pl.ANY)
SCALARS = pl.BlockSpec(memory_space=pltpu.SMEM)


LIGHT = pl.CostEstimate(flops=1024, transcendentals=0, bytes_accessed=1024)


def call(kernel, name, grid, in_specs, out_specs, out_shape, scratch=(), prefetch=0, aliases=None):
    return pl.pallas_call(
        kernel,
        grid_spec=pltpu.PrefetchScalarGridSpec(
            num_scalar_prefetch=prefetch,
            grid=grid,
            in_specs=in_specs,
            out_specs=out_specs,
            scratch_shapes=scratch,
        ),
        out_shape=out_shape,
        input_output_aliases=aliases or {},
        compiler_params=pltpu.CompilerParams(vmem_limit_bytes=VMEM_LIMIT),
        cost_estimate=LIGHT,
        name=name,
    )


def shape(dims, dtype):
    return jax.ShapeDtypeStruct(dims, dtype)


def dot(left, right):
    return jnp.dot(left, right, preferred_element_type=F32)


def dot_nt(left, right):
    return lax.dot_general(left, right, (((1,), (1,)), ((), ())), preferred_element_type=F32)


def dot_tn(left, right):
    return lax.dot_general(left, right, (((0,), (0,)), ((), ())), preferred_element_type=F32)


def moments(values):
    width = values.shape[-1]
    center = values - jnp.sum(values, axis=-1, keepdims=True) * (1.0 / width)
    spread = jnp.sum(center * center, axis=-1, keepdims=True) * (1.0 / width)
    inverse = lax.rsqrt(spread + EPSILON)
    return center * inverse, inverse


def norm_back(grad_out, normed, inverse, gain):
    width = normed.shape[-1]
    scaled = grad_out * gain
    mean = jnp.sum(scaled, axis=-1, keepdims=True) * (1.0 / width)
    along = jnp.sum(scaled * normed, axis=-1, keepdims=True) * (1.0 / width)
    return inverse * (scaled - mean - normed * along)


def start_all(copies):
    for copy in copies:
        copy.start()


def wait_all(copies):
    for copy in copies:
        copy.wait()


def aligned(begin, size, unit):
    return pl.ds(pl.multiple_of(begin, unit), size)


def pack_kernel(slots, where, *refs):
    pairs, (o, up, down), small, (first, second, third) = (
        refs[: 3 * slots], refs[3 * slots : 3 * slots + 3], refs[3 * slots + 3 : -3], refs[-3:],
    )
    rows, half = o.shape
    width = down.shape[1]
    for number, ref in enumerate(pairs):
        first[0:rows, number * PAIR : (number + 1) * PAIR] = ref[...]
    first[rows:, :] = jnp.zeros((first.shape[0] - rows, first.shape[1]), BF16)
    for number, ref in enumerate(small):
        value = ref[...].astype(F32).reshape(1, -1).astype(BF16)
        first[rows + number : rows + number + 1, 0 : ref.shape[0]] = value
    third[...] = down[...]
    row = 0
    for begin in range(0, up.shape[1], width):
        second[row : row + rows, :] = up[:, begin : begin + width]
        row += rows
    second[row : row + rows, 0:half] = o[...]
    second[row : row + rows, half:width] = jnp.zeros((rows, width - half), BF16)


def pack(where, q, k, v, o, up, down, small):
    rows, width = q.shape[0] // 4, q.shape[1]
    slots = width // PAIR // 2
    deep = down.shape[0] // 8
    first = (rows + SUM_ROWS, 3 * PAIR * slots)
    second = (rows * (up.shape[1] // 2 // width + 1), width)
    third = (deep, width)
    return call(
        partial(pack_kernel, slots),
        "pack",
        (1,),
        [
            pl.BlockSpec((rows, PAIR), lambda i, w, s=slot: (w[1], slots * w[2] + s))
            for slot in range(slots)
            for _ in range(3)
        ]
        + [
            pl.BlockSpec((rows, o.shape[1] // 2), lambda i, w: (w[1], w[2])),
            pl.BlockSpec((rows, up.shape[1] // 2), lambda i, w: (w[1], w[2])),
            pl.BlockSpec((deep, width), lambda i, w: (4 * w[2] + w[1], 0)),
        ]
        + [pl.BlockSpec(part.shape, lambda i, w: (0,)) for part in small],
        [pl.BlockSpec(part, lambda i, w: (0, 0)) for part in (first, second, third)],
        [shape(part, BF16) for part in (first, second, third)],
        prefetch=1,
    )(where, *([q, k, v] * slots), o, up, down, *small)


def split_kernel(parts, *refs):
    ins, outs = refs[: -len(parts)], refs[-len(parts) :]
    for (row, column), out in zip(parts, outs):
        rows, columns = out.shape[1:]
        for number, ref in enumerate(ins):
            out[number] = ref[row : row + rows, column : column + columns]


def split(arrays, parts):
    full = arrays[0].shape
    return call(
        partial(split_kernel, [part[:2] for part in parts]),
        "split",
        (1,),
        [pl.BlockSpec(full, lambda i: (0, 0))] * len(arrays),
        [pl.BlockSpec((len(arrays), *part[2:]), lambda i: (0, 0, 0)) for part in parts],
        [shape((len(arrays), *part[2:]), BF16) for part in parts],
    )(*arrays)


def remote_places(where, pieces, count):
    z, quad, core = where[0], where[1], where[2]
    for number, piece in enumerate(pieces):
        turn, side = number % 4, number // 4
        for step in range(1, count):
            yield piece, step - 1, z ^ step, quad ^ turn, core ^ side


def pair_copies(where, own, pieces, full, sems, count, slot):
    shard = own[0].shape[0]
    slots = own[0].shape[1] // PAIR // 2
    rows, half = pieces[0].shape[1:]
    copies = []
    for kind, ref in enumerate(own):
        for core in range(2):
            for number in range(half // (3 * PAIR)):
                source = (core * slots + slot + number) * PAIR
                target = core * half + (3 * number + kind) * PAIR
                copies.append(
                    pltpu.make_async_copy(
                        ref.at[:, source : source + PAIR],
                        full.at[aligned(where[0] * shard, shard, 16), target : target + PAIR],
                        sems.at[len(copies)],
                    )
                )
    for piece, step, z, quad, core in remote_places(where, pieces, count):
        copies.append(
            pltpu.make_async_copy(
                piece.at[step],
                full.at[aligned(z * shard + quad * rows, rows, 16), aligned(core * half, half, 128)],
                sems.at[len(copies)],
            )
        )
    return copies


def column_copies(where, own, pieces, full, sems, count, row):
    shard = own.shape[0]
    rows, half = shard // 4, own.shape[1] // 2
    width = pieces[0].shape[2]
    copies = [pltpu.make_async_copy(own, full.at[aligned(where[0] * shard, shard, 16)], sems.at[0])]
    for piece, step, z, quad, core in remote_places(where, pieces, count):
        for number, begin in enumerate(range(0, half, width)):
            size = min(width, half - begin)
            copies.append(
                pltpu.make_async_copy(
                    piece.at[step, row + number * rows : row + (number + 1) * rows, 0:size],
                    full.at[
                        aligned(z * shard + quad * rows, rows, 16),
                        aligned(core * half + begin, size, 128),
                    ],
                    sems.at[len(copies)],
                )
            )
    return copies


def row_copies(where, own, pieces, full, sems, count):
    shard = own.shape[0]
    rows = pieces[0].shape[1]
    copies = [
        pltpu.make_async_copy(own, full.at[aligned(where[0] * shard, shard, 16)], sems.at[0])
    ]
    for piece, step, z, quad, core in remote_places(where, pieces, count):
        copies.append(
            pltpu.make_async_copy(
                piece.at[step],
                full.at[aligned(z * shard + core * 4 * rows + quad * rows, rows, 16)],
                sems.at[len(copies)],
            )
        )
    return copies


def copy_count(count):
    return 1 + 8 * (count - 1)


def norm_kernel(count, shard, where, x_ref, *rest):
    small, (a_ref, t_ref, vec_ref, up_ref, bias_ref) = rest[:count], rest[count:]

    @pl.when(pl.program_id(0) == 0)
    def _():
        wide = up_ref.shape[1] // count
        for owner in range(count):
            value = small[0][...].astype(F32)
            for step in range(1, count):
                here = (where[0] ^ step) == owner
                value = jnp.where(here, small[step][...].astype(F32), value)
            vec_ref[:, owner * shard : (owner + 1) * shard] = value[0:8, 0:shard]
            up_ref[:, owner * wide : (owner + 1) * wide] = value[UP_B : UP_B + 1, 0:wide]
        slots = vec_ref.shape[1] // PAIR // 2
        for core in range(2):
            for slot in range(slots):
                span = slice((core * slots + slot) * PAIR, (core * slots + slot + 1) * PAIR)
                begin = 3 * PAIR * spot(slot, core, slots)
                bias_ref[:, begin : begin + PAIR] = vec_ref[QUERY_B : QUERY_B + 1, span]
                bias_ref[:, begin + PAIR : begin + 2 * PAIR] = jnp.zeros((1, PAIR), F32)
                bias_ref[:, begin + 2 * PAIR : begin + 3 * PAIR] = vec_ref[
                    VALUE_B : VALUE_B + 1, span
                ]

    normed, _ = moments(x_ref[...].astype(F32))
    rows = normed * vec_ref[GAIN_ONE : GAIN_ONE + 1, :] + vec_ref[SHIFT_ONE : SHIFT_ONE + 1, :]
    rows = rows.astype(BF16)
    a_ref[...] = rows
    t_ref[...] = rows.T


def spot(slot, core, slots):
    return jnp.where(slot == 0, core, 1 + core * (slots - 1) + slot) if not isinstance(
        slot, int
    ) else (core if slot == 0 else 1 + core * (slots - 1) + slot)


def first_norm(where, inputs, small, shard, wide, block=256):
    seq, width = inputs.shape
    count = len(small)
    fixed = lambda a, b: pl.BlockSpec((a, b), lambda i: (0, 0))
    last = small[0].shape[0] // SUM_ROWS - 1
    return call(
        partial(norm_kernel, count, shard),
        "first_norm",
        (seq // block,),
        [SCALARS, pl.BlockSpec((block, width), lambda i: (i, 0))]
        + [pl.BlockSpec((SUM_ROWS, part.shape[1]), lambda i: (last, 0)) for part in small],
        [
            pl.BlockSpec((block, width), lambda i: (i, 0)),
            pl.BlockSpec((width, block), lambda i: (0, i)),
            fixed(8, width),
            fixed(1, wide),
            fixed(1, 3 * width),
        ],
        [
            shape((seq, width), BF16),
            shape((width, seq), BF16),
            shape((8, width), F32),
            shape((1, wide), F32),
            shape((1, 3 * width), F32),
        ],
    )(where, inputs, *small)


def qkv_kernel(count, slot, slots, where, a_ref, bias_ref, q, k, v, *rest):
    pieces = rest[:8]
    out_ref, kept_ref, full, sems, out_sems = rest[-5:]
    step, part = pl.program_id(0), pl.program_id(1)
    half = pieces[0].shape[2]

    def keep():
        return [
            pltpu.make_async_copy(
                full.at[:, core * half : (core + 1) * half],
                kept_ref.at[
                    :, (core * slots + slot) * 3 * PAIR : (core * slots + slot) * 3 * PAIR + half
                ],
                out_sems.at[core],
            )
            for core in range(2)
        ]

    @pl.when((step == 0) & (part == 0))
    def _():
        copies = pair_copies(where, (q, k, v), pieces, full, sems, count, slot)
        start_all(copies)
        wait_all(copies)
        start_all(keep())

    wide = out_ref.shape[1]
    column = pl.multiple_of(part * wide, wide)
    rows = (dot(a_ref[...], full[:, pl.ds(column, wide)]) + bias_ref[...]).astype(BF16)
    for begin in range(0, wide, PAIR):
        value = rows[:, begin : begin + PAIR]
        if begin // PAIR % 3 == 0:
            value = value * jnp.asarray(HEAD_DIM**-0.5, BF16)
        out_ref[:, begin : begin + PAIR] = value

    @pl.when((step == pl.num_programs(0) - 1) & (part == pl.num_programs(1) - 1))
    def _():
        wait_all(keep())


def project_qkv(where, attn_in, bias, own, pieces, count, slot, kept=(), block=512):
    seq, width = attn_in.shape
    slots = own[0].shape[1] // PAIR // 2
    half = pieces[0].shape[2]
    wide, parts = (2 * half, 1) if slot == 0 else (half, 2)
    first = 0 if slot == 0 else 1
    copies = copy_count(count) - 1 + 2 * half // PAIR
    return call(
        partial(qkv_kernel, count, slot, slots),
        "project_qkv",
        (seq // block, parts),
        [
            SCALARS,
            pl.BlockSpec((block, width), lambda i, n: (i, 0)),
            pl.BlockSpec((1, wide), lambda i, n: (0, first + n)),
        ]
        + [WHOLE] * (11 + len(kept)),
        [pl.BlockSpec((block, wide), lambda i, n: (i, first + n)), WHOLE],
        [shape((seq, 3 * width), BF16), shape((width, 3 * width), BF16)],
        [
            pltpu.VMEM((width, 2 * half), BF16),
            pltpu.SemaphoreType.DMA((copies,)),
            pltpu.SemaphoreType.DMA((2,)),
        ],
        aliases={14 + i: i for i in range(len(kept))},
    )(where, attn_in, bias, *own, *pieces, *kept)


def attend_kernel(where, lengths, places, q_ref, k_ref, v_ref, *rest):
    o_ref, e_ref, r_ref = rest[-3:]
    seq, block = k_ref.shape[0], q_ref.shape[0]
    first = lax.broadcasted_iota(jnp.int32, (seq, PAIR), 1) < HEAD_DIM
    here = lax.broadcasted_iota(jnp.int32, (block, PAIR), 1) < HEAD_DIM
    place = lax.broadcasted_iota(jnp.int32, (1, seq), 1)
    bias = jnp.where(place < lengths[places[where[3]]], 0.0, NEGATIVE).astype(F32)
    queries, keys, values = q_ref[...], k_ref[...], v_ref[...]
    zeros = jnp.zeros_like(keys)
    blended, shares = [], []
    for head in range(2):
        head_keys = jnp.where(first, keys, zeros) if head == 0 else jnp.where(first, zeros, keys)
        scores = dot_nt(queries, head_keys) + bias
        raised = jnp.exp(scores - jnp.max(scores, axis=1, keepdims=True))
        shares.append(1.0 / jnp.sum(raised, axis=1, keepdims=True))
        raised = raised.astype(BF16)
        e_ref[head] = raised
        blended.append(dot(raised, values))
    share = jnp.where(here, shares[0], shares[1])
    r_ref[...] = share
    mixed = (jnp.where(here, blended[0], blended[1]) * share).astype(BF16)
    o_ref[...] = mixed


def attend(cell, qkv, spots, pairs, kept=(), block=512):
    seq, wide = qkv.shape
    total = wide // (3 * PAIR)
    there = lambda p: spots[0] + (spots[1] - spots[0]) * p
    here = lambda p: pairs[0] + (pairs[1] - pairs[0]) * p
    return call(
        attend_kernel,
        "attend",
        (2, seq // block),
        [
            SCALARS,
            SCALARS,
            SCALARS,
            pl.BlockSpec((block, PAIR), lambda p, b: (b, 3 * there(p))),
            pl.BlockSpec((seq, PAIR), lambda p, b: (0, 3 * there(p) + 1)),
            pl.BlockSpec((seq, PAIR), lambda p, b: (0, 3 * there(p) + 2)),
        ]
        + [WHOLE] * len(kept),
        [
            pl.BlockSpec((block, PAIR), lambda p, b: (b, here(p))),
            pl.BlockSpec((2, block, seq), lambda p, b: (here(p), b, 0)),
            pl.BlockSpec((block, PAIR), lambda p, b: (b, here(p))),
        ],
        [
            shape((seq, total * PAIR), BF16),
            shape((2 * total, seq, seq), BF16),
            shape((seq, total * PAIR), F32),
        ],
        aliases={6 + i: i for i in range(len(kept))},
    )(*cell, qkv, qkv, qkv, *kept)


ERF_P = 0.3275911 * 2.0**-0.5
ERF_A = (0.254829592, -0.284496736, 1.421413741, -1.453152027, 1.061405429)


def gelu_parts(values):
    bell = jnp.exp(values * values * -0.5)
    ratio = 1.0 / (1.0 + ERF_P * jnp.abs(values))
    tail = 0.5 * ERF_A[4]
    for term in ERF_A[3::-1]:
        tail = tail * ratio + 0.5 * term
    tail = tail * ratio * bell
    under = jnp.where(values > 0, 1.0 - tail, tail)
    return values * under, under + values * bell * 0.3989422804014327


def feed_kernel(
    count, where, x_ref, mix_ref, grad_ref, vec_ref, bias_ref, out_own, up_own, down_own, *rest
):
    second, third = rest[:8], rest[8:16]
    out_ref, gres_ref, gmix_ref, presum_ref, sums_ref = rest[16:21]
    halves = rest[21:27]
    w_out, w_up, w_down, t_out, t_up, t_down, sem_a, sem_b, sem_c, sem_out = rest[27:]
    step = pl.program_id(0)
    rows = up_own.shape[0] // 4
    blocks = up_own.shape[1] // 2 // second[0].shape[2]
    out_copies = column_copies(where, out_own, second, w_out, sem_a, count, blocks * rows)
    up_copies = column_copies(where, up_own, second, w_up, sem_b, count, 0)
    down_copies = row_copies(where, down_own, third, w_down, sem_c, count)

    @pl.when(step == 0)
    def _():
        start_all(out_copies)
        start_all(up_copies)
        start_all(down_copies)
        for ref in (t_out, t_up, t_down, presum_ref, sums_ref):
            ref[...] = jnp.zeros_like(ref)
        wait_all(out_copies)

    mix = mix_ref[...]
    grads = grad_ref[...]
    mixed = x_ref[...].astype(F32) + vec_ref[OUT_B : OUT_B + 1, :] + dot(mix, w_out[...])
    normed, inverse = moments(mixed)
    gain = vec_ref[GAIN_TWO : GAIN_TWO + 1, :]
    rows = (normed * gain + vec_ref[SHIFT_TWO : SHIFT_TWO + 1, :]).astype(BF16)

    @pl.when(step == 0)
    def _():
        wait_all(up_copies)
        wait_all(down_copies)

    def chunk(number, sums):
        result, grad_in = sums
        span = aligned(number * CHUNK, CHUNK, CHUNK)
        value, slope = gelu_parts(dot(rows, w_up[:, span]) + bias_ref[:, span])
        value = value.astype(BF16)
        result = result + dot(value, w_down[span, :])
        t_down[span, :] += dot_tn(value, grads)
        pre = (dot_nt(grads, w_down[span, :]) * slope).astype(BF16)
        presum_ref[:, span] += jnp.sum(pre.astype(F32), axis=0, keepdims=True)
        t_up[:, span] += dot_tn(rows, pre)
        return result, grad_in + dot_nt(pre, w_up[:, span])

    result, grad_in = lax.fori_loop(
        0,
        w_up.shape[1] // CHUNK,
        chunk,
        (mixed + vec_ref[DOWN_B : DOWN_B + 1, :], jnp.zeros(mixed.shape, F32)),
    )
    out_ref[...] = result.astype(BF16)
    grads = grads.astype(F32)
    grad_res = grads + norm_back(grad_in, normed, inverse, gain)
    gres_ref[...] = grad_res
    branch = grad_res.astype(BF16)
    gmix_ref[...] = dot_nt(branch, w_out[...]).astype(BF16)
    t_out[...] += dot_tn(mix, branch)
    sums_ref[0:1, :] += jnp.sum(grad_in * normed, axis=0, keepdims=True)
    sums_ref[1:2, :] += jnp.sum(grad_in, axis=0, keepdims=True)
    sums_ref[2:3, :] += jnp.sum(branch.astype(F32), axis=0, keepdims=True)
    sums_ref[3:4, :] += jnp.sum(grads, axis=0, keepdims=True)

    @pl.when(step == pl.num_programs(0) - 1)
    def _():
        copies = []
        half = w_down.shape[0] // 2
        part = half // count
        for place, core in enumerate((1 - where[2], where[2])):
            for z in range(count):
                begin = place * half + z * part
                source = aligned((2 * z + core) * part, part, 16)
                w_down[begin : begin + part, :] = t_down[source, :].astype(BF16)
            copies.append(
                pltpu.make_async_copy(
                    w_down.at[place * half : (place + 1) * half], halves[place], sem_out.at[place]
                )
            )
        start_all(copies)
        for number, (weight, total) in enumerate(((w_up, t_up), (w_out, t_out))):
            half = weight.shape[1] // 2
            for place, core in enumerate((1 - where[2], where[2])):
                span = slice(place * half, (place + 1) * half)
                weight[:, span] = total[:, aligned(core * half, half, 128)].astype(BF16)
                slot = 2 * number + 2 + place
                copies.append(
                    pltpu.make_async_copy(weight.at[:, span], halves[slot], sem_out.at[slot])
                )
                copies[-1].start()
        wait_all(copies)


def feed(
    where, inputs, mixed, grads, vectors, bias, out_own, up_own, down_own, second, third, count,
    block=256,
):
    seq, width = inputs.shape
    wide = up_own.shape[1]
    row = lambda n: pl.BlockSpec((block, n), lambda i: (i, 0))
    fixed = lambda a, b: pl.BlockSpec((a, b), lambda i: (0, 0))
    return call(
        partial(feed_kernel, count),
        "feed",
        (seq // block,),
        [SCALARS, row(width), row(width), row(width), fixed(*vectors.shape), fixed(1, wide)]
        + [WHOLE] * 19,
        [row(width), row(width), row(width), fixed(1, wide), fixed(8, width)] + [WHOLE] * 6,
        [
            shape((seq, width), BF16),
            shape((seq, width), F32),
            shape((seq, width), BF16),
            shape((1, wide), F32),
            shape((8, width), F32),
        ]
        + [shape((wide // 2, width), BF16)] * 2
        + [shape((width, wide // 2), BF16)] * 2
        + [shape((width, width // 2), BF16)] * 2,
        [
            pltpu.VMEM((width, width), BF16),
            pltpu.VMEM((width, wide), BF16),
            pltpu.VMEM((wide, width), BF16),
            pltpu.VMEM((width, width), F32),
            pltpu.VMEM((width, wide), F32),
            pltpu.VMEM((wide, width), F32),
        ]
        + [pltpu.SemaphoreType.DMA((2 * copy_count(count),))] * 3
        + [pltpu.SemaphoreType.DMA((6,))],
    )(where, inputs, mixed, grads, vectors, bias, out_own, up_own, down_own, *second, *third)


def attend_back_kernel(
    where, q_ref, k_ref, v_ref, do_ref, o_ref, r_ref, e_ref, in_ref, *rest
):
    out_ref, sum_ref, w_ref, k_acc, v_acc = rest[-5:]
    seq, block = k_ref.shape[0], q_ref.shape[0]
    step, last = pl.program_id(1), pl.num_programs(1) - 1
    first = lax.broadcasted_iota(jnp.int32, (seq, PAIR), 1) < HEAD_DIM
    here = lax.broadcasted_iota(jnp.int32, (block, PAIR), 1) < HEAD_DIM
    keys, values, queries = k_ref[...], v_ref[...], q_ref[...]
    zeros = jnp.zeros_like(values)

    @pl.when(step == 0)
    def _():
        k_acc[...] = jnp.zeros_like(k_acc)
        v_acc[...] = jnp.zeros_like(v_acc)

    grads = (do_ref[...].astype(F32) * r_ref[...]).astype(BF16)
    product = grads.astype(F32) * o_ref[...].astype(F32)
    whole = jnp.sum(product, axis=1, keepdims=True)
    part = jnp.sum(jnp.where(here, product, 0.0), axis=1, keepdims=True)
    inner = (part, whole - part)
    grads_t, queries_t = grads.T, queries.T
    grad_queries = []
    for head in range(2):
        head_values = (
            jnp.where(first, values, zeros) if head == 0 else jnp.where(first, zeros, values)
        )
        raised = e_ref[head]
        grad_shares = dot_nt(grads, head_values)
        grad_scores = (raised.astype(F32) * (grad_shares - inner[head])).astype(BF16)
        grad_queries.append(dot(grad_scores, keys))
        span = slice(head * HEAD_DIM, (head + 1) * HEAD_DIM)
        v_acc[span, :] += dot(grads_t[span], raised)
        k_acc[span, :] += dot(queries_t[span], grad_scores)
    rows = pl.ds(pl.multiple_of(step * block, block), block)
    mine = jnp.where(here, grad_queries[0], grad_queries[1]) * (HEAD_DIM**-0.5)
    out_ref[rows, 0:PAIR] = mine.astype(BF16)

    @pl.when(step == last)
    def _():
        out_ref[:, PAIR : 2 * PAIR] = k_acc[...].astype(BF16).T
        out_ref[:, 2 * PAIR : 3 * PAIR] = v_acc[...].astype(BF16).T
        sum_ref[...] = jnp.sum(out_ref[...].astype(F32), axis=0, keepdims=True)
        w_ref[...] = dot(in_ref[...], out_ref[...]).astype(BF16)


def attend_back(
    where, qkv, grad_mixed, mixed, shares, raised, in_t, other, block=512
):
    seq = qkv.shape[0]
    pairs = qkv.shape[1] // (3 * PAIR) // 2

    def pair(p, w):
        return side(w, other) * pairs + p

    def there(p, w):
        return spot(p, side(w, other), pairs)

    return call(
        attend_back_kernel,
        "attend_back",
        (pairs, seq // block),
        [
            pl.BlockSpec((block, PAIR), lambda p, b, w: (b, 3 * there(p, w))),
            pl.BlockSpec((seq, PAIR), lambda p, b, w: (0, 3 * there(p, w) + 1)),
            pl.BlockSpec((seq, PAIR), lambda p, b, w: (0, 3 * there(p, w) + 2)),
            pl.BlockSpec((block, PAIR), lambda p, b, w: (b, pair(p, w))),
            pl.BlockSpec((block, PAIR), lambda p, b, w: (b, pair(p, w))),
            pl.BlockSpec((block, PAIR), lambda p, b, w: (b, pair(p, w))),
            pl.BlockSpec((2, block, seq), lambda p, b, w: (pair(p, w), b, 0)),
            pl.BlockSpec(in_t.shape, lambda p, b, w: (0, 0), pipeline_mode=pl.Buffered(1)),
        ],
        [
            pl.BlockSpec((seq, 3 * PAIR), lambda p, b, w: (0, p)),
            pl.BlockSpec((1, 3 * PAIR), lambda p, b, w: (0, p)),
            pl.BlockSpec((in_t.shape[0], 3 * PAIR), lambda p, b, w: (0, p)),
        ],
        [shape((seq, 3 * PAIR * pairs), BF16), shape((1, 3 * PAIR * pairs), F32), shape((in_t.shape[0], 3 * PAIR * pairs), BF16)],
        [pltpu.VMEM((PAIR, seq), F32)] * 2,
        prefetch=1,
    )(where, qkv, qkv, qkv, grad_mixed, mixed, shares, raised, in_t)


def input_kernel(
    where, other_ref, mine_ref, x_ref, gres_ref, vec_ref, w_other, w_mine,
    two_ref, pre_ref, sum_other, sum_mine, out_ref, sums_ref,
):
    width = x_ref.shape[1]

    @pl.when(pl.program_id(0) == 0)
    def _():
        sums_ref[...] = jnp.zeros_like(sums_ref)
        sums_ref[OUT_B : OUT_B + 1, :] = two_ref[2:3, :]
        sums_ref[GAIN_TWO : SHIFT_TWO + 1, :] = two_ref[0:2, :]
        sums_ref[DOWN_B : DOWN_B + 1, :] = two_ref[3:4, :]
        half = sum_mine.shape[1]
        for core in range(2):
            pick = jnp.where(where[2] == core, sum_mine[...], sum_other[...])
            for slot in range(half // (3 * PAIR)):
                column = (core * (half // (3 * PAIR)) + slot) * PAIR
                for row, kind in ((QUERY_B, 0), (VALUE_B, 2)):
                    begin = (3 * slot + kind) * PAIR
                    sums_ref[row : row + 1, column : column + PAIR] = pick[:, begin : begin + PAIR]
        for row in range(pre_ref.shape[1] // width):
            sums_ref[UP_B + row : UP_B + row + 1, :] = pre_ref[:, row * width : (row + 1) * width]

    grad_in = dot_nt(other_ref[...], w_other[...]) + dot_nt(mine_ref[...], w_mine[...])
    normed, inverse = moments(x_ref[...].astype(F32))
    gain = vec_ref[GAIN_ONE : GAIN_ONE + 1, :]
    out_ref[...] = (gres_ref[...] + norm_back(grad_in, normed, inverse, gain)).astype(BF16)
    sums_ref[GAIN_ONE : GAIN_ONE + 1, :] += jnp.sum(grad_in * normed, axis=0, keepdims=True)
    sums_ref[SHIFT_ONE : SHIFT_ONE + 1, :] += jnp.sum(grad_in, axis=0, keepdims=True)


def input_back(where, other, mine, inputs, grad_res, vectors, full, sums, block=256):
    seq, width = inputs.shape
    wide = other.shape[1]
    row = lambda n: pl.BlockSpec((block, n), lambda i, w: (i, 0))
    fixed = lambda a, b: pl.BlockSpec((a, b), lambda i, w: (0, 0))
    return call(
        input_kernel,
        "input_back",
        (seq // block,),
        [
            row(wide),
            row(wide),
            row(width),
            row(width),
            fixed(*vectors.shape),
            pl.BlockSpec((width, wide), lambda i, w: (0, 1 - w[2])),
            pl.BlockSpec((width, wide), lambda i, w: (0, w[2])),
        ]
        + [fixed(*part.shape) for part in sums],
        [row(width), fixed(SUM_ROWS, width)],
        [shape((seq, width), BF16), shape((SUM_ROWS, width), F32)],
        prefetch=1,
    )(where, other, mine, inputs, grad_res, vectors, full, full, *sums)


def outer_call(kernel, name, where, grid, in_specs, out_specs, out_shape, scratch, arrays):
    return call(kernel, name, grid, in_specs, out_specs, out_shape, scratch, 1)(where, *arrays)


def part_rows(where, total, outs, shards, column=0):
    rows = total.shape[0] // shards // 4
    span = slice(column, column + total.shape[1])
    for turn, out in enumerate(outs):
        for z in range(shards):
            begin = (z * 4 + (where[1] ^ turn)) * rows
            out[z, :, span] = total[aligned(begin, rows, 16), :].astype(BF16)


def side(w, other):
    return (1 - w[2]) if other else w[2]


def add_parts_kernel(shards, where, *refs):
    inputs, outs, total = refs[:-5], refs[-5:-1], refs[-1]
    begin = 0
    for mine, got in zip(inputs[0::2], inputs[1::2]):
        span = slice(begin, begin + mine.shape[1])
        total[:, span] = mine[...].astype(F32) + got[...].astype(F32)
        begin += mine.shape[1]
    part_rows(where, total, outs, shards)


def add_parts(where, pairs, count, steps=2):
    deep = pairs[0][0].shape[0]
    wide = sum(mine.shape[1] for mine, _ in pairs)
    rows = deep // count // 4
    arrays = [part for pair in pairs for part in pair]
    return outer_call(
        partial(add_parts_kernel, count // steps),
        "add_parts",
        where,
        (steps,),
        [pl.BlockSpec((deep // steps, part.shape[1]), lambda i, w: (i, 0)) for part in arrays],
        [pl.BlockSpec((count // steps, rows, wide), lambda i, w: (i, 0, 0))] * 4,
        [shape((count, rows, wide), BF16)] * 4,
        [pltpu.VMEM((deep // steps, wide), F32)],
        arrays,
    )


def total_of(refs, z):
    total = refs[0][z].astype(F32)
    for ref in refs[1:]:
        total = total + ref[z].astype(F32)
    return total.astype(BF16)


def quad_kernel(count, where, *refs):
    for step in range(count):
        refs[4 + step][...] = total_of(refs[:4], where[0] ^ step)


def quad_sum(where, parts, count):
    full = parts[0].shape
    return call(
        partial(quad_kernel, count),
        "quad_sum",
        (1,),
        [SCALARS] + [pl.BlockSpec(full, lambda i: (0, 0, 0))] * 4,
        [pl.BlockSpec(full[1:], lambda i: (0, 0))] * count,
        [shape(full[1:], BF16)] * count,
    )(where, *parts)


def quad_pairs_kernel(half, where, *refs):
    near, far = refs[4:]
    for step in range(half):
        near[step] = total_of(refs[:4], where[0] ^ step)
        far[step] = total_of(refs[:4], where[0] ^ step ^ half)


def quad_pairs(where, parts, count):
    full = parts[0].shape
    half = count // 2
    return call(
        partial(quad_pairs_kernel, half),
        "quad_pairs",
        (1,),
        [SCALARS] + [pl.BlockSpec(full, lambda i: (0, 0, 0))] * 4,
        [pl.BlockSpec((half, *full[1:]), lambda i: (0, 0, 0))] * 2,
        [shape((half, *full[1:]), BF16)] * 2,
    )(where, *parts)


def halve_kernel(a, b, mine, other):
    total = (a[...].astype(F32) + b[...].astype(F32)).astype(BF16)
    mine[...] = total[0]
    other[...] = total[1]


def halve(near, got):
    full = near.shape
    spec = pl.BlockSpec(full, lambda i: (0, 0, 0))
    return call(
        halve_kernel,
        "halve",
        (1,),
        [spec] * 2,
        [pl.BlockSpec(full[1:], lambda i: (0, 0))] * 2,
        [shape(full[1:], BF16)] * 2,
    )(near, got)


def blocks_of(rows, wide, width):
    return [
        (rows * number, begin, min(width, wide - begin))
        for number, begin in enumerate(range(0, wide, width))
    ]


def merge_kernel(down, down_got, two, two_got, out):
    deep, width = down.shape
    rows, wide = two.shape
    out[0:deep, :] = (down[...].astype(F32) + down_got[...].astype(F32)).astype(BF16)
    total = (two[...].astype(F32) + two_got[...].astype(F32)).astype(BF16)
    for row, begin, size in blocks_of(rows, wide, width):
        row += deep
        out[row : row + rows, 0:size] = total[:, begin : begin + size]
        if size < width:
            out[row : row + rows, size:width] = jnp.zeros((rows, width - size), BF16)


def merge(down, down_got, two, two_got):
    deep, width = down.shape
    rows, wide = two.shape
    tall = deep + rows * len(blocks_of(rows, wide, width))
    whole = lambda part: pl.BlockSpec(part.shape, lambda i: (0, 0))
    return call(
        merge_kernel,
        "merge",
        (1,),
        [whole(part) for part in (down, down_got, two, two_got)],
        pl.BlockSpec((tall, width), lambda i: (0, 0)),
        shape((tall, width), BF16),
    )(down, down_got, two, two_got)


def add_kernel(*refs):
    total = refs[0][...].astype(F32)
    for ref in refs[1:-1]:
        total = total + ref[...].astype(F32)
    refs[-1][...] = total.astype(refs[-1].dtype)


def add_all(parts):
    full = parts[0].shape
    spec = pl.BlockSpec(full, lambda i: (0,) * len(full))
    return call(
        add_kernel, "add_all", (1,), [spec] * len(parts), spec, shape(full, parts[0].dtype)
    )(*parts)


def halves_of(where, pieces, turn):
    low = where[2] == 0
    near, far = pieces[turn][...].astype(F32), pieces[4 + turn][...].astype(F32)
    return jnp.where(low, near, far), jnp.where(low, far, near)


def lay_merged_kernel(where, *refs):
    pieces, (down, out, up) = refs[:8], refs[8:]
    width, half = down.shape[1], out.shape[1] // 2
    deep = down.shape[0] // 8
    rows, wide = up.shape[0] // 4, half + up.shape[1] // 2
    for turn in range(4):
        quad = where[1] ^ turn
        for core, value in enumerate(halves_of(where, pieces, turn)):
            down[aligned((4 * core + quad) * deep, deep, 16), :] = value[0:deep]
            for row, begin, size in blocks_of(rows, wide, width):
                part = value[deep + row : deep + row + rows, 0:size]
                place = aligned(quad * rows, rows, 16)
                if begin < half:
                    out[place, core * half : (core + 1) * half] = part[:, 0:half]
                    part, begin = part[:, half:], half
                column = core * (wide - half) + begin - half
                up[place, column : column + part.shape[1]] = part


def lay_pairs_kernel(where, *refs):
    pieces, outs = refs[:8], refs[8:]
    rows, half = pieces[0].shape
    for turn in range(4):
        place = aligned((where[1] ^ turn) * rows, rows, 16)
        for core, value in enumerate(halves_of(where, pieces, turn)):
            for slot in range(half // (3 * PAIR)):
                begin = (core * (half // (3 * PAIR)) + slot) * PAIR
                for kind, out in enumerate(outs):
                    column = (3 * slot + kind) * PAIR
                    out[place, begin : begin + PAIR] = value[:, column : column + PAIR]


def lay(kernel, name, where, pieces, outs):
    spec = pl.BlockSpec(pieces[0].shape, lambda i: (0, 0))
    return call(
        kernel,
        name,
        (1,),
        [SCALARS] + [spec] * 8,
        [pl.BlockSpec(dims, lambda i: (0, 0)) for dims in outs],
        [shape(dims, F32) for dims in outs],
    )(where, *pieces)


def tally_kernel(where, lengths, places, ids_ref, out_ref):
    ids = ids_ref[...]
    seq = ids.shape[1]
    live = lax.broadcasted_iota(jnp.int32, (1, seq), 1) < lengths[places[where[3]]]
    high, low = ids // 128, jnp.where(live, ids % 128, -1)
    tall = (lax.broadcasted_iota(jnp.int32, (TALLY_ROWS, seq), 0) == high).astype(F32).astype(BF16)
    wide = (lax.broadcasted_iota(jnp.int32, (128, seq), 0) == low).astype(F32).astype(BF16)
    out_ref[...] = dot_nt(tall, wide).astype(jnp.int32)


def tally(cell, ids):
    return call(
        tally_kernel,
        "tally",
        (1,),
        [SCALARS] * 3 + [pl.BlockSpec(ids.shape, lambda i: (0, 0))],
        pl.BlockSpec((TALLY_ROWS, 128), lambda i: (0, 0)),
        shape((TALLY_ROWS, 128), jnp.int32),
    )(*cell, ids)


def body(
    dp_size,
    fsdp_size,
    cells_in,
    out_grad,
    cell_length,
    cell_place,
    gene_ids,
    attn_norm_gain,
    attn_norm_bias,
    query_weight,
    query_bias,
    key_weight,
    value_weight,
    value_bias,
    out_weight,
    out_bias,
    ffn_norm_gain,
    ffn_norm_bias,
    up_weight,
    up_bias,
    down_weight,
    down_bias,
):
    count = fsdp_size
    seq, width = cells_in.shape[1:]
    place = lax.axis_index("dp")
    z = lax.axis_index("fsdp")
    core, quad = place & 1, (place >> 1) & 3
    where = jnp.stack([z, quad, core, place * fsdp_size + z]).astype(jnp.int32)
    cell = (where, cell_length.astype(jnp.int32), cell_place.astype(jnp.int32))

    def swap(value, mask):
        return lax.ppermute(value, "dp", [(i, i ^ mask) for i in range(dp_size)])

    def turn(value, step):
        return lax.ppermute(value, "fsdp", [(i, i ^ step) for i in range(count)])

    def from_quad(value):
        return [swap(value, 2 * mask) for mask in (1, 2, 3)]

    def to_quad(parts):
        return [swap(parts[mask], 2 * mask) for mask in (1, 2, 3)]

    def from_column(value):
        return [turn(value, step) for step in range(1, count)]

    def to_column(parts):
        return [turn(parts[step], step) for step in range(1, count)]

    def to_core(parts, beside=None, at_once=2):
        first = lambda: (
            [swap(part, 1) for part in parts[:at_once]], beside() if beside else ()
        )
        got, result = during(first)
        if at_once < len(parts):
            got = got + during(lambda: [swap(part, 1) for part in parts[at_once:]])
        return (got, result) if beside else got

    def beyond(total):
        mask = 8
        while mask < dp_size:
            total = add_all([total, swap(total, mask)])
            mask *= 2
        return total

    inputs = cells_in.reshape(seq, width)
    grads = out_grad.reshape(seq, width)
    live = cell_length[0] > 0

    def during(run):
        outs = jax.eval_shape(run)
        blank = lambda: jax.tree.map(lambda out: jnp.zeros(out.shape, out.dtype), outs)
        return lax.cond(live, run, blank)

    shard = attn_norm_gain.shape[0]
    small = [
        attn_norm_gain,
        attn_norm_bias,
        out_bias,
        ffn_norm_gain,
        ffn_norm_bias,
        down_bias,
        query_bias,
        value_bias,
        up_bias,
    ]
    own = (query_weight, key_weight, value_weight)
    pairs = width // PAIR
    deep = down_weight.shape[0] // 8
    first, second, third = pack(where, *own, out_weight, up_weight, down_weight, small)

    rows, wide = first.shape[0] - SUM_ROWS, first.shape[1]
    group = 3 * PAIR
    tall = second.shape[0]

    far, counts = during(lambda: (from_column(first), tally(cell, gene_ids)))
    early, later = split(far, [(0, 0, rows, group), (0, group, rows, wide - group)])
    small = [first] + far

    def stage():
        return (
            turn(second, 1),
            turn(third, 1),
            first_norm(where, inputs, small, shard, count * up_bias.shape[0]),
        )

    near, (second_a, third_a, (attn_in, attn_in_t, vectors, up_b, bias)) = during(
        lambda: (from_quad(early), during(stage))
    )
    near = [early] + near
    pieces = near + to_core(near, at_once=4)

    def stage():
        kept = project_qkv(where, attn_in, bias, own, pieces, count, 0)
        return (
            turn(second, 2),
            turn(second_a, 2),
            kept,
            attend(cell, kept[0], (0, 1), (0, pairs // 2)),
        )

    far, (second_b, second_c, kept, mixed) = during(lambda: (from_quad(later), during(stage)))
    later = [later] + far
    (second,) = split([second_a, second_b, second_c], [(0, 0, *second.shape)])

    def stage():
        pieces = later + to_core(later)

        def inner():
            out = project_qkv(where, attn_in, bias, own, pieces, count, 1, kept)
            return turn(third, 2), turn(third_a, 2), out, attend(cell, out[0], (2, 3), (1, 2), mixed)

        return during(inner)

    far, (third_b, third_c, (qkv, qkv_full), mixed) = during(
        lambda: (from_quad(second), during(stage))
    )
    second = [second] + far
    (third,) = split([third_a, third_b, third_c], [(0, 0, *third.shape)])
    last = pairs // 2
    far, (other, (mixed, raised, shares)) = during(
        lambda: (
            from_quad(third),
            to_core(
                second,
                lambda: attend(cell, qkv, (4, 5), (last + 1, last + 2), mixed),
            ),
        )
    )
    second, third = second + other, [third] + far
    third = third + to_core(third, at_once=4)
    block_out, grad_res, grad_mixed, pre_sum, two_sums, *halves = feed(
        where, inputs, mixed, grads, vectors, up_b, out_weight, up_weight, down_weight, second,
        third, count,
    )
    down_theirs, down_mine, up_theirs, up_mine, out_theirs, out_mine = halves
    down_got, tally_got = during(lambda: (swap(down_theirs, 1), swap(counts, 1)))
    counts = counts + tally_got
    down_parts = add_parts(where, [(down_mine, down_got)], count)

    got, (up_got, out_got, (grads_other, sums_other, qkv_theirs)) = during(
        lambda: (
            to_quad(down_parts),
            during(
                lambda: (
                    swap(up_theirs, 1),
                    swap(out_theirs, 1),
                    attend_back(
                        where, qkv, grad_mixed, mixed, shares, raised, attn_in_t, True
                    ),
                )
            ),
        )
    )
    two_parts = add_parts(where, [(out_mine, out_got), (up_mine, up_got)], count)
    down_near, down_far = quad_pairs(where, [down_parts[0]] + got, count)

    def stage():
        got, far, (grads_mine, sums_mine, mine) = during(
            lambda: (
                swap(qkv_theirs, 1),
                turn(down_far, 2),
                attend_back(where, qkv, grad_mixed, mixed, shares, raised, attn_in_t, False),
            )
        )
        parts = add_parts(where, [(mine, got)], count)
        piece, following = halve(down_near, far)
        got, tally_got, (back, sums) = during(
            lambda: (
                turn(following, 1),
                swap(counts, 2),
                input_back(
                    where, grads_other, grads_mine, inputs, grad_res, vectors, qkv_full,
                    (two_sums, pre_sum, sums_other, sums_mine),
                ),
            )
        )
        return parts, piece, got, back, sums, counts + tally_got

    got, (qkv_parts, down_piece, down_got, input_grad, sums, counts) = during(
        lambda: (to_quad(two_parts), during(stage))
    )

    def stage():
        near, far = quad_pairs(where, [two_parts[0]] + got, count)
        far, more = during(lambda: (turn(far, 2), swap(sums, 1)))
        piece, following = halve(near, far)
        total = add_all([sums, more])
        got_too, more = during(lambda: (turn(following, 1), swap(total, 2)))
        merged = beyond(merge(down_piece, down_got, piece, got_too))
        return merged, add_all([total, more])

    got, (merged, sums) = during(lambda: (to_quad(qkv_parts), during(stage)))
    qkv_parts = quad_sum(where, [qkv_parts[0]] + got, count)
    got, (side, other_side) = during(
        lambda: (to_column(qkv_parts), during(lambda: (swap(merged, 2), swap(merged, 4))))
    )
    qkv_piece = beyond(add_all([qkv_parts[0]] + got))
    far, (across, more) = during(
        lambda: (from_quad(qkv_piece), during(lambda: (swap(merged, 6), swap(sums, 4))))
    )
    qkv_pieces, merged = [qkv_piece] + far, [merged, side, other_side, across]
    sums = add_all([sums, more])
    other, tally_got = during(
        lambda: ([swap(part, 1) for part in qkv_pieces], swap(counts, 4))
    )
    counts = counts + tally_got
    mask = 8
    while mask < dp_size:
        sums, counts = sums + swap(sums, mask), counts + swap(counts, mask)
        mask *= 2
    sums_got, (far, (grad_query, grad_key, grad_value)) = during(
        lambda: (
            turn(sums, 1),
            to_core(
                merged,
                lambda: lay(
                    lay_pairs_kernel, "lay_qkv", where, qkv_pieces + other,
                    [query_weight.shape] * 3,
                ),
                4,
            ),
        )
    )
    sums = add_all([sums, sums_got])
    more, tally_got, (grad_down, grad_out, grad_up) = during(
        lambda: (
            turn(sums, 2),
            turn(counts, 1),
            lay(
                lay_merged_kernel, "lay_merged", where, merged + far,
                [down_weight.shape, out_weight.shape, up_weight.shape],
            ),
        )
    )
    sums, counts = add_all([sums, more]), counts + tally_got
    counts = counts + turn(counts, 2)
    pieces = lax.dynamic_slice(sums, (0, z * shard), (8, shard))
    vec = [pieces[i] for i in range(8)]
    size = up_bias.shape[0]
    grad_up_b = lax.dynamic_slice(sums[UP_B:].reshape(-1), (z * size,), (size,))

    gene_counts = counts.reshape(-1)[:VOCAB]

    return (
        block_out.reshape(cells_in.shape),
        input_grad.reshape(cells_in.shape),
        vec[0],
        vec[1],
        grad_query,
        vec[6],
        grad_key,
        grad_value,
        vec[7],
        grad_out,
        vec[2],
        vec[3],
        vec[4],
        grad_up,
        grad_up_b,
        grad_down,
        vec[5],
        gene_counts,
    )


def solution(mesh):
    cells = P(("dp", "fsdp"), None, None)
    vector = P("fsdp")
    matrix = P("fsdp", None)
    in_specs = (
        cells,
        cells,
        P(),
        P(),
        P(("dp", "fsdp"), None),
        vector,
        vector,
        matrix,
        vector,
        matrix,
        matrix,
        vector,
        matrix,
        vector,
        vector,
        vector,
        matrix,
        vector,
        matrix,
        vector,
    )
    out_specs = (
        cells,
        cells,
        vector,
        vector,
        matrix,
        vector,
        matrix,
        matrix,
        vector,
        matrix,
        vector,
        vector,
        vector,
        matrix,
        vector,
        matrix,
        vector,
        P(),
    )
    return jax.shard_map(
        partial(body, mesh.shape["dp"], mesh.shape["fsdp"]),
        mesh=mesh,
        in_specs=in_specs,
        out_specs=out_specs,
        check_vma=False,
    )
```

```python
from functools import partial

import jax
import jax.numpy as jnp
from jax import lax
from jax.experimental import pallas as pl
from jax.experimental.pallas import tpu as pltpu
from jax.sharding import PartitionSpec as P

HEADS = 12
HEAD_DIM = 64
VOCAB = 36000
EPSILON = 1e-05
NEGATIVE = -1e30
PAIR = 2 * HEAD_DIM
CHUNK = 1536
TALLY_ROWS = 288

F32 = jnp.float32
BF16 = jnp.bfloat16
VMEM_LIMIT = 60 << 20

GAIN_ONE, SHIFT_ONE, OUT_B, GAIN_TWO, SHIFT_TWO, DOWN_B, QUERY_B, VALUE_B, UP_B = range(9)
SUM_ROWS = 16

WHOLE = pl.BlockSpec(memory_space=pl.ANY)
SCALARS = pl.BlockSpec(memory_space=pltpu.SMEM)


LIGHT = pl.CostEstimate(flops=1024, transcendentals=0, bytes_accessed=1024)


def call(kernel, name, grid, in_specs, out_specs, out_shape, scratch=(), prefetch=0, aliases=None):
    return pl.pallas_call(
        kernel,
        grid_spec=pltpu.PrefetchScalarGridSpec(
            num_scalar_prefetch=prefetch,
            grid=grid,
            in_specs=in_specs,
            out_specs=out_specs,
            scratch_shapes=scratch,
        ),
        out_shape=out_shape,
        input_output_aliases=aliases or {},
        compiler_params=pltpu.CompilerParams(vmem_limit_bytes=VMEM_LIMIT),
        cost_estimate=LIGHT,
        name=name,
    )


def shape(dims, dtype):
    return jax.ShapeDtypeStruct(dims, dtype)


def dot(left, right):
    return jnp.dot(left, right, preferred_element_type=F32)


def dot_nt(left, right):
    return lax.dot_general(left, right, (((1,), (1,)), ((), ())), preferred_element_type=F32)


def dot_tn(left, right):
    return lax.dot_general(left, right, (((0,), (0,)), ((), ())), preferred_element_type=F32)


def moments(values):
    width = values.shape[-1]
    center = values - jnp.sum(values, axis=-1, keepdims=True) * (1.0 / width)
    spread = jnp.sum(center * center, axis=-1, keepdims=True) * (1.0 / width)
    inverse = lax.rsqrt(spread + EPSILON)
    return center * inverse, inverse


def norm_back(grad_out, normed, inverse, gain):
    width = normed.shape[-1]
    scaled = grad_out * gain
    mean = jnp.sum(scaled, axis=-1, keepdims=True) * (1.0 / width)
    along = jnp.sum(scaled * normed, axis=-1, keepdims=True) * (1.0 / width)
    return inverse * (scaled - mean - normed * along)


def start_all(copies):
    for copy in copies:
        copy.start()


def wait_all(copies):
    for copy in copies:
        copy.wait()


def aligned(begin, size, unit):
    return pl.ds(pl.multiple_of(begin, unit), size)


def pack_kernel(slots, where, *refs):
    pairs, (o, up, down), small, (first, rest) = (
        refs[: 3 * slots], refs[3 * slots : 3 * slots + 3], refs[3 * slots + 3 : -2], refs[-2:],
    )
    rows, half = o.shape
    width = down.shape[1]
    for number, ref in enumerate(pairs):
        first[0:rows, number * PAIR : (number + 1) * PAIR] = ref[...]
    first[rows:, :] = jnp.zeros((first.shape[0] - rows, first.shape[1]), BF16)
    for number, ref in enumerate(small):
        value = ref[...].astype(F32).reshape(1, -1).astype(BF16)
        first[rows + number : rows + number + 1, 0 : ref.shape[0]] = value
    row = 0
    for begin in range(0, up.shape[1], width):
        rest[row : row + rows, :] = up[:, begin : begin + width]
        row += rows
    rest[row : row + rows, 0:half] = o[...]
    rest[row : row + rows, half:width] = jnp.zeros((rows, width - half), BF16)
    rest[row + rows :, :] = down[...]


def pack(where, q, k, v, o, up, down, small):
    rows, width = q.shape[0] // 4, q.shape[1]
    slots = width // PAIR // 2
    deep = down.shape[0] // 8
    first = (rows + SUM_ROWS, 3 * PAIR * slots)
    rest = (rows * (up.shape[1] // 2 // width + 1) + deep, width)
    return call(
        partial(pack_kernel, slots),
        "pack",
        (1,),
        [
            pl.BlockSpec((rows, PAIR), lambda i, w, s=slot: (w[1], slots * w[2] + s))
            for slot in range(slots)
            for _ in range(3)
        ]
        + [
            pl.BlockSpec((rows, o.shape[1] // 2), lambda i, w: (w[1], w[2])),
            pl.BlockSpec((rows, up.shape[1] // 2), lambda i, w: (w[1], w[2])),
            pl.BlockSpec((deep, width), lambda i, w: (4 * w[2] + w[1], 0)),
        ]
        + [pl.BlockSpec(part.shape, lambda i, w: (0,)) for part in small],
        [pl.BlockSpec(part, lambda i, w: (0, 0)) for part in (first, rest)],
        [shape(part, BF16) for part in (first, rest)],
        prefetch=1,
    )(where, *([q, k, v] * slots), o, up, down, *small)


def split_kernel(parts, *refs):
    ins, outs = refs[: -len(parts)], refs[-len(parts) :]
    for (row, column), out in zip(parts, outs):
        rows, columns = out.shape[1:]
        for number, ref in enumerate(ins):
            out[number] = ref[row : row + rows, column : column + columns]


def split(arrays, parts):
    full = arrays[0].shape
    return call(
        partial(split_kernel, [part[:2] for part in parts]),
        "split",
        (1,),
        [pl.BlockSpec(full, lambda i: (0, 0))] * len(arrays),
        [pl.BlockSpec((len(arrays), *part[2:]), lambda i: (0, 0, 0)) for part in parts],
        [shape((len(arrays), *part[2:]), BF16) for part in parts],
    )(*arrays)


def sort_kernel(where, gathered, *outs):
    begin = 0
    for out in outs:
        rows = out.shape[1]
        for number in range(out.shape[0]):
            out[number] = gathered[where[0] ^ (number + 1), begin : begin + rows, :]
        begin += rows


def sort(where, gathered, sizes):
    count, _, width = gathered.shape
    return call(
        sort_kernel,
        "sort",
        (1,),
        [SCALARS, pl.BlockSpec(gathered.shape, lambda i: (0, 0, 0))],
        [pl.BlockSpec((count - 1, size, width), lambda i: (0, 0, 0)) for size in sizes],
        [shape((count - 1, size, width), BF16) for size in sizes],
    )(where, gathered)


def remote_places(where, pieces, count):
    z, quad, core = where[0], where[1], where[2]
    for number, piece in enumerate(pieces):
        turn, side = number % 4, number // 4
        for step in range(1, count):
            yield piece, step - 1, z ^ step, quad ^ turn, core ^ side


def pair_copies(where, own, pieces, full, sems, count, slot):
    shard = own[0].shape[0]
    slots = own[0].shape[1] // PAIR // 2
    rows, half = pieces[0].shape[1:]
    copies = []
    for kind, ref in enumerate(own):
        for core in range(2):
            for number in range(half // (3 * PAIR)):
                source = (core * slots + slot + number) * PAIR
                target = core * half + (3 * number + kind) * PAIR
                copies.append(
                    pltpu.make_async_copy(
                        ref.at[:, source : source + PAIR],
                        full.at[aligned(where[0] * shard, shard, 16), target : target + PAIR],
                        sems.at[len(copies)],
                    )
                )
    for piece, step, z, quad, core in remote_places(where, pieces, count):
        copies.append(
            pltpu.make_async_copy(
                piece.at[step],
                full.at[aligned(z * shard + quad * rows, rows, 16), aligned(core * half, half, 128)],
                sems.at[len(copies)],
            )
        )
    return copies


def column_copies(where, own, pieces, full, sems, count, row):
    shard = own.shape[0]
    rows, half = shard // 4, own.shape[1] // 2
    width = pieces[0].shape[2]
    copies = [pltpu.make_async_copy(own, full.at[aligned(where[0] * shard, shard, 16)], sems.at[0])]
    for piece, step, z, quad, core in remote_places(where, pieces, count):
        for number, begin in enumerate(range(0, half, width)):
            size = min(width, half - begin)
            copies.append(
                pltpu.make_async_copy(
                    piece.at[step, row + number * rows : row + (number + 1) * rows, 0:size],
                    full.at[
                        aligned(z * shard + quad * rows, rows, 16),
                        aligned(core * half + begin, size, 128),
                    ],
                    sems.at[len(copies)],
                )
            )
    return copies


def row_copies(where, own, pieces, full, sems, count):
    shard = own.shape[0]
    rows = pieces[0].shape[1]
    copies = [
        pltpu.make_async_copy(own, full.at[aligned(where[0] * shard, shard, 16)], sems.at[0])
    ]
    for piece, step, z, quad, core in remote_places(where, pieces, count):
        copies.append(
            pltpu.make_async_copy(
                piece.at[step],
                full.at[aligned(z * shard + core * 4 * rows + quad * rows, rows, 16)],
                sems.at[len(copies)],
            )
        )
    return copies


def copy_count(count):
    return 1 + 8 * (count - 1)


def norm_kernel(count, shard, where, x_ref, *rest):
    small, (a_ref, t_ref, vec_ref, up_ref, bias_ref) = rest[:count], rest[count:]

    @pl.when(pl.program_id(0) == 0)
    def _():
        wide = up_ref.shape[1] // count
        for owner in range(count):
            value = small[0][...].astype(F32)
            for step in range(1, count):
                here = (where[0] ^ step) == owner
                value = jnp.where(here, small[step][...].astype(F32), value)
            vec_ref[:, owner * shard : (owner + 1) * shard] = value[0:8, 0:shard]
            up_ref[:, owner * wide : (owner + 1) * wide] = value[UP_B : UP_B + 1, 0:wide]
        slots = vec_ref.shape[1] // PAIR // 2
        for core in range(2):
            for slot in range(slots):
                span = slice((core * slots + slot) * PAIR, (core * slots + slot + 1) * PAIR)
                begin = 3 * PAIR * spot(slot, core, slots)
                bias_ref[:, begin : begin + PAIR] = vec_ref[QUERY_B : QUERY_B + 1, span]
                bias_ref[:, begin + PAIR : begin + 2 * PAIR] = jnp.zeros((1, PAIR), F32)
                bias_ref[:, begin + 2 * PAIR : begin + 3 * PAIR] = vec_ref[
                    VALUE_B : VALUE_B + 1, span
                ]

    normed, _ = moments(x_ref[...].astype(F32))
    rows = normed * vec_ref[GAIN_ONE : GAIN_ONE + 1, :] + vec_ref[SHIFT_ONE : SHIFT_ONE + 1, :]
    rows = rows.astype(BF16)
    a_ref[...] = rows
    t_ref[...] = rows.T


def spot(slot, core, slots):
    return jnp.where(slot == 0, core, 1 + core * (slots - 1) + slot) if not isinstance(
        slot, int
    ) else (core if slot == 0 else 1 + core * (slots - 1) + slot)


def first_norm(where, inputs, small, shard, wide, block=512):
    seq, width = inputs.shape
    count = len(small)
    fixed = lambda a, b: pl.BlockSpec((a, b), lambda i: (0, 0))
    last = small[0].shape[0] // SUM_ROWS - 1
    return call(
        partial(norm_kernel, count, shard),
        "first_norm",
        (seq // block,),
        [SCALARS, pl.BlockSpec((block, width), lambda i: (i, 0))]
        + [pl.BlockSpec((SUM_ROWS, part.shape[1]), lambda i: (last, 0)) for part in small],
        [
            pl.BlockSpec((block, width), lambda i: (i, 0)),
            pl.BlockSpec((width, block), lambda i: (0, i)),
            fixed(8, width),
            fixed(1, wide),
            fixed(1, 3 * width),
        ],
        [
            shape((seq, width), BF16),
            shape((width, seq), BF16),
            shape((8, width), F32),
            shape((1, wide), F32),
            shape((1, 3 * width), F32),
        ],
    )(where, inputs, *small)


def qkv_kernel(count, slot, slots, where, a_ref, bias_ref, q, k, v, *rest):
    pieces = rest[:8]
    out_ref, kept_ref, full, sems, out_sems = rest[-5:]
    step, part = pl.program_id(0), pl.program_id(1)
    half = pieces[0].shape[2]

    def keep():
        return [
            pltpu.make_async_copy(
                full.at[:, core * half : (core + 1) * half],
                kept_ref.at[
                    :, (core * slots + slot) * 3 * PAIR : (core * slots + slot) * 3 * PAIR + half
                ],
                out_sems.at[core],
            )
            for core in range(2)
        ]

    @pl.when((step == 0) & (part == 0))
    def _():
        copies = pair_copies(where, (q, k, v), pieces, full, sems, count, slot)
        start_all(copies)
        wait_all(copies)
        start_all(keep())

    wide = out_ref.shape[1]
    column = pl.multiple_of(part * wide, wide)
    rows = (dot(a_ref[...], full[:, pl.ds(column, wide)]) + bias_ref[...]).astype(BF16)
    for begin in range(0, wide, PAIR):
        value = rows[:, begin : begin + PAIR]
        if begin // PAIR % 3 == 0:
            value = value * jnp.asarray(HEAD_DIM**-0.5, BF16)
        out_ref[:, begin : begin + PAIR] = value

    @pl.when((step == pl.num_programs(0) - 1) & (part == pl.num_programs(1) - 1))
    def _():
        wait_all(keep())


def project_qkv(where, attn_in, bias, own, pieces, count, slot, kept=()):
    seq, width = attn_in.shape
    slots = own[0].shape[1] // PAIR // 2
    half = pieces[0].shape[2]
    wide, parts, block = (2 * half, 1, 512) if slot == 0 else (half, 2, seq)
    first = 0 if slot == 0 else 1
    copies = copy_count(count) - 1 + 2 * half // PAIR
    return call(
        partial(qkv_kernel, count, slot, slots),
        "project_qkv",
        (seq // block, parts),
        [
            SCALARS,
            pl.BlockSpec((block, width), lambda i, n: (i, 0)),
            pl.BlockSpec((1, wide), lambda i, n: (0, first + n)),
        ]
        + [WHOLE] * (11 + len(kept)),
        [pl.BlockSpec((block, wide), lambda i, n: (i, first + n)), WHOLE],
        [shape((seq, 3 * width), BF16), shape((width, 3 * width), BF16)],
        [
            pltpu.VMEM((width, 2 * half), BF16),
            pltpu.SemaphoreType.DMA((copies,)),
            pltpu.SemaphoreType.DMA((2,)),
        ],
        aliases={14 + i: i for i in range(len(kept))},
    )(where, attn_in, bias, *own, *pieces, *kept)


def attend_kernel(where, lengths, places, q_ref, k_ref, v_ref, *rest):
    o_ref, e_ref, r_ref = rest[-3:]
    seq, block = k_ref.shape[0], q_ref.shape[0]
    first = lax.broadcasted_iota(jnp.int32, (seq, PAIR), 1) < HEAD_DIM
    here = lax.broadcasted_iota(jnp.int32, (block, PAIR), 1) < HEAD_DIM
    place = lax.broadcasted_iota(jnp.int32, (1, seq), 1)
    bias = jnp.where(place < lengths[places[where[3]]], 0.0, NEGATIVE).astype(F32)
    queries, keys, values = q_ref[...], k_ref[...], v_ref[...]
    zeros = jnp.zeros_like(keys)

    lanes = lax.broadcasted_iota(jnp.int32, (PAIR, PAIR), 0) < HEAD_DIM
    same = lanes == (lax.broadcasted_iota(jnp.int32, (PAIR, PAIR), 1) < HEAD_DIM)
    heads = same.astype(F32).astype(BF16)

    def longest(rows):
        return jnp.max(dot(rows * rows, heads))

    def run(shifted):
        blended, shares = [], []
        for head in range(2):
            head_keys = (
                jnp.where(first, keys, zeros) if head == 0 else jnp.where(first, zeros, keys)
            )
            scores = dot_nt(queries, head_keys) + bias
            if shifted:
                scores = scores - jnp.max(scores, axis=1, keepdims=True)
            raised = jnp.exp(scores)
            shares.append(1.0 / jnp.sum(raised, axis=1, keepdims=True))
            raised = raised.astype(BF16)
            e_ref[head] = raised
            blended.append(dot(raised, values))
        share = jnp.where(here, shares[0], shares[1])
        r_ref[...] = share
        o_ref[...] = (jnp.where(here, blended[0], blended[1]) * share).astype(BF16)

    small = longest(queries) * longest(keys) <= 3600.0

    @pl.when(small)
    def _():
        run(False)

    @pl.when(jnp.logical_not(small))
    def _():
        run(True)


def attend(cell, qkv, spots, pairs, kept=(), block=1024):
    seq, wide = qkv.shape
    total = wide // (3 * PAIR)
    there = lambda p: spots[0] + (spots[1] - spots[0]) * p
    here = lambda p: pairs[0] + (pairs[1] - pairs[0]) * p
    return call(
        attend_kernel,
        "attend",
        (2, seq // block),
        [
            SCALARS,
            SCALARS,
            SCALARS,
            pl.BlockSpec((block, PAIR), lambda p, b: (b, 3 * there(p))),
            pl.BlockSpec((seq, PAIR), lambda p, b: (0, 3 * there(p) + 1)),
            pl.BlockSpec((seq, PAIR), lambda p, b: (0, 3 * there(p) + 2)),
        ]
        + [WHOLE] * len(kept),
        [
            pl.BlockSpec((block, PAIR), lambda p, b: (b, here(p))),
            pl.BlockSpec((2, block, seq), lambda p, b: (here(p), b, 0)),
            pl.BlockSpec((block, PAIR), lambda p, b: (b, here(p))),
        ],
        [
            shape((seq, total * PAIR), BF16),
            shape((2 * total, seq, seq), BF16),
            shape((seq, total * PAIR), F32),
        ],
        aliases={6 + i: i for i in range(len(kept))},
    )(*cell, qkv, qkv, qkv, *kept)


ERF_P = 0.3275911 * 2.0**-0.5
ERF_A = (0.254829592, -0.284496736, 1.421413741, -1.453152027, 1.061405429)


def gelu_parts(values):
    bell = jnp.exp(values * values * -0.5)
    ratio = 1.0 / (1.0 + ERF_P * jnp.abs(values))
    tail = 0.5 * ERF_A[4]
    for term in ERF_A[3::-1]:
        tail = tail * ratio + 0.5 * term
    tail = tail * ratio * bell
    under = jnp.where(values > 0, 1.0 - tail, tail)
    return values * under, under + values * bell * 0.3989422804014327


def feed_kernel(
    count, where, x_ref, mix_ref, grad_ref, vec_ref, bias_ref, out_own, up_own, down_own, *rest
):
    second, third = rest[:8], rest[8:16]
    out_ref, gres_ref, gmix_ref, presum_ref, sums_ref = rest[16:21]
    halves = rest[21:27]
    w_out, w_up, w_down, t_out, t_up, t_down, sem_a, sem_b, sem_c, sem_out = rest[27:]
    step = pl.program_id(0)
    rows = up_own.shape[0] // 4
    blocks = up_own.shape[1] // 2 // second[0].shape[2]
    out_copies = column_copies(where, out_own, second, w_out, sem_a, count, blocks * rows)
    up_copies = column_copies(where, up_own, second, w_up, sem_b, count, 0)
    down_copies = row_copies(where, down_own, third, w_down, sem_c, count)

    @pl.when(step == 0)
    def _():
        start_all(out_copies)
        start_all(up_copies)
        start_all(down_copies)
        for ref in (t_out, t_up, t_down, presum_ref, sums_ref):
            ref[...] = jnp.zeros_like(ref)
        wait_all(out_copies)

    mix = mix_ref[...]
    grads = grad_ref[...]
    mixed = x_ref[...].astype(F32) + vec_ref[OUT_B : OUT_B + 1, :] + dot(mix, w_out[...])
    normed, inverse = moments(mixed)
    gain = vec_ref[GAIN_TWO : GAIN_TWO + 1, :]
    rows = (normed * gain + vec_ref[SHIFT_TWO : SHIFT_TWO + 1, :]).astype(BF16)

    @pl.when(step == 0)
    def _():
        wait_all(up_copies)
        wait_all(down_copies)

    def chunk(number, sums):
        result, grad_in = sums
        span = aligned(number * CHUNK, CHUNK, CHUNK)
        value, slope = gelu_parts(dot(rows, w_up[:, span]) + bias_ref[:, span])
        value = value.astype(BF16)
        result = result + dot(value, w_down[span, :])
        t_down[span, :] += dot_tn(value, grads)
        pre = (dot_nt(grads, w_down[span, :]) * slope).astype(BF16)
        presum_ref[:, span] += jnp.sum(pre.astype(F32), axis=0, keepdims=True)
        t_up[:, span] += dot_tn(rows, pre)
        return result, grad_in + dot_nt(pre, w_up[:, span])

    result, grad_in = lax.fori_loop(
        0,
        w_up.shape[1] // CHUNK,
        chunk,
        (mixed + vec_ref[DOWN_B : DOWN_B + 1, :], jnp.zeros(mixed.shape, F32)),
    )
    out_ref[...] = result.astype(BF16)
    grads = grads.astype(F32)
    grad_res = grads + norm_back(grad_in, normed, inverse, gain)
    gres_ref[...] = grad_res
    branch = grad_res.astype(BF16)
    gmix_ref[...] = dot_nt(branch, w_out[...]).astype(BF16)
    t_out[...] += dot_tn(mix, branch)
    sums_ref[0:1, :] += jnp.sum(grad_in * normed, axis=0, keepdims=True)
    sums_ref[1:2, :] += jnp.sum(grad_in, axis=0, keepdims=True)
    sums_ref[2:3, :] += jnp.sum(branch.astype(F32), axis=0, keepdims=True)
    sums_ref[3:4, :] += jnp.sum(grads, axis=0, keepdims=True)

    @pl.when(step == pl.num_programs(0) - 1)
    def _():
        copies = []
        half = w_down.shape[0] // 2
        part = half // count
        for place, core in enumerate((1 - where[2], where[2])):
            for z in range(count):
                begin = place * half + z * part
                source = aligned((2 * z + core) * part, part, 16)
                w_down[begin : begin + part, :] = t_down[source, :].astype(BF16)
            copies.append(
                pltpu.make_async_copy(
                    w_down.at[place * half : (place + 1) * half], halves[place], sem_out.at[place]
                )
            )
        start_all(copies)
        for number, (weight, total) in enumerate(((w_up, t_up), (w_out, t_out))):
            half = weight.shape[1] // 2
            for place, core in enumerate((1 - where[2], where[2])):
                span = slice(place * half, (place + 1) * half)
                weight[:, span] = total[:, aligned(core * half, half, 128)].astype(BF16)
                slot = 2 * number + 2 + place
                copies.append(
                    pltpu.make_async_copy(weight.at[:, span], halves[slot], sem_out.at[slot])
                )
                copies[-1].start()
        wait_all(copies)


def feed(
    where, inputs, mixed, grads, vectors, bias, out_own, up_own, down_own, second, third, count,
    block=256,
):
    seq, width = inputs.shape
    wide = up_own.shape[1]
    row = lambda n: pl.BlockSpec((block, n), lambda i: (i, 0))
    fixed = lambda a, b: pl.BlockSpec((a, b), lambda i: (0, 0))
    return call(
        partial(feed_kernel, count),
        "feed",
        (seq // block,),
        [SCALARS, row(width), row(width), row(width), fixed(*vectors.shape), fixed(1, wide)]
        + [WHOLE] * 19,
        [row(width), row(width), row(width), fixed(1, wide), fixed(8, width)] + [WHOLE] * 6,
        [
            shape((seq, width), BF16),
            shape((seq, width), F32),
            shape((seq, width), BF16),
            shape((1, wide), F32),
            shape((8, width), F32),
        ]
        + [shape((wide // 2, width), BF16)] * 2
        + [shape((width, wide // 2), BF16)] * 2
        + [shape((width, width // 2), BF16)] * 2,
        [
            pltpu.VMEM((width, width), BF16),
            pltpu.VMEM((width, wide), BF16),
            pltpu.VMEM((wide, width), BF16),
            pltpu.VMEM((width, width), F32),
            pltpu.VMEM((width, wide), F32),
            pltpu.VMEM((wide, width), F32),
        ]
        + [pltpu.SemaphoreType.DMA((2 * copy_count(count),))] * 3
        + [pltpu.SemaphoreType.DMA((6,))],
    )(where, inputs, mixed, grads, vectors, bias, out_own, up_own, down_own, *second, *third)


def attend_back_kernel(
    where, q_ref, k_ref, v_ref, do_ref, o_ref, r_ref, e_ref, in_ref, *rest
):
    out_ref, sum_ref, w_ref, k_acc, v_acc = rest[-5:]
    seq, block = k_ref.shape[0], q_ref.shape[0]
    step, last = pl.program_id(1), pl.num_programs(1) - 1
    first = lax.broadcasted_iota(jnp.int32, (seq, PAIR), 1) < HEAD_DIM
    here = lax.broadcasted_iota(jnp.int32, (block, PAIR), 1) < HEAD_DIM
    keys, values, queries = k_ref[...], v_ref[...], q_ref[...]
    zeros = jnp.zeros_like(values)

    @pl.when(step == 0)
    def _():
        k_acc[...] = jnp.zeros_like(k_acc)
        v_acc[...] = jnp.zeros_like(v_acc)

    grads = (do_ref[...].astype(F32) * r_ref[...]).astype(BF16)
    product = grads.astype(F32) * o_ref[...].astype(F32)
    whole = jnp.sum(product, axis=1, keepdims=True)
    part = jnp.sum(jnp.where(here, product, 0.0), axis=1, keepdims=True)
    inner = (part, whole - part)
    grads_t, queries_t = grads.T, queries.T
    grad_queries = []
    for head in range(2):
        head_values = (
            jnp.where(first, values, zeros) if head == 0 else jnp.where(first, zeros, values)
        )
        raised = e_ref[head]
        grad_shares = dot_nt(grads, head_values)
        grad_scores = (raised.astype(F32) * (grad_shares - inner[head])).astype(BF16)
        grad_queries.append(dot(grad_scores, keys))
        span = slice(head * HEAD_DIM, (head + 1) * HEAD_DIM)
        v_acc[span, :] += dot(grads_t[span], raised)
        k_acc[span, :] += dot(queries_t[span], grad_scores)
    rows = pl.ds(pl.multiple_of(step * block, block), block)
    mine = jnp.where(here, grad_queries[0], grad_queries[1]) * (HEAD_DIM**-0.5)
    out_ref[rows, 0:PAIR] = mine.astype(BF16)

    @pl.when(step == last)
    def _():
        out_ref[:, PAIR : 2 * PAIR] = k_acc[...].astype(BF16).T
        out_ref[:, 2 * PAIR : 3 * PAIR] = v_acc[...].astype(BF16).T
        sum_ref[...] = jnp.sum(out_ref[...].astype(F32), axis=0, keepdims=True)
        w_ref[...] = dot(in_ref[...], out_ref[...]).astype(BF16)


def attend_back(
    where, qkv, grad_mixed, mixed, shares, raised, in_t, other, block=1024
):
    seq = qkv.shape[0]
    pairs = qkv.shape[1] // (3 * PAIR) // 2

    def pair(p, w):
        return side(w, other) * pairs + p

    def there(p, w):
        return spot(p, side(w, other), pairs)

    return call(
        attend_back_kernel,
        "attend_back",
        (pairs, seq // block),
        [
            pl.BlockSpec((block, PAIR), lambda p, b, w: (b, 3 * there(p, w))),
            pl.BlockSpec((seq, PAIR), lambda p, b, w: (0, 3 * there(p, w) + 1)),
            pl.BlockSpec((seq, PAIR), lambda p, b, w: (0, 3 * there(p, w) + 2)),
            pl.BlockSpec((block, PAIR), lambda p, b, w: (b, pair(p, w))),
            pl.BlockSpec((block, PAIR), lambda p, b, w: (b, pair(p, w))),
            pl.BlockSpec((block, PAIR), lambda p, b, w: (b, pair(p, w))),
            pl.BlockSpec((2, block, seq), lambda p, b, w: (pair(p, w), b, 0)),
            pl.BlockSpec(in_t.shape, lambda p, b, w: (0, 0), pipeline_mode=pl.Buffered(1)),
        ],
        [
            pl.BlockSpec((seq, 3 * PAIR), lambda p, b, w: (0, p)),
            pl.BlockSpec((1, 3 * PAIR), lambda p, b, w: (0, p)),
            pl.BlockSpec((in_t.shape[0], 3 * PAIR), lambda p, b, w: (0, p)),
        ],
        [shape((seq, 3 * PAIR * pairs), BF16), shape((1, 3 * PAIR * pairs), F32), shape((in_t.shape[0], 3 * PAIR * pairs), BF16)],
        [pltpu.VMEM((PAIR, seq), F32)] * 2,
        prefetch=1,
    )(where, qkv, qkv, qkv, grad_mixed, mixed, shares, raised, in_t)


def input_kernel(
    where, other_ref, mine_ref, x_ref, gres_ref, vec_ref, w_other, w_mine,
    two_ref, pre_ref, sum_other, sum_mine, out_ref, sums_ref,
):
    width = x_ref.shape[1]

    @pl.when(pl.program_id(0) == 0)
    def _():
        sums_ref[...] = jnp.zeros_like(sums_ref)
        sums_ref[OUT_B : OUT_B + 1, :] = two_ref[2:3, :]
        sums_ref[GAIN_TWO : SHIFT_TWO + 1, :] = two_ref[0:2, :]
        sums_ref[DOWN_B : DOWN_B + 1, :] = two_ref[3:4, :]
        half = sum_mine.shape[1]
        for core in range(2):
            pick = jnp.where(where[2] == core, sum_mine[...], sum_other[...])
            for slot in range(half // (3 * PAIR)):
                column = (core * (half // (3 * PAIR)) + slot) * PAIR
                for row, kind in ((QUERY_B, 0), (VALUE_B, 2)):
                    begin = (3 * slot + kind) * PAIR
                    sums_ref[row : row + 1, column : column + PAIR] = pick[:, begin : begin + PAIR]
        for row in range(pre_ref.shape[1] // width):
            sums_ref[UP_B + row : UP_B + row + 1, :] = pre_ref[:, row * width : (row + 1) * width]

    grad_in = dot_nt(other_ref[...], w_other[...]) + dot_nt(mine_ref[...], w_mine[...])
    normed, inverse = moments(x_ref[...].astype(F32))
    gain = vec_ref[GAIN_ONE : GAIN_ONE + 1, :]
    out_ref[...] = (gres_ref[...] + norm_back(grad_in, normed, inverse, gain)).astype(BF16)
    sums_ref[GAIN_ONE : GAIN_ONE + 1, :] += jnp.sum(grad_in * normed, axis=0, keepdims=True)
    sums_ref[SHIFT_ONE : SHIFT_ONE + 1, :] += jnp.sum(grad_in, axis=0, keepdims=True)


def input_back(where, other, mine, inputs, grad_res, vectors, full, sums, block=256):
    seq, width = inputs.shape
    wide = other.shape[1]
    row = lambda n: pl.BlockSpec((block, n), lambda i, w: (i, 0))
    fixed = lambda a, b: pl.BlockSpec((a, b), lambda i, w: (0, 0))
    return call(
        input_kernel,
        "input_back",
        (seq // block,),
        [
            row(wide),
            row(wide),
            row(width),
            row(width),
            fixed(*vectors.shape),
            pl.BlockSpec((width, wide), lambda i, w: (0, 1 - w[2])),
            pl.BlockSpec((width, wide), lambda i, w: (0, w[2])),
        ]
        + [fixed(*part.shape) for part in sums],
        [row(width), fixed(SUM_ROWS, width)],
        [shape((seq, width), BF16), shape((SUM_ROWS, width), F32)],
        prefetch=1,
    )(where, other, mine, inputs, grad_res, vectors, full, full, *sums)


def outer_call(kernel, name, where, grid, in_specs, out_specs, out_shape, scratch, arrays):
    return call(kernel, name, grid, in_specs, out_specs, out_shape, scratch, 1)(where, *arrays)


def part_rows(where, total, outs, shards, column=0):
    rows = total.shape[0] // shards // 4
    span = slice(column, column + total.shape[1])
    for turn, out in enumerate(outs):
        for z in range(shards):
            begin = (z * 4 + (where[1] ^ turn)) * rows
            out[z, :, span] = total[aligned(begin, rows, 16), :].astype(BF16)


def side(w, other):
    return (1 - w[2]) if other else w[2]


def add_parts_kernel(shards, where, *refs):
    inputs, outs, total = refs[:-5], refs[-5:-1], refs[-1]
    begin = 0
    for mine, got in zip(inputs[0::2], inputs[1::2]):
        span = slice(begin, begin + mine.shape[1])
        total[:, span] = mine[...].astype(F32) + got[...].astype(F32)
        begin += mine.shape[1]
    part_rows(where, total, outs, shards)


def add_parts(where, pairs, count, steps=2):
    deep = pairs[0][0].shape[0]
    wide = sum(mine.shape[1] for mine, _ in pairs)
    rows = deep // count // 4
    arrays = [part for pair in pairs for part in pair]
    return outer_call(
        partial(add_parts_kernel, count // steps),
        "add_parts",
        where,
        (steps,),
        [pl.BlockSpec((deep // steps, part.shape[1]), lambda i, w: (i, 0)) for part in arrays],
        [pl.BlockSpec((count // steps, rows, wide), lambda i, w: (i, 0, 0))] * 4,
        [shape((count, rows, wide), BF16)] * 4,
        [pltpu.VMEM((deep // steps, wide), F32)],
        arrays,
    )


def total_of(refs, z):
    total = refs[0][z].astype(F32)
    for ref in refs[1:]:
        total = total + ref[z].astype(F32)
    return total.astype(BF16)


def quad_kernel(count, where, *refs):
    for step in range(count):
        refs[4 + step][...] = total_of(refs[:4], where[0] ^ step)


def quad_sum(where, parts, count):
    full = parts[0].shape
    return call(
        partial(quad_kernel, count),
        "quad_sum",
        (1,),
        [SCALARS] + [pl.BlockSpec(full, lambda i: (0, 0, 0))] * 4,
        [pl.BlockSpec(full[1:], lambda i: (0, 0))] * count,
        [shape(full[1:], BF16)] * count,
    )(where, *parts)


def quad_pairs_kernel(half, where, *refs):
    near, far = refs[4:]
    for step in range(half):
        near[step] = total_of(refs[:4], where[0] ^ (2 * step))
        far[step] = total_of(refs[:4], where[0] ^ (2 * step) ^ 1)


def quad_pairs(where, parts, count):
    full = parts[0].shape
    half = count // 2
    return call(
        partial(quad_pairs_kernel, half),
        "quad_pairs",
        (1,),
        [SCALARS] + [pl.BlockSpec(full, lambda i: (0, 0, 0))] * 4,
        [pl.BlockSpec((half, *full[1:]), lambda i: (0, 0, 0))] * 2,
        [shape((half, *full[1:]), BF16)] * 2,
    )(where, *parts)


def halve_kernel(a, b, mine, other):
    total = (a[...].astype(F32) + b[...].astype(F32)).astype(BF16)
    mine[...] = total[0]
    other[...] = total[1]


def halve(near, got):
    full = near.shape
    spec = pl.BlockSpec(full, lambda i: (0, 0, 0))
    return call(
        halve_kernel,
        "halve",
        (1,),
        [spec] * 2,
        [pl.BlockSpec(full[1:], lambda i: (0, 0))] * 2,
        [shape(full[1:], BF16)] * 2,
    )(near, got)


def blocks_of(rows, wide, width):
    return [
        (rows * number, begin, min(width, wide - begin))
        for number, begin in enumerate(range(0, wide, width))
    ]


def merge_kernel(down, down_got, two, two_got, out):
    deep, width = down.shape
    rows, wide = two.shape
    out[0:deep, :] = (down[...].astype(F32) + down_got[...].astype(F32)).astype(BF16)
    total = (two[...].astype(F32) + two_got[...].astype(F32)).astype(BF16)
    for row, begin, size in blocks_of(rows, wide, width):
        row += deep
        out[row : row + rows, 0:size] = total[:, begin : begin + size]
        if size < width:
            out[row : row + rows, size:width] = jnp.zeros((rows, width - size), BF16)


def merge(down, down_got, two, two_got):
    deep, width = down.shape
    rows, wide = two.shape
    tall = deep + rows * len(blocks_of(rows, wide, width))
    whole = lambda part: pl.BlockSpec(part.shape, lambda i: (0, 0))
    return call(
        merge_kernel,
        "merge",
        (1,),
        [whole(part) for part in (down, down_got, two, two_got)],
        pl.BlockSpec((tall, width), lambda i: (0, 0)),
        shape((tall, width), BF16),
    )(down, down_got, two, two_got)


def add_kernel(*refs):
    total = refs[0][...].astype(F32)
    for ref in refs[1:-1]:
        total = total + ref[...].astype(F32)
    refs[-1][...] = total.astype(refs[-1].dtype)


def add_all(parts):
    full = parts[0].shape
    spec = pl.BlockSpec(full, lambda i: (0,) * len(full))
    return call(
        add_kernel, "add_all", (1,), [spec] * len(parts), spec, shape(full, parts[0].dtype)
    )(*parts)


def halves_of(where, pieces, turn):
    low = where[2] == 0
    near, far = pieces[turn][...].astype(F32), pieces[4 + turn][...].astype(F32)
    return jnp.where(low, near, far), jnp.where(low, far, near)


def lay_merged_kernel(where, *refs):
    pieces, (down, out, up) = refs[:8], refs[8:]
    width, half = down.shape[1], out.shape[1] // 2
    deep = down.shape[0] // 8
    rows, wide = up.shape[0] // 4, half + up.shape[1] // 2
    for turn in range(4):
        quad = where[1] ^ turn
        for core, value in enumerate(halves_of(where, pieces, turn)):
            down[aligned((4 * core + quad) * deep, deep, 16), :] = value[0:deep]
            for row, begin, size in blocks_of(rows, wide, width):
                part = value[deep + row : deep + row + rows, 0:size]
                place = aligned(quad * rows, rows, 16)
                if begin < half:
                    out[place, core * half : (core + 1) * half] = part[:, 0:half]
                    part, begin = part[:, half:], half
                column = core * (wide - half) + begin - half
                up[place, column : column + part.shape[1]] = part


def lay_pairs_kernel(where, *refs):
    pieces, outs = refs[:8], refs[8:]
    rows, half = pieces[0].shape
    for turn in range(4):
        place = aligned((where[1] ^ turn) * rows, rows, 16)
        for core, value in enumerate(halves_of(where, pieces, turn)):
            for slot in range(half // (3 * PAIR)):
                begin = (core * (half // (3 * PAIR)) + slot) * PAIR
                for kind, out in enumerate(outs):
                    column = (3 * slot + kind) * PAIR
                    out[place, begin : begin + PAIR] = value[:, column : column + PAIR]


def lay(kernel, name, where, pieces, outs):
    spec = pl.BlockSpec(pieces[0].shape, lambda i: (0, 0))
    return call(
        kernel,
        name,
        (1,),
        [SCALARS] + [spec] * 8,
        [pl.BlockSpec(dims, lambda i: (0, 0)) for dims in outs],
        [shape(dims, F32) for dims in outs],
    )(where, *pieces)


def pick_kernel(count, where, a, b, *outs):
    total = a[...] + b[...]
    shard = outs[0].shape[0]
    for row, out in enumerate(outs[:UP_B]):
        value = total[row : row + 1, 0:shard]
        for z in range(1, count):
            value = jnp.where(where[0] == z, total[row : row + 1, z * shard : (z + 1) * shard], value)
        out[...] = value.reshape(shard)
    value = total[UP_B : UP_B + 1, :]
    for z in range(1, count):
        value = jnp.where(where[0] == z, total[UP_B + z : UP_B + z + 1, :], value)
    outs[UP_B][...] = value.reshape(outs[UP_B].shape[0])


def pick(where, a, b, shard, wide):
    sizes = [shard] * UP_B + [wide]
    return call(
        partial(pick_kernel, a.shape[1] // shard),
        "pick",
        (1,),
        [SCALARS] + [pl.BlockSpec(a.shape, lambda i: (0, 0))] * 2,
        [pl.BlockSpec((size,), lambda i: (0,)) for size in sizes],
        [shape((size,), F32) for size in sizes],
    )(where, a, b)


def tally_kernel(where, lengths, places, ids_ref, out_ref):
    ids = ids_ref[...]
    seq = ids.shape[1]
    live = lax.broadcasted_iota(jnp.int32, (1, seq), 1) < lengths[places[where[3]]]
    high, low = ids // 128, jnp.where(live, ids % 128, -1)
    tall = (lax.broadcasted_iota(jnp.int32, (TALLY_ROWS, seq), 0) == high).astype(F32).astype(BF16)
    wide = (lax.broadcasted_iota(jnp.int32, (128, seq), 0) == low).astype(F32).astype(BF16)
    out_ref[...] = dot_nt(tall, wide).astype(jnp.int32)


def tally(cell, ids):
    return call(
        tally_kernel,
        "tally",
        (1,),
        [SCALARS] * 3 + [pl.BlockSpec(ids.shape, lambda i: (0, 0))],
        pl.BlockSpec((TALLY_ROWS, 128), lambda i: (0, 0)),
        shape((TALLY_ROWS, 128), jnp.int32),
    )(*cell, ids)


def body(
    dp_size,
    fsdp_size,
    cells_in,
    out_grad,
    cell_length,
    cell_place,
    gene_ids,
    attn_norm_gain,
    attn_norm_bias,
    query_weight,
    query_bias,
    key_weight,
    value_weight,
    value_bias,
    out_weight,
    out_bias,
    ffn_norm_gain,
    ffn_norm_bias,
    up_weight,
    up_bias,
    down_weight,
    down_bias,
):
    count = fsdp_size
    seq, width = cells_in.shape[1:]
    place = lax.axis_index("dp")
    z = lax.axis_index("fsdp")
    core, quad = place & 1, (place >> 1) & 3
    where = jnp.stack([z, quad, core, place * fsdp_size + z]).astype(jnp.int32)
    cell = (where, cell_length.astype(jnp.int32), cell_place.astype(jnp.int32))

    def swap(value, mask):
        return lax.ppermute(value, "dp", [(i, i ^ mask) for i in range(dp_size)])

    def turn(value, step):
        return lax.ppermute(value, "fsdp", [(i, i ^ step) for i in range(count)])

    def from_quad(value):
        return [swap(value, 2 * mask) for mask in (1, 2, 3)]

    def to_quad(parts):
        return [swap(parts[mask], 2 * mask) for mask in (1, 2, 3)]

    def from_column(value):
        return [turn(value, step) for step in range(1, count)]

    def to_column(parts):
        return [turn(parts[step], step) for step in range(1, count)]

    def to_core(parts, beside=None, at_once=2):
        first = lambda: (
            [swap(part, 1) for part in parts[:at_once]], beside() if beside else ()
        )
        got, result = during(first)
        if at_once < len(parts):
            got = got + during(lambda: [swap(part, 1) for part in parts[at_once:]])
        return (got, result) if beside else got

    def beyond(total):
        mask = 8
        while mask < dp_size:
            total = add_all([total, swap(total, mask)])
            mask *= 2
        return total

    inputs = cells_in.reshape(seq, width)
    grads = out_grad.reshape(seq, width)
    live = cell_length[0] > 0

    def during(run):
        outs = jax.eval_shape(run)
        blank = lambda: jax.tree.map(lambda out: jnp.zeros(out.shape, out.dtype), outs)
        return lax.cond(live, run, blank)

    shard = attn_norm_gain.shape[0]
    small = [
        attn_norm_gain,
        attn_norm_bias,
        out_bias,
        ffn_norm_gain,
        ffn_norm_bias,
        down_bias,
        query_bias,
        value_bias,
        up_bias,
    ]
    own = (query_weight, key_weight, value_weight)
    pairs = width // PAIR
    deep = down_weight.shape[0] // 8
    first, rest = pack(where, *own, out_weight, up_weight, down_weight, small)

    rows, wide = first.shape[0] - SUM_ROWS, first.shape[1]
    group = 3 * PAIR

    far, counts = during(lambda: (from_column(first), tally(cell, gene_ids)))
    early, later = split(far, [(0, 0, rows, group), (0, group, rows, wide - group)])
    small = [first] + far
    last = pairs // 2

    def first_stage():
        near, norm = during(
            lambda: (
                from_quad(early),
                first_norm(where, inputs, small, shard, count * up_bias.shape[0]),
            )
        )
        near = [early] + near
        pieces = near + to_core(near, at_once=4)

        def stage():
            kept = project_qkv(where, norm[0], norm[4], own, pieces, count, 0)
            return kept, attend(cell, kept[0], (0, 1), (0, last))

        far, (kept, mixed) = during(lambda: (from_quad(later), during(stage)))
        return norm, far, kept, mixed

    rest, ((attn_in, attn_in_t, vectors, up_b, bias), far, kept, mixed) = during(
        lambda: (lax.all_gather(rest, "fsdp", axis=0), during(first_stage))
    )
    second, third = sort(where, rest, (rest.shape[1] - deep, deep))
    later = [later] + far

    def stage():
        pieces = later + to_core(later)
        out = project_qkv(where, attn_in, bias, own, pieces, count, 1, kept)
        return out, attend(cell, out[0], (2, 3), (1, 2), mixed)

    far, ((qkv, qkv_full), mixed) = during(lambda: (from_quad(second), during(stage)))
    second = [second] + far
    far, (other, (mixed, raised, shares)) = during(
        lambda: (
            from_quad(third),
            to_core(
                second,
                lambda: attend(cell, qkv, (4, 5), (last + 1, last + 2), mixed),
            ),
        )
    )
    second, third = second + other, [third] + far
    third = third + to_core(third, at_once=4)
    counts, (block_out, grad_res, grad_mixed, pre_sum, two_sums, *halves) = during(
        lambda: (
            lax.psum(counts, "fsdp"),
            feed(
                where, inputs, mixed, grads, vectors, up_b, out_weight, up_weight, down_weight,
                second, third, count,
            ),
        )
    )
    down_theirs, down_mine, up_theirs, up_mine, out_theirs, out_mine = halves

    def backward():
        down_got = during(lambda: swap(down_theirs, 1))
        down_parts = add_parts(where, [(down_mine, down_got)], count)

        got, (up_got, out_got, (grads_other, sums_other, qkv_theirs)) = during(
            lambda: (
                to_quad(down_parts),
                during(
                    lambda: (
                        swap(up_theirs, 1),
                        swap(out_theirs, 1),
                        attend_back(
                            where, qkv, grad_mixed, mixed, shares, raised, attn_in_t, True
                        ),
                    )
                ),
            )
        )
        two_parts = add_parts(where, [(out_mine, out_got), (up_mine, up_got)], count)
        down_near, down_far = quad_pairs(where, [down_parts[0]] + got, count)

        def stage():
            got, far, (grads_mine, sums_mine, mine) = during(
                lambda: (
                    swap(qkv_theirs, 1),
                    turn(down_far, 1),
                    attend_back(where, qkv, grad_mixed, mixed, shares, raised, attn_in_t, False),
                )
            )
            parts = add_parts(where, [(mine, got)], count)
            return parts, halve(down_near, far), grads_mine, sums_mine

        got, (qkv_parts, (down_piece, down_next), grads_mine, sums_mine) = during(
            lambda: (to_quad(two_parts), during(stage))
        )

        def stage():
            near, far = quad_pairs(where, [two_parts[0]] + got, count)
            far, down_got, (back, sums) = during(
                lambda: (
                    turn(far, 1),
                    turn(down_next, 2),
                    input_back(
                        where, grads_other, grads_mine, inputs, grad_res, vectors, qkv_full,
                        (two_sums, pre_sum, sums_other, sums_mine),
                    ),
                )
            )
            piece, following = halve(near, far)
            got_too, more = during(lambda: (turn(following, 2), swap(sums, 1)))
            sums = add_all([sums, more])
            merged = beyond(merge(down_piece, down_got, piece, got_too))
            return merged, back, sums

        got, (merged, input_grad, sums) = during(lambda: (to_quad(qkv_parts), during(stage)))
        qkv_parts = quad_sum(where, [qkv_parts[0]] + got, count)
        got, (side, other_side) = during(
            lambda: (to_column(qkv_parts), during(lambda: (swap(merged, 2), swap(merged, 4))))
        )
        qkv_piece = beyond(add_all([qkv_parts[0]] + got))
        far, (across, more) = during(
            lambda: (from_quad(qkv_piece), during(lambda: (swap(merged, 6), swap(sums, 2))))
        )
        qkv_pieces, merged = [qkv_piece] + far, [merged, side, other_side, across]
        sums = add_all([sums, more])
        other, more = during(lambda: ([swap(part, 1) for part in qkv_pieces], swap(sums, 4)))
        sums = sums + more
        mask = 8
        while mask < dp_size:
            sums = sums + swap(sums, mask)
            mask *= 2
        sums_got, (far, (grad_query, grad_key, grad_value)) = during(
            lambda: (
                turn(sums, 1),
                to_core(
                    merged,
                    lambda: lay(
                        lay_pairs_kernel, "lay_qkv", where, qkv_pieces + other,
                        [query_weight.shape] * 3,
                    ),
                    4,
                ),
            )
        )
        sums = add_all([sums, sums_got])
        more, (grad_down, grad_out, grad_up) = during(
            lambda: (
                turn(sums, 2),
                lay(
                    lay_merged_kernel, "lay_merged", where, merged + far,
                    [down_weight.shape, out_weight.shape, up_weight.shape],
                ),
            )
        )
        vec = pick(where, sums, more, shard, up_bias.shape[0])
        return input_grad, vec, grad_query, grad_key, grad_value, grad_out, grad_up, grad_down

    counts, results = during(lambda: (lax.psum(counts, "dp"), during(backward)))
    input_grad, vec, grad_query, grad_key, grad_value, grad_out, grad_up, grad_down = results
    gene_counts = counts.reshape(-1)[:VOCAB]

    return (
        block_out.reshape(cells_in.shape),
        input_grad.reshape(cells_in.shape),
        vec[0],
        vec[1],
        grad_query,
        vec[6],
        grad_key,
        grad_value,
        vec[7],
        grad_out,
        vec[2],
        vec[3],
        vec[4],
        grad_up,
        vec[UP_B],
        grad_down,
        vec[5],
        gene_counts,
    )


def solution(mesh):
    cells = P(("dp", "fsdp"), None, None)
    vector = P("fsdp")
    matrix = P("fsdp", None)
    in_specs = (
        cells,
        cells,
        P(),
        P(),
        P(("dp", "fsdp"), None),
        vector,
        vector,
        matrix,
        vector,
        matrix,
        matrix,
        vector,
        matrix,
        vector,
        vector,
        vector,
        matrix,
        vector,
        matrix,
        vector,
    )
    out_specs = (
        cells,
        cells,
        vector,
        vector,
        matrix,
        vector,
        matrix,
        matrix,
        vector,
        matrix,
        vector,
        vector,
        vector,
        matrix,
        vector,
        matrix,
        vector,
        P(),
    )
    return jax.shard_map(
        partial(body, mesh.shape["dp"], mesh.shape["fsdp"]),
        mesh=mesh,
        in_specs=in_specs,
        out_specs=out_specs,
        check_vma=False,
    )
```

```python
from functools import partial

import jax
import jax.numpy as jnp
from jax import lax
from jax.experimental import pallas as pl
from jax.experimental.pallas import tpu as pltpu
from jax.sharding import PartitionSpec as P

HEADS = 12
HEAD_DIM = 64
VOCAB = 36000
EPSILON = 1e-05
NEGATIVE = -1e30
PAIR = 2 * HEAD_DIM
CHUNK = 1536
TALLY_ROWS = 288

F32 = jnp.float32
BF16 = jnp.bfloat16
VMEM_LIMIT = 60 << 20

GAIN_ONE, SHIFT_ONE, OUT_B, GAIN_TWO, SHIFT_TWO, DOWN_B, QUERY_B, VALUE_B, UP_B = range(9)
SUM_ROWS = 16

WHOLE = pl.BlockSpec(memory_space=pl.ANY)
SCALARS = pl.BlockSpec(memory_space=pltpu.SMEM)


LIGHT = pl.CostEstimate(flops=1024, transcendentals=0, bytes_accessed=1024)


def call(kernel, name, grid, in_specs, out_specs, out_shape, scratch=(), prefetch=0, aliases=None):
    return pl.pallas_call(
        kernel,
        grid_spec=pltpu.PrefetchScalarGridSpec(
            num_scalar_prefetch=prefetch,
            grid=grid,
            in_specs=in_specs,
            out_specs=out_specs,
            scratch_shapes=scratch,
        ),
        out_shape=out_shape,
        input_output_aliases=aliases or {},
        compiler_params=pltpu.CompilerParams(vmem_limit_bytes=VMEM_LIMIT),
        cost_estimate=LIGHT,
        name=name,
    )


def shape(dims, dtype):
    return jax.ShapeDtypeStruct(dims, dtype)


def dot(left, right):
    return jnp.dot(left, right, preferred_element_type=F32)


def dot_nt(left, right):
    return lax.dot_general(left, right, (((1,), (1,)), ((), ())), preferred_element_type=F32)


def dot_tn(left, right):
    return lax.dot_general(left, right, (((0,), (0,)), ((), ())), preferred_element_type=F32)


def moments(values):
    width = values.shape[-1]
    center = values - jnp.sum(values, axis=-1, keepdims=True) * (1.0 / width)
    spread = jnp.sum(center * center, axis=-1, keepdims=True) * (1.0 / width)
    inverse = lax.rsqrt(spread + EPSILON)
    return center * inverse, inverse


def norm_back(grad_out, normed, inverse, gain):
    width = normed.shape[-1]
    scaled = grad_out * gain
    mean = jnp.sum(scaled, axis=-1, keepdims=True) * (1.0 / width)
    along = jnp.sum(scaled * normed, axis=-1, keepdims=True) * (1.0 / width)
    return inverse * (scaled - mean - normed * along)


def start_all(copies):
    for copy in copies:
        copy.start()


def wait_all(copies):
    for copy in copies:
        copy.wait()


def aligned(begin, size, unit):
    return pl.ds(pl.multiple_of(begin, unit), size)


def pack_kernel(slots, where, *refs):
    pairs, (o, up, down), small, (first, rest) = (
        refs[: 3 * slots], refs[3 * slots : 3 * slots + 3], refs[3 * slots + 3 : -2], refs[-2:],
    )
    rows, half = o.shape
    width = down.shape[1]
    for number, ref in enumerate(pairs):
        first[0:rows, number * PAIR : (number + 1) * PAIR] = ref[...]
    first[rows:, :] = jnp.zeros((first.shape[0] - rows, first.shape[1]), BF16)
    for number, ref in enumerate(small):
        value = ref[...].astype(F32).reshape(1, -1).astype(BF16)
        first[rows + number : rows + number + 1, 0 : ref.shape[0]] = value
    row = 0
    for begin in range(0, up.shape[1], width):
        rest[row : row + rows, :] = up[:, begin : begin + width]
        row += rows
    rest[row : row + rows, 0:half] = o[...]
    rest[row : row + rows, half:width] = jnp.zeros((rows, width - half), BF16)
    rest[row + rows :, :] = down[...]


def pack(where, q, k, v, o, up, down, small):
    rows, width = q.shape[0] // 4, q.shape[1]
    slots = width // PAIR // 2
    deep = down.shape[0] // 8
    first = (rows + SUM_ROWS, 3 * PAIR * slots)
    rest = (rows * (up.shape[1] // 2 // width + 1) + deep, width)
    return call(
        partial(pack_kernel, slots),
        "pack",
        (1,),
        [
            pl.BlockSpec((rows, PAIR), lambda i, w, s=slot: (w[1], slots * w[2] + s))
            for slot in range(slots)
            for _ in range(3)
        ]
        + [
            pl.BlockSpec((rows, o.shape[1] // 2), lambda i, w: (w[1], w[2])),
            pl.BlockSpec((rows, up.shape[1] // 2), lambda i, w: (w[1], w[2])),
            pl.BlockSpec((deep, width), lambda i, w: (4 * w[2] + w[1], 0)),
        ]
        + [pl.BlockSpec(part.shape, lambda i, w: (0,)) for part in small],
        [pl.BlockSpec(part, lambda i, w: (0, 0)) for part in (first, rest)],
        [shape(part, BF16) for part in (first, rest)],
        prefetch=1,
    )(where, *([q, k, v] * slots), o, up, down, *small)


def split_kernel(parts, *refs):
    ins, outs = refs[: -len(parts)], refs[-len(parts) :]
    for (row, column), out in zip(parts, outs):
        rows, columns = out.shape[1:]
        for number, ref in enumerate(ins):
            out[number] = ref[row : row + rows, column : column + columns]


def split(arrays, parts):
    full = arrays[0].shape
    return call(
        partial(split_kernel, [part[:2] for part in parts]),
        "split",
        (1,),
        [pl.BlockSpec(full, lambda i: (0, 0))] * len(arrays),
        [pl.BlockSpec((len(arrays), *part[2:]), lambda i: (0, 0, 0)) for part in parts],
        [shape((len(arrays), *part[2:]), BF16) for part in parts],
    )(*arrays)


def sort_kernel(where, gathered, *outs):
    begin = 0
    for out in outs:
        rows = out.shape[1]
        for number in range(out.shape[0]):
            out[number] = gathered[where[0] ^ (number + 1), begin : begin + rows, :]
        begin += rows


def sort(where, gathered, sizes):
    count, _, width = gathered.shape
    return call(
        sort_kernel,
        "sort",
        (1,),
        [SCALARS, pl.BlockSpec(gathered.shape, lambda i: (0, 0, 0))],
        [pl.BlockSpec((count - 1, size, width), lambda i: (0, 0, 0)) for size in sizes],
        [shape((count - 1, size, width), BF16) for size in sizes],
    )(where, gathered)


def remote_places(where, pieces, count):
    z, quad, core = where[0], where[1], where[2]
    for number, piece in enumerate(pieces):
        turn, side = number % 4, number // 4
        for step in range(1, count):
            yield piece, step - 1, z ^ step, quad ^ turn, core ^ side


def pair_copies(where, own, pieces, full, sems, count, slot):
    shard = own[0].shape[0]
    slots = own[0].shape[1] // PAIR // 2
    rows, half = pieces[0].shape[1:]
    copies = []
    for kind, ref in enumerate(own):
        for core in range(2):
            for number in range(half // (3 * PAIR)):
                source = (core * slots + slot + number) * PAIR
                target = core * half + (3 * number + kind) * PAIR
                copies.append(
                    pltpu.make_async_copy(
                        ref.at[:, source : source + PAIR],
                        full.at[aligned(where[0] * shard, shard, 16), target : target + PAIR],
                        sems.at[len(copies)],
                    )
                )
    for piece, step, z, quad, core in remote_places(where, pieces, count):
        copies.append(
            pltpu.make_async_copy(
                piece.at[step],
                full.at[aligned(z * shard + quad * rows, rows, 16), aligned(core * half, half, 128)],
                sems.at[len(copies)],
            )
        )
    return copies


def column_copies(where, own, pieces, full, sems, count, row):
    shard = own.shape[0]
    rows, half = shard // 4, own.shape[1] // 2
    width = pieces[0].shape[2]
    copies = [pltpu.make_async_copy(own, full.at[aligned(where[0] * shard, shard, 16)], sems.at[0])]
    for piece, step, z, quad, core in remote_places(where, pieces, count):
        for number, begin in enumerate(range(0, half, width)):
            size = min(width, half - begin)
            copies.append(
                pltpu.make_async_copy(
                    piece.at[step, row + number * rows : row + (number + 1) * rows, 0:size],
                    full.at[
                        aligned(z * shard + quad * rows, rows, 16),
                        aligned(core * half + begin, size, 128),
                    ],
                    sems.at[len(copies)],
                )
            )
    return copies


def row_copies(where, own, pieces, full, sems, count):
    shard = own.shape[0]
    rows = pieces[0].shape[1]
    copies = [
        pltpu.make_async_copy(own, full.at[aligned(where[0] * shard, shard, 16)], sems.at[0])
    ]
    for piece, step, z, quad, core in remote_places(where, pieces, count):
        copies.append(
            pltpu.make_async_copy(
                piece.at[step],
                full.at[aligned(z * shard + core * 4 * rows + quad * rows, rows, 16)],
                sems.at[len(copies)],
            )
        )
    return copies


def copy_count(count):
    return 1 + 8 * (count - 1)


def norm_kernel(count, shard, where, x_ref, *rest):
    small, (a_ref, t_ref, vec_ref, up_ref, bias_ref) = rest[:count], rest[count:]

    @pl.when(pl.program_id(0) == 0)
    def _():
        wide = up_ref.shape[1] // count
        for owner in range(count):
            value = small[0][...].astype(F32)
            for step in range(1, count):
                here = (where[0] ^ step) == owner
                value = jnp.where(here, small[step][...].astype(F32), value)
            vec_ref[:, owner * shard : (owner + 1) * shard] = value[0:8, 0:shard]
            up_ref[:, owner * wide : (owner + 1) * wide] = value[UP_B : UP_B + 1, 0:wide]
        slots = vec_ref.shape[1] // PAIR // 2
        for core in range(2):
            for slot in range(slots):
                span = slice((core * slots + slot) * PAIR, (core * slots + slot + 1) * PAIR)
                begin = 3 * PAIR * spot(slot, core, slots)
                bias_ref[:, begin : begin + PAIR] = vec_ref[QUERY_B : QUERY_B + 1, span]
                bias_ref[:, begin + PAIR : begin + 2 * PAIR] = jnp.zeros((1, PAIR), F32)
                bias_ref[:, begin + 2 * PAIR : begin + 3 * PAIR] = vec_ref[
                    VALUE_B : VALUE_B + 1, span
                ]

    normed, _ = moments(x_ref[...].astype(F32))
    rows = normed * vec_ref[GAIN_ONE : GAIN_ONE + 1, :] + vec_ref[SHIFT_ONE : SHIFT_ONE + 1, :]
    rows = rows.astype(BF16)
    a_ref[...] = rows
    t_ref[...] = rows.T


def spot(slot, core, slots):
    return jnp.where(slot == 0, core, 1 + core * (slots - 1) + slot) if not isinstance(
        slot, int
    ) else (core if slot == 0 else 1 + core * (slots - 1) + slot)


def first_norm(where, inputs, small, shard, wide, block=512):
    seq, width = inputs.shape
    count = len(small)
    fixed = lambda a, b: pl.BlockSpec((a, b), lambda i: (0, 0))
    last = small[0].shape[0] // SUM_ROWS - 1
    return call(
        partial(norm_kernel, count, shard),
        "first_norm",
        (seq // block,),
        [SCALARS, pl.BlockSpec((block, width), lambda i: (i, 0))]
        + [pl.BlockSpec((SUM_ROWS, part.shape[1]), lambda i: (last, 0)) for part in small],
        [
            pl.BlockSpec((block, width), lambda i: (i, 0)),
            pl.BlockSpec((width, block), lambda i: (0, i)),
            fixed(8, width),
            fixed(1, wide),
            fixed(1, 3 * width),
        ],
        [
            shape((seq, width), BF16),
            shape((width, seq), BF16),
            shape((8, width), F32),
            shape((1, wide), F32),
            shape((1, 3 * width), F32),
        ],
    )(where, inputs, *small)


def qkv_kernel(count, slot, slots, where, a_ref, bias_ref, q, k, v, *rest):
    pieces = rest[:8]
    out_ref, kept_ref, full, sems, out_sems = rest[-5:]
    step, part = pl.program_id(0), pl.program_id(1)
    half = pieces[0].shape[2]

    def keep():
        return [
            pltpu.make_async_copy(
                full.at[:, core * half : (core + 1) * half],
                kept_ref.at[
                    :, (core * slots + slot) * 3 * PAIR : (core * slots + slot) * 3 * PAIR + half
                ],
                out_sems.at[core],
            )
            for core in range(2)
        ]

    @pl.when((step == 0) & (part == 0))
    def _():
        copies = pair_copies(where, (q, k, v), pieces, full, sems, count, slot)
        start_all(copies)
        wait_all(copies)
        start_all(keep())

    wide = out_ref.shape[1]
    column = pl.multiple_of(part * wide, wide)
    rows = (dot(a_ref[...], full[:, pl.ds(column, wide)]) + bias_ref[...]).astype(BF16)
    for begin in range(0, wide, PAIR):
        value = rows[:, begin : begin + PAIR]
        if begin // PAIR % 3 == 0:
            value = value * jnp.asarray(HEAD_DIM**-0.5, BF16)
        out_ref[:, begin : begin + PAIR] = value

    @pl.when((step == pl.num_programs(0) - 1) & (part == pl.num_programs(1) - 1))
    def _():
        wait_all(keep())


def project_qkv(where, attn_in, bias, own, pieces, count, slot, kept=()):
    seq, width = attn_in.shape
    slots = own[0].shape[1] // PAIR // 2
    half = pieces[0].shape[2]
    wide, parts, block = (2 * half, 1, 512) if slot == 0 else (half, 2, seq)
    first = 0 if slot == 0 else 1
    copies = copy_count(count) - 1 + 2 * half // PAIR
    return call(
        partial(qkv_kernel, count, slot, slots),
        "project_qkv",
        (seq // block, parts),
        [
            SCALARS,
            pl.BlockSpec((block, width), lambda i, n: (i, 0)),
            pl.BlockSpec((1, wide), lambda i, n: (0, first + n)),
        ]
        + [WHOLE] * (11 + len(kept)),
        [pl.BlockSpec((block, wide), lambda i, n: (i, first + n)), WHOLE],
        [shape((seq, 3 * width), BF16), shape((width, 3 * width), BF16)],
        [
            pltpu.VMEM((width, 2 * half), BF16),
            pltpu.SemaphoreType.DMA((copies,)),
            pltpu.SemaphoreType.DMA((2,)),
        ],
        aliases={14 + i: i for i in range(len(kept))},
    )(where, attn_in, bias, *own, *pieces, *kept)


def attend_kernel(where, lengths, places, q_ref, k_ref, v_ref, *rest):
    o_ref, e_ref, r_ref = rest[-3:]
    seq, block = k_ref.shape[0], q_ref.shape[0]
    first = lax.broadcasted_iota(jnp.int32, (seq, PAIR), 1) < HEAD_DIM
    place = lax.broadcasted_iota(jnp.int32, (1, seq), 1)
    bias = jnp.where(place < lengths[places[where[3]]], 0.0, NEGATIVE).astype(F32)
    queries, keys, values = q_ref[...], k_ref[...], v_ref[...]
    zeros = jnp.zeros_like(keys)

    lanes = lax.broadcasted_iota(jnp.int32, (PAIR, PAIR), 0) < HEAD_DIM
    same = lanes == (lax.broadcasted_iota(jnp.int32, (PAIR, PAIR), 1) < HEAD_DIM)
    heads = same.astype(F32).astype(BF16)

    def longest(rows):
        return jnp.max(dot(rows * rows, heads))

    def run(rows, size, shifted):
        here = lax.broadcasted_iota(jnp.int32, (size, PAIR), 1) < HEAD_DIM
        part = q_ref[rows, :]
        blended, shares = [], []
        for head in range(2):
            head_keys = (
                jnp.where(first, keys, zeros) if head == 0 else jnp.where(first, zeros, keys)
            )
            scores = dot_nt(part, head_keys) + bias
            if shifted:
                scores = scores - jnp.max(scores, axis=1, keepdims=True)
            raised = jnp.exp(scores)
            shares.append(1.0 / jnp.sum(raised, axis=1, keepdims=True))
            raised = raised.astype(BF16)
            e_ref[head, rows, :] = raised
            blended.append(dot(raised, values))
        share = jnp.where(here, shares[0], shares[1])
        r_ref[rows, :] = share
        o_ref[rows, :] = (jnp.where(here, blended[0], blended[1]) * share).astype(BF16)

    small = longest(queries) * longest(keys) <= 3600.0

    @pl.when(small)
    def _():
        run(slice(0, block), block, False)

    @pl.when(jnp.logical_not(small))
    def _():
        size = 128

        @pl.loop(0, block // size)
        def _(number):
            run(aligned(number * size, size, size), size, True)


def attend(cell, qkv, spots, pairs, kept=(), block=1024):
    seq, wide = qkv.shape
    total = wide // (3 * PAIR)
    there = lambda p: spots[0] + (spots[1] - spots[0]) * p
    here = lambda p: pairs[0] + (pairs[1] - pairs[0]) * p
    return call(
        attend_kernel,
        "attend",
        (2, seq // block),
        [
            SCALARS,
            SCALARS,
            SCALARS,
            pl.BlockSpec((block, PAIR), lambda p, b: (b, 3 * there(p))),
            pl.BlockSpec((seq, PAIR), lambda p, b: (0, 3 * there(p) + 1)),
            pl.BlockSpec((seq, PAIR), lambda p, b: (0, 3 * there(p) + 2)),
        ]
        + [WHOLE] * len(kept),
        [
            pl.BlockSpec((block, PAIR), lambda p, b: (b, here(p))),
            pl.BlockSpec((2, block, seq), lambda p, b: (here(p), b, 0)),
            pl.BlockSpec((block, PAIR), lambda p, b: (b, here(p))),
        ],
        [
            shape((seq, total * PAIR), BF16),
            shape((2 * total, seq, seq), BF16),
            shape((seq, total * PAIR), F32),
        ],
        aliases={6 + i: i for i in range(len(kept))},
    )(*cell, qkv, qkv, qkv, *kept)


ERF_P = 0.3275911 * 2.0**-0.5
ERF_A = (0.254829592, -0.284496736, 1.421413741, -1.453152027, 1.061405429)


def gelu_parts(values):
    bell = jnp.exp(values * values * -0.5)
    ratio = 1.0 / (1.0 + ERF_P * jnp.abs(values))
    tail = 0.5 * ERF_A[4]
    for term in ERF_A[3::-1]:
        tail = tail * ratio + 0.5 * term
    tail = tail * ratio * bell
    under = jnp.where(values > 0, 1.0 - tail, tail)
    return values * under, under + values * bell * 0.3989422804014327


def feed_kernel(
    count, where, x_ref, mix_ref, grad_ref, vec_ref, bias_ref, out_own, up_own, down_own, *rest
):
    second, third = rest[:8], rest[8:16]
    out_ref, gres_ref, gmix_ref, presum_ref, sums_ref = rest[16:21]
    halves = rest[21:27]
    w_out, w_up, w_down, t_out, t_up, t_down, sem_a, sem_b, sem_c, sem_out = rest[27:]
    step = pl.program_id(0)
    rows = up_own.shape[0] // 4
    blocks = up_own.shape[1] // 2 // second[0].shape[2]
    out_copies = column_copies(where, out_own, second, w_out, sem_a, count, blocks * rows)
    up_copies = column_copies(where, up_own, second, w_up, sem_b, count, 0)
    down_copies = row_copies(where, down_own, third, w_down, sem_c, count)

    @pl.when(step == 0)
    def _():
        start_all(out_copies)
        start_all(up_copies)
        start_all(down_copies)
        for ref in (t_out, t_up, t_down, presum_ref, sums_ref):
            ref[...] = jnp.zeros_like(ref)
        wait_all(out_copies)

    mix = mix_ref[...]
    grads = grad_ref[...]
    mixed = x_ref[...].astype(F32) + vec_ref[OUT_B : OUT_B + 1, :] + dot(mix, w_out[...])
    normed, inverse = moments(mixed)
    gain = vec_ref[GAIN_TWO : GAIN_TWO + 1, :]
    rows = (normed * gain + vec_ref[SHIFT_TWO : SHIFT_TWO + 1, :]).astype(BF16)

    @pl.when(step == 0)
    def _():
        wait_all(up_copies)
        wait_all(down_copies)

    def chunk(number, sums):
        result, grad_in = sums
        span = aligned(number * CHUNK, CHUNK, CHUNK)
        value, slope = gelu_parts(dot(rows, w_up[:, span]) + bias_ref[:, span])
        value = value.astype(BF16)
        result = result + dot(value, w_down[span, :])
        t_down[span, :] += dot_tn(value, grads)
        pre = (dot_nt(grads, w_down[span, :]) * slope).astype(BF16)
        presum_ref[:, span] += jnp.sum(pre.astype(F32), axis=0, keepdims=True)
        t_up[:, span] += dot_tn(rows, pre)
        return result, grad_in + dot_nt(pre, w_up[:, span])

    result, grad_in = lax.fori_loop(
        0,
        w_up.shape[1] // CHUNK,
        chunk,
        (mixed + vec_ref[DOWN_B : DOWN_B + 1, :], jnp.zeros(mixed.shape, F32)),
    )
    out_ref[...] = result.astype(BF16)
    grads = grads.astype(F32)
    grad_res = grads + norm_back(grad_in, normed, inverse, gain)
    gres_ref[...] = grad_res
    branch = grad_res.astype(BF16)
    gmix_ref[...] = dot_nt(branch, w_out[...]).astype(BF16)
    t_out[...] += dot_tn(mix, branch)
    sums_ref[0:1, :] += jnp.sum(grad_in * normed, axis=0, keepdims=True)
    sums_ref[1:2, :] += jnp.sum(grad_in, axis=0, keepdims=True)
    sums_ref[2:3, :] += jnp.sum(branch.astype(F32), axis=0, keepdims=True)
    sums_ref[3:4, :] += jnp.sum(grads, axis=0, keepdims=True)

    @pl.when(step == pl.num_programs(0) - 1)
    def _():
        copies = []
        half = w_down.shape[0] // 2
        part = half // count
        for place, core in enumerate((1 - where[2], where[2])):
            for z in range(count):
                begin = place * half + z * part
                source = aligned((2 * z + core) * part, part, 16)
                w_down[begin : begin + part, :] = t_down[source, :].astype(BF16)
            copies.append(
                pltpu.make_async_copy(
                    w_down.at[place * half : (place + 1) * half], halves[place], sem_out.at[place]
                )
            )
        start_all(copies)
        for number, (weight, total) in enumerate(((w_up, t_up), (w_out, t_out))):
            half = weight.shape[1] // 2
            for place, core in enumerate((1 - where[2], where[2])):
                span = slice(place * half, (place + 1) * half)
                weight[:, span] = total[:, aligned(core * half, half, 128)].astype(BF16)
                slot = 2 * number + 2 + place
                copies.append(
                    pltpu.make_async_copy(weight.at[:, span], halves[slot], sem_out.at[slot])
                )
                copies[-1].start()
        wait_all(copies)


def feed(
    where, inputs, mixed, grads, vectors, bias, out_own, up_own, down_own, second, third, count,
    block=256,
):
    seq, width = inputs.shape
    wide = up_own.shape[1]
    row = lambda n: pl.BlockSpec((block, n), lambda i: (i, 0))
    fixed = lambda a, b: pl.BlockSpec((a, b), lambda i: (0, 0))
    return call(
        partial(feed_kernel, count),
        "feed",
        (seq // block,),
        [SCALARS, row(width), row(width), row(width), fixed(*vectors.shape), fixed(1, wide)]
        + [WHOLE] * 19,
        [row(width), row(width), row(width), fixed(1, wide), fixed(8, width)] + [WHOLE] * 6,
        [
            shape((seq, width), BF16),
            shape((seq, width), F32),
            shape((seq, width), BF16),
            shape((1, wide), F32),
            shape((8, width), F32),
        ]
        + [shape((wide // 2, width), BF16)] * 2
        + [shape((width, wide // 2), BF16)] * 2
        + [shape((width, width // 2), BF16)] * 2,
        [
            pltpu.VMEM((width, width), BF16),
            pltpu.VMEM((width, wide), BF16),
            pltpu.VMEM((wide, width), BF16),
            pltpu.VMEM((width, width), F32),
            pltpu.VMEM((width, wide), F32),
            pltpu.VMEM((wide, width), F32),
        ]
        + [pltpu.SemaphoreType.DMA((2 * copy_count(count),))] * 3
        + [pltpu.SemaphoreType.DMA((6,))],
    )(where, inputs, mixed, grads, vectors, bias, out_own, up_own, down_own, *second, *third)


def attend_back_kernel(
    where, q_ref, k_ref, v_ref, do_ref, o_ref, r_ref, e_ref, in_ref, *rest
):
    out_ref, sum_ref, w_ref, k_acc, v_acc = rest[-5:]
    seq, block = k_ref.shape[0], q_ref.shape[0]
    step, last = pl.program_id(1), pl.num_programs(1) - 1
    first = lax.broadcasted_iota(jnp.int32, (seq, PAIR), 1) < HEAD_DIM
    here = lax.broadcasted_iota(jnp.int32, (block, PAIR), 1) < HEAD_DIM
    keys, values, queries = k_ref[...], v_ref[...], q_ref[...]
    zeros = jnp.zeros_like(values)

    @pl.when(step == 0)
    def _():
        k_acc[...] = jnp.zeros_like(k_acc)
        v_acc[...] = jnp.zeros_like(v_acc)

    grads = (do_ref[...].astype(F32) * r_ref[...]).astype(BF16)
    product = grads.astype(F32) * o_ref[...].astype(F32)
    whole = jnp.sum(product, axis=1, keepdims=True)
    part = jnp.sum(jnp.where(here, product, 0.0), axis=1, keepdims=True)
    inner = (part, whole - part)
    grads_t, queries_t = grads.T, queries.T
    grad_queries = []
    for head in range(2):
        head_values = (
            jnp.where(first, values, zeros) if head == 0 else jnp.where(first, zeros, values)
        )
        raised = e_ref[head]
        grad_shares = dot_nt(grads, head_values)
        grad_scores = (raised.astype(F32) * (grad_shares - inner[head])).astype(BF16)
        grad_queries.append(dot(grad_scores, keys))
        span = slice(head * HEAD_DIM, (head + 1) * HEAD_DIM)
        v_acc[span, :] += dot(grads_t[span], raised)
        k_acc[span, :] += dot(queries_t[span], grad_scores)
    rows = pl.ds(pl.multiple_of(step * block, block), block)
    mine = jnp.where(here, grad_queries[0], grad_queries[1]) * (HEAD_DIM**-0.5)
    out_ref[rows, 0:PAIR] = mine.astype(BF16)

    @pl.when(step == last)
    def _():
        out_ref[:, PAIR : 2 * PAIR] = k_acc[...].astype(BF16).T
        out_ref[:, 2 * PAIR : 3 * PAIR] = v_acc[...].astype(BF16).T
        sum_ref[...] = jnp.sum(out_ref[...].astype(F32), axis=0, keepdims=True)
        w_ref[...] = dot(in_ref[...], out_ref[...]).astype(BF16)


def attend_back(
    where, qkv, grad_mixed, mixed, shares, raised, in_t, other, block=1024
):
    seq = qkv.shape[0]
    pairs = qkv.shape[1] // (3 * PAIR) // 2

    def pair(p, w):
        return side(w, other) * pairs + p

    def there(p, w):
        return spot(p, side(w, other), pairs)

    return call(
        attend_back_kernel,
        "attend_back",
        (pairs, seq // block),
        [
            pl.BlockSpec((block, PAIR), lambda p, b, w: (b, 3 * there(p, w))),
            pl.BlockSpec((seq, PAIR), lambda p, b, w: (0, 3 * there(p, w) + 1)),
            pl.BlockSpec((seq, PAIR), lambda p, b, w: (0, 3 * there(p, w) + 2)),
            pl.BlockSpec((block, PAIR), lambda p, b, w: (b, pair(p, w))),
            pl.BlockSpec((block, PAIR), lambda p, b, w: (b, pair(p, w))),
            pl.BlockSpec((block, PAIR), lambda p, b, w: (b, pair(p, w))),
            pl.BlockSpec((2, block, seq), lambda p, b, w: (pair(p, w), b, 0)),
            pl.BlockSpec(in_t.shape, lambda p, b, w: (0, 0), pipeline_mode=pl.Buffered(1)),
        ],
        [
            pl.BlockSpec((seq, 3 * PAIR), lambda p, b, w: (0, p)),
            pl.BlockSpec((1, 3 * PAIR), lambda p, b, w: (0, p)),
            pl.BlockSpec((in_t.shape[0], 3 * PAIR), lambda p, b, w: (0, p)),
        ],
        [shape((seq, 3 * PAIR * pairs), BF16), shape((1, 3 * PAIR * pairs), F32), shape((in_t.shape[0], 3 * PAIR * pairs), BF16)],
        [pltpu.VMEM((PAIR, seq), F32)] * 2,
        prefetch=1,
    )(where, qkv, qkv, qkv, grad_mixed, mixed, shares, raised, in_t)


def input_kernel(
    where, other_ref, mine_ref, x_ref, gres_ref, vec_ref, w_other, w_mine,
    two_ref, pre_ref, sum_other, sum_mine, out_ref, sums_ref,
):
    width = x_ref.shape[1]

    @pl.when(pl.program_id(0) == 0)
    def _():
        sums_ref[...] = jnp.zeros_like(sums_ref)
        sums_ref[OUT_B : OUT_B + 1, :] = two_ref[2:3, :]
        sums_ref[GAIN_TWO : SHIFT_TWO + 1, :] = two_ref[0:2, :]
        sums_ref[DOWN_B : DOWN_B + 1, :] = two_ref[3:4, :]
        half = sum_mine.shape[1]
        for core in range(2):
            pick = jnp.where(where[2] == core, sum_mine[...], sum_other[...])
            for slot in range(half // (3 * PAIR)):
                column = (core * (half // (3 * PAIR)) + slot) * PAIR
                for row, kind in ((QUERY_B, 0), (VALUE_B, 2)):
                    begin = (3 * slot + kind) * PAIR
                    sums_ref[row : row + 1, column : column + PAIR] = pick[:, begin : begin + PAIR]
        for row in range(pre_ref.shape[1] // width):
            sums_ref[UP_B + row : UP_B + row + 1, :] = pre_ref[:, row * width : (row + 1) * width]

    grad_in = dot_nt(other_ref[...], w_other[...]) + dot_nt(mine_ref[...], w_mine[...])
    normed, inverse = moments(x_ref[...].astype(F32))
    gain = vec_ref[GAIN_ONE : GAIN_ONE + 1, :]
    out_ref[...] = (gres_ref[...] + norm_back(grad_in, normed, inverse, gain)).astype(BF16)
    sums_ref[GAIN_ONE : GAIN_ONE + 1, :] += jnp.sum(grad_in * normed, axis=0, keepdims=True)
    sums_ref[SHIFT_ONE : SHIFT_ONE + 1, :] += jnp.sum(grad_in, axis=0, keepdims=True)


def input_back(where, other, mine, inputs, grad_res, vectors, full, sums, block=256):
    seq, width = inputs.shape
    wide = other.shape[1]
    row = lambda n: pl.BlockSpec((block, n), lambda i, w: (i, 0))
    fixed = lambda a, b: pl.BlockSpec((a, b), lambda i, w: (0, 0))
    return call(
        input_kernel,
        "input_back",
        (seq // block,),
        [
            row(wide),
            row(wide),
            row(width),
            row(width),
            fixed(*vectors.shape),
            pl.BlockSpec((width, wide), lambda i, w: (0, 1 - w[2])),
            pl.BlockSpec((width, wide), lambda i, w: (0, w[2])),
        ]
        + [fixed(*part.shape) for part in sums],
        [row(width), fixed(SUM_ROWS, width)],
        [shape((seq, width), BF16), shape((SUM_ROWS, width), F32)],
        prefetch=1,
    )(where, other, mine, inputs, grad_res, vectors, full, full, *sums)


def outer_call(kernel, name, where, grid, in_specs, out_specs, out_shape, scratch, arrays):
    return call(kernel, name, grid, in_specs, out_specs, out_shape, scratch, 1)(where, *arrays)


def part_rows(where, total, outs, shards, column=0):
    rows = total.shape[0] // shards // 4
    span = slice(column, column + total.shape[1])
    for turn, out in enumerate(outs):
        for z in range(shards):
            begin = (z * 4 + (where[1] ^ turn)) * rows
            out[z, :, span] = total[aligned(begin, rows, 16), :].astype(BF16)


def side(w, other):
    return (1 - w[2]) if other else w[2]


def add_parts_kernel(shards, where, *refs):
    inputs, outs, total = refs[:-5], refs[-5:-1], refs[-1]
    begin = 0
    for mine, got in zip(inputs[0::2], inputs[1::2]):
        span = slice(begin, begin + mine.shape[1])
        total[:, span] = mine[...].astype(F32) + got[...].astype(F32)
        begin += mine.shape[1]
    part_rows(where, total, outs, shards)


def add_parts(where, pairs, count, steps=2):
    deep = pairs[0][0].shape[0]
    wide = sum(mine.shape[1] for mine, _ in pairs)
    rows = deep // count // 4
    arrays = [part for pair in pairs for part in pair]
    return outer_call(
        partial(add_parts_kernel, count // steps),
        "add_parts",
        where,
        (steps,),
        [pl.BlockSpec((deep // steps, part.shape[1]), lambda i, w: (i, 0)) for part in arrays],
        [pl.BlockSpec((count // steps, rows, wide), lambda i, w: (i, 0, 0))] * 4,
        [shape((count, rows, wide), BF16)] * 4,
        [pltpu.VMEM((deep // steps, wide), F32)],
        arrays,
    )


def total_of(refs, z):
    total = refs[0][z].astype(F32)
    for ref in refs[1:]:
        total = total + ref[z].astype(F32)
    return total.astype(BF16)


def quad_kernel(count, where, *refs):
    for step in range(count):
        refs[4 + step][...] = total_of(refs[:4], where[0] ^ step)


def quad_sum(where, parts, count):
    full = parts[0].shape
    return call(
        partial(quad_kernel, count),
        "quad_sum",
        (1,),
        [SCALARS] + [pl.BlockSpec(full, lambda i: (0, 0, 0))] * 4,
        [pl.BlockSpec(full[1:], lambda i: (0, 0))] * count,
        [shape(full[1:], BF16)] * count,
    )(where, *parts)


def quad_pairs_kernel(half, where, *refs):
    near, far = refs[4:]
    for step in range(half):
        near[step] = total_of(refs[:4], where[0] ^ (2 * step))
        far[step] = total_of(refs[:4], where[0] ^ (2 * step) ^ 1)


def quad_pairs(where, parts, count):
    full = parts[0].shape
    half = count // 2
    return call(
        partial(quad_pairs_kernel, half),
        "quad_pairs",
        (1,),
        [SCALARS] + [pl.BlockSpec(full, lambda i: (0, 0, 0))] * 4,
        [pl.BlockSpec((half, *full[1:]), lambda i: (0, 0, 0))] * 2,
        [shape((half, *full[1:]), BF16)] * 2,
    )(where, *parts)


def halve_kernel(a, b, mine, other):
    total = (a[...].astype(F32) + b[...].astype(F32)).astype(BF16)
    mine[...] = total[0]
    other[...] = total[1]


def halve(near, got):
    full = near.shape
    spec = pl.BlockSpec(full, lambda i: (0, 0, 0))
    return call(
        halve_kernel,
        "halve",
        (1,),
        [spec] * 2,
        [pl.BlockSpec(full[1:], lambda i: (0, 0))] * 2,
        [shape(full[1:], BF16)] * 2,
    )(near, got)


def blocks_of(rows, wide, width):
    return [
        (rows * number, begin, min(width, wide - begin))
        for number, begin in enumerate(range(0, wide, width))
    ]


def merge_kernel(down, down_got, two, two_got, out):
    deep, width = down.shape
    rows, wide = two.shape
    out[0:deep, :] = (down[...].astype(F32) + down_got[...].astype(F32)).astype(BF16)
    total = (two[...].astype(F32) + two_got[...].astype(F32)).astype(BF16)
    for row, begin, size in blocks_of(rows, wide, width):
        row += deep
        out[row : row + rows, 0:size] = total[:, begin : begin + size]
        if size < width:
            out[row : row + rows, size:width] = jnp.zeros((rows, width - size), BF16)


def merge(down, down_got, two, two_got):
    deep, width = down.shape
    rows, wide = two.shape
    tall = deep + rows * len(blocks_of(rows, wide, width))
    whole = lambda part: pl.BlockSpec(part.shape, lambda i: (0, 0))
    return call(
        merge_kernel,
        "merge",
        (1,),
        [whole(part) for part in (down, down_got, two, two_got)],
        pl.BlockSpec((tall, width), lambda i: (0, 0)),
        shape((tall, width), BF16),
    )(down, down_got, two, two_got)


def add_kernel(*refs):
    total = refs[0][...].astype(F32)
    for ref in refs[1:-1]:
        total = total + ref[...].astype(F32)
    refs[-1][...] = total.astype(refs[-1].dtype)


def add_all(parts):
    full = parts[0].shape
    spec = pl.BlockSpec(full, lambda i: (0,) * len(full))
    return call(
        add_kernel, "add_all", (1,), [spec] * len(parts), spec, shape(full, parts[0].dtype)
    )(*parts)


def halves_of(where, pieces, turn):
    low = where[2] == 0
    near, far = pieces[turn][...].astype(F32), pieces[4 + turn][...].astype(F32)
    return jnp.where(low, near, far), jnp.where(low, far, near)


def lay_merged_kernel(where, *refs):
    pieces, (down, out, up) = refs[:8], refs[8:]
    width, half = down.shape[1], out.shape[1] // 2
    deep = down.shape[0] // 8
    rows, wide = up.shape[0] // 4, half + up.shape[1] // 2
    for turn in range(4):
        quad = where[1] ^ turn
        for core, value in enumerate(halves_of(where, pieces, turn)):
            down[aligned((4 * core + quad) * deep, deep, 16), :] = value[0:deep]
            for row, begin, size in blocks_of(rows, wide, width):
                part = value[deep + row : deep + row + rows, 0:size]
                place = aligned(quad * rows, rows, 16)
                if begin < half:
                    out[place, core * half : (core + 1) * half] = part[:, 0:half]
                    part, begin = part[:, half:], half
                column = core * (wide - half) + begin - half
                up[place, column : column + part.shape[1]] = part


def lay_pairs_kernel(where, *refs):
    pieces, outs = refs[:8], refs[8:]
    rows, half = pieces[0].shape
    for turn in range(4):
        place = aligned((where[1] ^ turn) * rows, rows, 16)
        for core, value in enumerate(halves_of(where, pieces, turn)):
            for slot in range(half // (3 * PAIR)):
                begin = (core * (half // (3 * PAIR)) + slot) * PAIR
                for kind, out in enumerate(outs):
                    column = (3 * slot + kind) * PAIR
                    out[place, begin : begin + PAIR] = value[:, column : column + PAIR]


def lay(kernel, name, where, pieces, outs):
    spec = pl.BlockSpec(pieces[0].shape, lambda i: (0, 0))
    return call(
        kernel,
        name,
        (1,),
        [SCALARS] + [spec] * 8,
        [pl.BlockSpec(dims, lambda i: (0, 0)) for dims in outs],
        [shape(dims, F32) for dims in outs],
    )(where, *pieces)


def pick_kernel(count, where, a, b, *outs):
    total = a[...] + b[...]
    shard = outs[0].shape[0]
    for row, out in enumerate(outs[:UP_B]):
        value = total[row : row + 1, 0:shard]
        for z in range(1, count):
            value = jnp.where(where[0] == z, total[row : row + 1, z * shard : (z + 1) * shard], value)
        out[...] = value.reshape(shard)
    value = total[UP_B : UP_B + 1, :]
    for z in range(1, count):
        value = jnp.where(where[0] == z, total[UP_B + z : UP_B + z + 1, :], value)
    outs[UP_B][...] = value.reshape(outs[UP_B].shape[0])


def pick(where, a, b, shard, wide):
    sizes = [shard] * UP_B + [wide]
    return call(
        partial(pick_kernel, a.shape[1] // shard),
        "pick",
        (1,),
        [SCALARS] + [pl.BlockSpec(a.shape, lambda i: (0, 0))] * 2,
        [pl.BlockSpec((size,), lambda i: (0,)) for size in sizes],
        [shape((size,), F32) for size in sizes],
    )(where, a, b)


def tally_kernel(where, lengths, places, ids_ref, out_ref):
    ids = ids_ref[...]
    seq = ids.shape[1]
    live = lax.broadcasted_iota(jnp.int32, (1, seq), 1) < lengths[places[where[3]]]
    high, low = ids // 128, jnp.where(live, ids % 128, -1)
    tall = (lax.broadcasted_iota(jnp.int32, (TALLY_ROWS, seq), 0) == high).astype(F32).astype(BF16)
    wide = (lax.broadcasted_iota(jnp.int32, (128, seq), 0) == low).astype(F32).astype(BF16)
    out_ref[...] = dot_nt(tall, wide).astype(jnp.int32)


def tally(cell, ids):
    return call(
        tally_kernel,
        "tally",
        (1,),
        [SCALARS] * 3 + [pl.BlockSpec(ids.shape, lambda i: (0, 0))],
        pl.BlockSpec((TALLY_ROWS, 128), lambda i: (0, 0)),
        shape((TALLY_ROWS, 128), jnp.int32),
    )(*cell, ids)


def body(
    dp_size,
    fsdp_size,
    cells_in,
    out_grad,
    cell_length,
    cell_place,
    gene_ids,
    attn_norm_gain,
    attn_norm_bias,
    query_weight,
    query_bias,
    key_weight,
    value_weight,
    value_bias,
    out_weight,
    out_bias,
    ffn_norm_gain,
    ffn_norm_bias,
    up_weight,
    up_bias,
    down_weight,
    down_bias,
):
    count = fsdp_size
    seq, width = cells_in.shape[1:]
    place = lax.axis_index("dp")
    z = lax.axis_index("fsdp")
    core, quad = place & 1, (place >> 1) & 3
    where = jnp.stack([z, quad, core, place * fsdp_size + z]).astype(jnp.int32)
    cell = (where, cell_length.astype(jnp.int32), cell_place.astype(jnp.int32))

    def swap(value, mask):
        return lax.ppermute(value, "dp", [(i, i ^ mask) for i in range(dp_size)])

    def turn(value, step):
        return lax.ppermute(value, "fsdp", [(i, i ^ step) for i in range(count)])

    def from_quad(value):
        return [swap(value, 2 * mask) for mask in (1, 2, 3)]

    def to_quad(parts):
        return [swap(parts[mask], 2 * mask) for mask in (1, 2, 3)]

    def from_column(value):
        return [turn(value, step) for step in range(1, count)]

    def to_column(parts):
        return [turn(parts[step], step) for step in range(1, count)]

    def to_core(parts, beside=None, at_once=2):
        first = lambda: (
            [swap(part, 1) for part in parts[:at_once]], beside() if beside else ()
        )
        got, result = during(first)
        if at_once < len(parts):
            got = got + during(lambda: [swap(part, 1) for part in parts[at_once:]])
        return (got, result) if beside else got

    def beyond(total):
        mask = 8
        while mask < dp_size:
            total = add_all([total, swap(total, mask)])
            mask *= 2
        return total

    inputs = cells_in.reshape(seq, width)
    grads = out_grad.reshape(seq, width)
    live = cell_length[0] > 0

    def during(run):
        outs = jax.eval_shape(run)
        blank = lambda: jax.tree.map(lambda out: jnp.zeros(out.shape, out.dtype), outs)
        return lax.cond(live, run, blank)

    shard = attn_norm_gain.shape[0]
    small = [
        attn_norm_gain,
        attn_norm_bias,
        out_bias,
        ffn_norm_gain,
        ffn_norm_bias,
        down_bias,
        query_bias,
        value_bias,
        up_bias,
    ]
    own = (query_weight, key_weight, value_weight)
    pairs = width // PAIR
    deep = down_weight.shape[0] // 8
    first, rest = pack(where, *own, out_weight, up_weight, down_weight, small)

    rows, wide = first.shape[0] - SUM_ROWS, first.shape[1]
    group = 3 * PAIR

    far, counts = during(lambda: (from_column(first), tally(cell, gene_ids)))
    early, later = split(far, [(0, 0, rows, group), (0, group, rows, wide - group)])
    small = [first] + far
    last = pairs // 2

    def first_stage():
        near, norm = during(
            lambda: (
                from_quad(early),
                first_norm(where, inputs, small, shard, count * up_bias.shape[0]),
            )
        )
        near = [early] + near
        pieces = near + to_core(near, at_once=4)

        def stage():
            kept = project_qkv(where, norm[0], norm[4], own, pieces, count, 0)
            return kept, attend(cell, kept[0], (0, 1), (0, last))

        far, (kept, mixed) = during(lambda: (from_quad(later), during(stage)))
        return norm, far, kept, mixed

    rest, ((attn_in, attn_in_t, vectors, up_b, bias), far, kept, mixed) = during(
        lambda: (lax.all_gather(rest, "fsdp", axis=0), during(first_stage))
    )
    second, third = sort(where, rest, (rest.shape[1] - deep, deep))
    later = [later] + far

    def stage():
        pieces = later + to_core(later)
        out = project_qkv(where, attn_in, bias, own, pieces, count, 1, kept)
        return out, attend(cell, out[0], (2, 3), (1, 2), mixed)

    far, ((qkv, qkv_full), mixed) = during(lambda: (from_quad(second), during(stage)))
    second = [second] + far
    far, (other, (mixed, raised, shares)) = during(
        lambda: (
            from_quad(third),
            to_core(
                second,
                lambda: attend(cell, qkv, (4, 5), (last + 1, last + 2), mixed),
            ),
        )
    )
    second, third = second + other, [third] + far
    third = third + to_core(third, at_once=4)
    counts, (block_out, grad_res, grad_mixed, pre_sum, two_sums, *halves) = during(
        lambda: (
            lax.psum(counts, "fsdp"),
            feed(
                where, inputs, mixed, grads, vectors, up_b, out_weight, up_weight, down_weight,
                second, third, count,
            ),
        )
    )
    down_theirs, down_mine, up_theirs, up_mine, out_theirs, out_mine = halves

    def backward():
        down_got = during(lambda: swap(down_theirs, 1))
        down_parts = add_parts(where, [(down_mine, down_got)], count)

        def stage():
            up_got, out_got, back = during(
                lambda: (
                    swap(up_theirs, 1),
                    swap(out_theirs, 1),
                    attend_back(where, qkv, grad_mixed, mixed, shares, raised, attn_in_t, True),
                )
            )
            return back, add_parts(where, [(out_mine, out_got), (up_mine, up_got)], count)

        got, ((grads_other, sums_other, qkv_theirs), two_parts) = during(
            lambda: (to_quad(down_parts), during(stage))
        )
        down_all = [down_parts[0]] + got

        def stage():
            down_near, down_far = quad_pairs(where, down_all, count)
            got, far, (grads_mine, sums_mine, mine) = during(
                lambda: (
                    swap(qkv_theirs, 1),
                    turn(down_far, 1),
                    attend_back(where, qkv, grad_mixed, mixed, shares, raised, attn_in_t, False),
                )
            )
            parts = add_parts(where, [(mine, got)], count)
            return parts, halve(down_near, far), grads_mine, sums_mine

        got, (qkv_parts, (down_piece, down_next), grads_mine, sums_mine) = during(
            lambda: (to_quad(two_parts), during(stage))
        )

        def stage():
            near, far = quad_pairs(where, [two_parts[0]] + got, count)
            far, down_got, (back, sums) = during(
                lambda: (
                    turn(far, 1),
                    turn(down_next, 2),
                    input_back(
                        where, grads_other, grads_mine, inputs, grad_res, vectors, qkv_full,
                        (two_sums, pre_sum, sums_other, sums_mine),
                    ),
                )
            )
            piece, following = halve(near, far)
            got_too, more = during(lambda: (turn(following, 2), swap(sums, 1)))
            sums = add_all([sums, more])
            merged = beyond(merge(down_piece, down_got, piece, got_too))
            return merged, back, sums

        got, (merged, input_grad, sums) = during(lambda: (to_quad(qkv_parts), during(stage)))
        qkv_parts = quad_sum(where, [qkv_parts[0]] + got, count)
        got, (side, other_side) = during(
            lambda: (to_column(qkv_parts), during(lambda: (swap(merged, 2), swap(merged, 4))))
        )
        qkv_piece = beyond(add_all([qkv_parts[0]] + got))
        far, (across, more) = during(
            lambda: (from_quad(qkv_piece), during(lambda: (swap(merged, 6), swap(sums, 2))))
        )
        qkv_pieces, merged = [qkv_piece] + far, [merged, side, other_side, across]
        sums = add_all([sums, more])
        other, more = during(lambda: ([swap(part, 1) for part in qkv_pieces], swap(sums, 4)))
        sums = sums + more
        mask = 8
        while mask < dp_size:
            sums = sums + swap(sums, mask)
            mask *= 2
        sums_got, (far, (grad_query, grad_key, grad_value)) = during(
            lambda: (
                turn(sums, 1),
                to_core(
                    merged,
                    lambda: lay(
                        lay_pairs_kernel, "lay_qkv", where, qkv_pieces + other,
                        [query_weight.shape] * 3,
                    ),
                    4,
                ),
            )
        )
        sums = add_all([sums, sums_got])
        more, (grad_down, grad_out, grad_up) = during(
            lambda: (
                turn(sums, 2),
                lay(
                    lay_merged_kernel, "lay_merged", where, merged + far,
                    [down_weight.shape, out_weight.shape, up_weight.shape],
                ),
            )
        )
        vec = pick(where, sums, more, shard, up_bias.shape[0])
        return input_grad, vec, grad_query, grad_key, grad_value, grad_out, grad_up, grad_down

    counts, results = during(lambda: (lax.psum(counts, "dp"), during(backward)))
    input_grad, vec, grad_query, grad_key, grad_value, grad_out, grad_up, grad_down = results
    gene_counts = counts.reshape(-1)[:VOCAB]

    return (
        block_out.reshape(cells_in.shape),
        input_grad.reshape(cells_in.shape),
        vec[0],
        vec[1],
        grad_query,
        vec[6],
        grad_key,
        grad_value,
        vec[7],
        grad_out,
        vec[2],
        vec[3],
        vec[4],
        grad_up,
        vec[UP_B],
        grad_down,
        vec[5],
        gene_counts,
    )


def solution(mesh):
    cells = P(("dp", "fsdp"), None, None)
    vector = P("fsdp")
    matrix = P("fsdp", None)
    in_specs = (
        cells,
        cells,
        P(),
        P(),
        P(("dp", "fsdp"), None),
        vector,
        vector,
        matrix,
        vector,
        matrix,
        matrix,
        vector,
        matrix,
        vector,
        vector,
        vector,
        matrix,
        vector,
        matrix,
        vector,
    )
    out_specs = (
        cells,
        cells,
        vector,
        vector,
        matrix,
        vector,
        matrix,
        matrix,
        vector,
        matrix,
        vector,
        vector,
        vector,
        matrix,
        vector,
        matrix,
        vector,
        P(),
    )
    return jax.shard_map(
        partial(body, mesh.shape["dp"], mesh.shape["fsdp"]),
        mesh=mesh,
        in_specs=in_specs,
        out_specs=out_specs,
        check_vma=False,
    )
```
